128 devices in a mesh: plane: 8 (over x, core), tile: 16 (over y, z).
Axes of the slice: x: 4, y: 4, z: 4, core: 2. Of those that a mesh axis runs over, the one named last changes fastest.
Arguments:
- primal: float32 [5, 16, 64, 512], P(None, 'plane', 'tile'), may hold values from -6 to 6
- dual: float32 [5, 16, 16, 1024], P(None, 'plane', 'tile'), may hold values from -6 to 6
- measured: float32 [16, 16, 1024], P('plane', 'tile'), may hold values from -6 to 6
- footprint_weights: float32 [16, 16, 12, 128, 128], P('tile'), may hold values from -0.15625 to 0.15625
- pixel_index: int32 [16, 16, 12], P('tile'), may hold values from 0 to 15
- bin_index: int32 [16, 16, 12], replicated, may hold values from 0 to 7
- slot_count: int32 [16, 16], P('tile'), may hold values from 6 to 12, as said below
- dual_kernel: float32 [32, 7, 3, 3, 3], replicated, may hold values from -0.4375 to 0.4375
- dual_bias: float32 [32], replicated, may hold values from -1.5 to 1.5
- dual_slope: float32 [32], replicated, may hold values from 0.05 to 0.8
- dual_mixing: float32 [5, 32], replicated, may hold values from -1 to 1
- dual_shift: float32 [5], replicated, may hold values from -1.5 to 1.5
- primal_kernel: float32 [32, 6, 3, 3, 3], replicated, may hold values from -0.5 to 0.5
- primal_bias: float32 [32], replicated, may hold values from -1.5 to 1.5
- primal_slope: float32 [32], replicated, may hold values from 0.05 to 0.8
- primal_mixing: float32 [5, 32], replicated, may hold values from -1 to 1
- primal_shift: float32 [5], replicated, may hold values from -1.5 to 1.5
Outputs:
- new_primal: float32 [5, 16, 64, 512], P(None, 'plane', 'tile')
- new_dual: float32 [5, 16, 16, 1024], P(None, 'plane', 'tile')
The draws below stay inside these ranges and needn't reach their ends.
Inputs may be any that keep to these rules, and one draw needn't show every extreme that they name: slot_count is at least 6 everywhere, and equals 12 for some strip and angle in every draw.
All inputs are finite; a program needn't handle non-finite values.
Results may differ from the reference program's by a relative error of at most 0.0003.
Values sent between devices are 32-bit elements; how exact they have to be, the bound alone decides.
No kernel may reach another device: no remote copies, remote signals or barrier semaphores. Data moves between devices by JAX's collectives and lax.ppermute only.
A program may use at most 64 MiB of HBM per device.

```python
import math
import jax
import jax.numpy as jnp
from jax import lax

NCOL = 512
BINS = 1024
BLK = 128
SLOTS = 12
CH = 32
MEM = 5
ANGLES = 16
STRIPS = 16
PLANES = 16
NROW = 64
PIXBLK = 16
BINBLK = 8


def draw_slot_count(key, part):
    key_counts, key_strip, key_angle = jax.random.split(jax.random.fold_in(key, 17), 3)
    counts = jax.random.randint(key_counts, (STRIPS, ANGLES), SLOTS // 2, SLOTS + 1)
    strip_pick = jax.random.randint(key_strip, (), 0, STRIPS)
    angle_pick = jax.random.randint(key_angle, (), 0, ANGLES)
    return counts.at[strip_pick, angle_pick].set(SLOTS).astype(jnp.int32)


def touch_ends(drawn, own_key, low, high):
    place = [jax.random.randint(jax.random.fold_in(own_key, axis), (), 0, length) for axis, length in enumerate(drawn.shape)]
    main_axis = drawn.shape.index(max(drawn.shape))
    next_to = place[:main_axis] + [(place[main_axis] + 1) % drawn.shape[main_axis]] + place[main_axis + 1:]
    return drawn.at[tuple(place)].set(low).at[tuple(next_to)].set(high)


def raised(entries, rng, source, target, blocks, factor):
    owner, partner = [(jnp.arange(entries.shape[dim]) // (entries.shape[dim] // blocks)).reshape([-1 if axis == dim else 1 for axis in range(entries.ndim)]) for dim in (source, target)]
    chosen = jax.random.permutation(rng, blocks)[partner]
    strong = (owner == chosen) | (owner == (partner + blocks // 2) % blocks)
    return jnp.where(strong, factor * entries, entries)


def shard_levels(stream_key, shape, cuts, smallest, largest):
    factor_of = 1.0
    for dim, blocks in cuts:
        steps = jax.random.uniform(jax.random.fold_in(jax.random.fold_in(stream_key, 6), dim), (blocks,), jnp.float32, smallest / len(cuts), largest / len(cuts))
        factor_of = factor_of * jnp.repeat(jnp.exp(steps), shape[dim] // blocks).reshape((-1,) + (1,) * (len(shape) - 1 - dim))
    return factor_of


def scatter_about(own_key, dims, scale, reach, cuts=(), kind=jnp.bfloat16):
    drawn = jax.random.normal(own_key, dims, jnp.float32) * scale
    if len(cuts) > 0:
        drawn = shard_levels(own_key, dims, cuts, -0.22, 0.18) * drawn
    return jnp.clip(drawn, min=-reach, max=reach).astype(kind)


def noise_with(stream_key, dims, width, reach, shards, heavy, kind=jnp.bfloat16):
    values = width * jax.random.normal(stream_key, dims, jnp.float32)
    if shards:
        values = values * shard_levels(stream_key, dims, shards, -0.22, 0.18)
    return jnp.clip(raised(values, jax.random.fold_in(stream_key, 3), *heavy), -reach, reach).astype(kind)


def setup_inputs(seed: int = 0) -> dict:
    arg_keys = jax.random.split(jax.random.key(seed), 18)
    primal = scatter_about(arg_keys[0], (MEM, PLANES, NROW, NCOL), 1.0, 6.0, ((1, 8), (2, 16)), jnp.float32)
    dual = scatter_about(arg_keys[1], (MEM, PLANES, ANGLES, BINS), 1.0, 6.0, ((1, 8), (2, 16)), jnp.float32)
    measured = scatter_about(arg_keys[2], (PLANES, ANGLES, BINS), 1.0, 6.0, ((0, 8), (1, 16)), jnp.float32)
    footprint_weights = noise_with(arg_keys[3], (STRIPS, ANGLES, SLOTS, BLK, BLK), (SLOTS * STRIPS * BLK * BLK // BINS) ** -0.5, 0.15625, ((0, 16),), (0, 1, 16, 2.0), jnp.float32)
    pixel_index = touch_ends(jax.random.randint(arg_keys[4], (STRIPS, ANGLES, SLOTS), 0, PIXBLK), jax.random.fold_in(arg_keys[4], 1), 0, PIXBLK - 1).astype(jnp.int32)
    bin_index = touch_ends(jax.random.randint(arg_keys[5], (STRIPS, ANGLES, SLOTS), 0, BINBLK), jax.random.fold_in(arg_keys[5], 1), 0, BINBLK - 1).astype(jnp.int32)
    slot_count = draw_slot_count(jax.random.fold_in(arg_keys[17], 71), 0)
    dual_kernel = scatter_about(arg_keys[7], (CH, MEM + 2, 3, 3, 3), (27 * (MEM + 2)) ** -0.5, 0.4375, (), jnp.float32)
    dual_bias = scatter_about(arg_keys[8], (CH,), 0.3, 1.5, (), jnp.float32)
    dual_slope = jnp.clip(jnp.exp(jax.random.uniform(arg_keys[9], (CH,), jnp.float32, math.log(0.05), math.log(0.8))), 0.05, 0.8)
    dual_mixing = scatter_about(arg_keys[10], (MEM, CH), CH ** -0.5, 1.0, (), jnp.float32)
    dual_shift = scatter_about(arg_keys[11], (MEM,), 0.3, 1.5, (), jnp.float32)
    primal_kernel = scatter_about(arg_keys[12], (CH, MEM + 1, 3, 3, 3), (27 * (MEM + 1)) ** -0.5, 0.5, (), jnp.float32)
    primal_bias = scatter_about(arg_keys[13], (CH,), 0.3, 1.5, (), jnp.float32)
    primal_slope = jnp.clip(jnp.exp(jax.random.uniform(arg_keys[14], (CH,), jnp.float32, math.log(0.05), math.log(0.8))), 0.05, 0.8)
    primal_mixing = scatter_about(arg_keys[15], (MEM, CH), CH ** -0.5, 1.0, (), jnp.float32)
    primal_shift = scatter_about(arg_keys[16], (MEM,), 0.3, 1.5, (), jnp.float32)
    return dict(primal=primal, dual=dual, measured=measured, footprint_weights=footprint_weights, pixel_index=pixel_index, bin_index=bin_index, slot_count=slot_count, dual_kernel=dual_kernel, dual_bias=dual_bias, dual_slope=dual_slope, dual_mixing=dual_mixing, dual_shift=dual_shift, primal_kernel=primal_kernel, primal_bias=primal_bias, primal_slope=primal_slope, primal_mixing=primal_mixing, primal_shift=primal_shift)


HIGHEST = lax.Precision.HIGHEST


def indicator(indices, total_count):
    return (indices[..., None] == jnp.arange(total_count, dtype=jnp.int32)).astype(jnp.float32)


def network(inputs, kernel, bias_first, leak_slope, mixing, bias_last):
    padded = jnp.pad(inputs, ((0, 0), (1, 1), (1, 1), (1, 1)))
    hidden = lax.conv_general_dilated(padded[None], kernel, (1, 1, 1), "VALID", dimension_numbers=("NCDHW", "OIDHW", "NCDHW"), precision=HIGHEST)[0]
    hidden = hidden + bias_first[:, None, None, None]
    hidden = jnp.where(hidden > 0, hidden, leak_slope[:, None, None, None] * hidden)
    return jnp.einsum("oc,czyx->ozyx", mixing, hidden, precision=HIGHEST) + bias_last[:, None, None, None]


def reference(primal, dual, measured, footprint_weights, pixel_index, bin_index, slot_count, dual_kernel, dual_bias, dual_slope, dual_mixing, dual_shift, primal_kernel, primal_bias, primal_slope, primal_mixing, primal_shift):
    live_slots = (jnp.arange(SLOTS, dtype=jnp.int32) < slot_count[..., None]).astype(jnp.float32)
    source = primal[1].reshape(PLANES, STRIPS, PIXBLK, BLK).transpose(1, 0, 2, 3)

    def forward_strip(running, strip_items):
        blocks_here, weights_here, pixels_here, bins_here, live_here = strip_items
        picked = blocks_here[:, pixels_here, :]
        products = jnp.einsum("zasj,asjk->zask", picked, weights_here, precision=HIGHEST) * live_here[None, :, :, None]
        added = jnp.einsum("zask,asb->zabk", products, indicator(bins_here, BINBLK), precision=HIGHEST)
        return running + added, None

    start_sum = jnp.zeros((PLANES, ANGLES, BINBLK, BLK), jnp.float32)
    summed, _ = lax.scan(forward_strip, start_sum, (source, footprint_weights, pixel_index, bin_index, live_slots))
    projected = summed.reshape(PLANES, ANGLES, BINS)
    dual_input = jnp.concatenate([dual, projected[None], measured[None]], 0)
    new_dual = dual + network(dual_input, dual_kernel, dual_bias, dual_slope, dual_mixing, dual_shift)

    dual_blocks = new_dual[0].reshape(PLANES, ANGLES, BINBLK, BLK)
    angle_ids = jnp.arange(ANGLES, dtype=jnp.int32)[:, None]

    def backward_strip(strip_items):
        weights_here, pixels_here, bins_here, live_here = strip_items
        picked = dual_blocks[:, angle_ids, bins_here, :]
        spread = jnp.einsum("zask,asjk->zasj", picked, weights_here, precision=HIGHEST) * live_here[None, :, :, None]
        return jnp.einsum("zasj,asq->zqj", spread, indicator(pixels_here, PIXBLK), precision=HIGHEST)

    back = lax.map(backward_strip, (footprint_weights, pixel_index, bin_index, live_slots))
    back = back.transpose(1, 0, 2, 3).reshape(PLANES, NROW, NCOL)
    primal_input = jnp.concatenate([primal, back[None]], 0)
    new_primal = primal + network(primal_input, primal_kernel, primal_bias, primal_slope, primal_mixing, primal_shift)
    return new_primal, new_dual
```

```python
import functools

import jax
import jax.numpy as jnp
from jax import lax
from jax.experimental import pallas as pl
from jax.experimental.pallas import tpu as pltpu
from jax.sharding import PartitionSpec as P

F32 = jnp.float32
BF16 = jnp.bfloat16
VMEM = pl.BlockSpec(memory_space=pltpu.VMEM)
SMEM = pl.BlockSpec(memory_space=pltpu.SMEM)


def split(x):
    hi = x.astype(BF16)
    return hi, (x - hi.astype(F32)).astype(BF16)


def dot3(a, b, dims):
    (a_hi, a_lo), (b_hi, b_lo) = a, b
    dot = functools.partial(
        lax.dot_general, dimension_numbers=(dims, ((), ())), preferred_element_type=F32
    )
    return dot(a_hi, b_hi) + dot(a_lo, b_hi) + dot(a_hi, b_lo)


def column(ref, count):
    rows = -(-count // 8) * 8
    index = lax.broadcasted_iota(jnp.int32, (rows, 128), 0)
    out = jnp.zeros((rows, 128), F32)
    for i in range(count):
        out = jnp.where(index == i, ref[i], out)
    return out[:, 0:1]


def shifted_sum(stack):
    left, mid, right = stack
    width = mid.shape[1]
    lane = lax.broadcasted_iota(jnp.int32, mid.shape, 1)
    left = jnp.where(lane == 0, 0.0, pltpu.roll(left, 1, 1))
    right = jnp.where(lane == width - 1, 0.0, pltpu.roll(right, width - 1, 1))
    return left + mid + right


def pack_kernel(dual_ref, measured_ref, primal_ref, out_ref):
    zero = jnp.zeros((1, 1024), F32)
    for z in range(2):
        for c in range(5):
            out_ref[z * 8 + c : z * 8 + c + 1, :] = dual_ref[c, z]
        out_ref[z * 8 + 5 : z * 8 + 6, :] = zero
        out_ref[z * 8 + 6 : z * 8 + 7, :] = measured_ref[z]
        out_ref[z * 8 + 7 : z * 8 + 8, :] = zero
    for k, row in enumerate((0, 3)):
        for c in range(5):
            for z in range(2):
                i = 16 + k * 5 + c
                out_ref[i : i + 1, z * 512 : (z + 1) * 512] = primal_ref[c, z, row : row + 1, :]
    out_ref[26:32, :] = jnp.zeros((6, 1024), F32)


def project_kernel(pix_ref, bin_ref, cnt_ref, primal_ref, w_ref, out_ref, hi_ref, lo_ref, hot_ref):
    a = pl.program_id(0)
    t = lax.axis_index("tile")

    @pl.when(a == 0)
    def _():
        for q in range(16):
            r, col = q // 4, (q % 4) * 128
            v = jnp.concatenate(
                [
                    jnp.broadcast_to(primal_ref[1, z, r : r + 1, col : col + 128], (8, 128))
                    for z in range(2)
                ],
                0,
            )
            hi_ref[q], lo_ref[q] = split(v)
        row = lax.broadcasted_iota(jnp.int32, (16, 128), 0)
        for b in range(9):
            hot_ref[b] = jnp.where((row & 7) == b, 1.0, 0.0).astype(BF16)
        out_ref[0, 0] = jnp.zeros((16, 128), F32)
        out_ref[15, 2] = jnp.zeros((16, 128), F32)

    count = cnt_ref[0, a]
    parts = []
    for s in range(12):
        q = pix_ref[s, 0, a]
        b = jnp.where(s < count, bin_ref[s, t, a], 8)
        hot = hot_ref[b]
        parts.append(jnp.concatenate([hi_ref[q] * hot, lo_ref[q] * hot], 0))
    left = jnp.concatenate(parts, 1)
    w_hi, w_lo = split(w_ref[0, 0].reshape(12 * 128, 128))
    right = jnp.concatenate([w_hi, w_lo], 1)
    d = jnp.dot(left, right, preferred_element_type=F32)
    res = d[0:16, 0:128] + (d[0:16, 128:256] + d[16:32, 0:128])
    out_ref[a, 1] = res

    @pl.when(a > 0)
    def _():
        out_ref[jnp.maximum(a - 1, 0), 2] = res

    @pl.when(a < 15)
    def _():
        out_ref[jnp.minimum(a + 1, 15), 0] = res


def assemble_kernel(got_ref, own_ref, left_ref, right_ref, primal_ref, sp_ref, sm_ref):
    t = lax.axis_index("tile")
    total = got_ref[0]
    for i in range(1, 16):
        total = total + got_ref[i]
    ok = (t > 0, None, t < 15)
    for k, src in enumerate((left_ref, own_ref, right_ref)):
        keep = (lambda v: v) if ok[k] is None else (lambda v, m=ok[k]: jnp.where(m, v, 0.0))
        for z in range(2):
            base = z * 24 + k * 8
            block = keep(src[z * 8 : z * 8 + 8, :])
            for out in (sp_ref, sm_ref):
                out[base : base + 8, :] = block
                for b in range(8):
                    i = z * 8 + b
                    out[base + 5 : base + 6, b * 128 : (b + 1) * 128] = keep(total[k, i : i + 1, :])
    for z, out in ((0, sm_ref), (1, sp_ref)):
        for row in range(6):
            for c in range(5):
                if row == 0:
                    v = jnp.where(ok[0], left_ref[21 + c : 22 + c, z * 512 : (z + 1) * 512], 0.0)
                elif row == 5:
                    v = jnp.where(ok[2], right_ref[16 + c : 17 + c, z * 512 : (z + 1) * 512], 0.0)
                else:
                    v = primal_ref[c, z, row - 1 : row, :]
                i = row * 5 + c
                lane = (i // 16) * 512
                out[48 + i % 16 : 49 + i % 16, lane : lane + 512] = v
        out[62:64, 512:1024] = jnp.zeros((2, 512), F32)


def dual_kernel_body(
    own_ref, prev_ref, next_ref, kern_ref, mix_ref, bias_ref, slope_ref, shift_ref,
    new_ref, send_ref, tt_ref,
):
    p = lax.axis_index("plane")
    tt_ref[...] = jnp.zeros((72, 96), F32)
    for dz in range(3):
        for da in range(3):
            base = dz * 24 + da * 8
            tt_ref[base : base + 7, :] = jnp.concatenate(
                [kern_ref[dz, da, db] for db in range(3)], 1
            )
    x = jnp.concatenate(
        [
            jnp.where(p > 0, prev_ref[0:48, :], 0.0),
            own_ref[0:48, :],
            jnp.where(p < 7, next_ref[0:48, :], 0.0),
        ],
        0,
    )
    x_hi, x_lo = split(x)
    tt = split(tt_ref[...].T)
    bias, slope, shift = column(bias_ref, 32), column(slope_ref, 32), column(shift_ref, 5)
    mix = split(jnp.concatenate([mix_ref[...], jnp.zeros((3, 32), F32)], 0))
    for z in range(4):
        rows = slice(z * 24, z * 24 + 72)
        h = dot3(tt, (x_hi[rows], x_lo[rows]), ((1,), (0,)))
        h = shifted_sum([h[i * 32 : (i + 1) * 32] for i in range(3)]) + bias
        h = jnp.where(h > 0, h, slope * h)
        out = dot3(mix, split(h), ((1,), (0,))) + shift
        out = out + x[(z + 1) * 24 + 8 : (z + 1) * 24 + 16]
        if z in (1, 2):
            for c in range(5):
                new_ref[c, z - 1] = out[c : c + 1, :]
        for b in range(8):
            piece = jnp.broadcast_to(out[0:1, b * 128 : (b + 1) * 128], (16, 128))
            send_ref[:, b, z, :] = piece


def back_kernel(pix_ref, bin_ref, cnt_ref, nd_ref, w_ref, out_ref, up_ref, down_ref, tab_ref, hot_ref, acc_ref):
    a = pl.program_id(0)
    t = lax.axis_index("tile")

    @pl.when(a == 0)
    def _():
        row = lax.broadcasted_iota(jnp.int32, (16, 128), 0)
        for q in range(17):
            hot_ref[q] = jnp.where(row == q, 1.0, 0.0).astype(BF16)
        acc_ref[...] = jnp.zeros_like(acc_ref)

    for b in range(8):
        hi, lo = split(
            jnp.concatenate(
                [jnp.broadcast_to(nd_ref[0, b, z : z + 1, :], (16, 128)) for z in range(4)], 0
            )
        )
        tab_ref[b, 0:64] = hi
        tab_ref[b, 64:128] = lo
    count = cnt_ref[0, a]
    parts = []
    for s in range(12):
        q = jnp.where(s < count, pix_ref[s, 0, a], 16)
        hot = hot_ref[q]
        parts.append(tab_ref[bin_ref[s, t, a]] * jnp.concatenate([hot] * 8, 0))
    left = jnp.concatenate(parts, 1)
    rights = []
    for s in range(12):
        w_hi, w_lo = split(w_ref[0, 0, s])
        rights.append(jnp.concatenate([w_hi, w_lo], 0))
    right = jnp.concatenate(rights, 1)
    acc_ref[...] += lax.dot_general(
        left, right, (((1,), (1,)), ((), ())), preferred_element_type=F32
    )

    @pl.when(a == 15)
    def _():
        d = acc_ref[...]
        res = d[0:64, 0:128] + (d[0:64, 128:256] + d[64:128, 0:128])
        out_ref[...] = res
        for z in range(4):
            up_ref[z * 4 : z * 4 + 4, :] = res[z * 16 : z * 16 + 4]
            down_ref[z * 4 : z * 4 + 4, :] = res[z * 16 + 12 : z * 16 + 16]


def primal_kernel_body(
    sp_ref, sm_ref, prev_ref, next_ref, back_ref, above_ref, below_ref, primal_ref, kern_ref,
    mix_ref, bias_ref, slope_ref, shift_ref, new_ref, tt_ref, tb_ref, x_ref, y_ref,
):
    p = lax.axis_index("plane")
    t = lax.axis_index("tile")
    keeps = (p > 0, None, None, p < 7)
    for plane, src in enumerate((prev_ref, sm_ref, sp_ref, next_ref)):
        for half in range(2):
            v = src[48:64, half * 512 : (half + 1) * 512]
            if keeps[plane] is not None:
                v = jnp.where(keeps[plane], v, 0.0)
            x_ref[plane * 32 + half * 16 : plane * 32 + half * 16 + 16, :] = v
    y_ref[...] = jnp.zeros((32, 512), F32)
    for plane in range(4):
        for row in range(6):
            for col in range(4):
                if row == 0:
                    v = jnp.where(t > 0, above_ref[plane * 4 + col : plane * 4 + col + 1, :], 0.0)
                elif row == 5:
                    v = jnp.where(t < 15, below_ref[plane * 4 + col : plane * 4 + col + 1, :], 0.0)
                else:
                    i = plane * 16 + (row - 1) * 4 + col
                    v = back_ref[i : i + 1, :]
                if keeps[plane] is not None:
                    v = jnp.where(keeps[plane], v, 0.0)
                y_ref[plane * 8 + row : plane * 8 + row + 1, col * 128 : (col + 1) * 128] = v
    tt_ref[...] = jnp.zeros((96, 384), F32)
    tb_ref[...] = jnp.zeros((24, 384), F32)
    for dz in range(3):
        for dr in range(3):
            rows = [
                jnp.concatenate([kern_ref[c, dz, dr, db : db + 1, :] for db in range(3)], 1)
                for c in range(6)
            ]
            block = jnp.concatenate(rows, 0)
            for r in range(4):
                i = dz * 32 + (r + dr) * 5
                tt_ref[i : i + 5, r * 96 : (r + 1) * 96] = block[0:5]
                i = dz * 8 + r + dr
                tb_ref[i : i + 1, r * 96 : (r + 1) * 96] = block[5:6]
    tt = split(tt_ref[...].T)
    tb = split(tb_ref[...].T)
    x_hi, x_lo = split(x_ref[...])
    y_hi, y_lo = split(y_ref[...])
    bias, slope, shift = column(bias_ref, 32), column(slope_ref, 32), column(shift_ref, 5)
    mix = split(jnp.concatenate([mix_ref[...], jnp.zeros((3, 32), F32)], 0))
    for z in range(2):
        rows = slice(z * 32, z * 32 + 96)
        h = dot3(tt, (x_hi[rows], x_lo[rows]), ((1,), (0,)))
        rows = slice(z * 8, z * 8 + 24)
        h = h + dot3(tb, (y_hi[rows], y_lo[rows]), ((1,), (0,)))
        for r in range(4):
            g = shifted_sum([h[r * 96 + i * 32 : r * 96 + (i + 1) * 32] for i in range(3)]) + bias
            g = jnp.where(g > 0, g, slope * g)
            out = dot3(mix, split(g), ((1,), (0,))) + shift
            for c in range(5):
                new_ref[c, z, r : r + 1, :] = out[c : c + 1, :] + primal_ref[c, z, r : r + 1, :]


def call(body, name, outs, in_specs, scratch=(), limit=16 << 20):
    return pl.pallas_call(
        body,
        name=name,
        out_shape=tuple(jax.ShapeDtypeStruct(s, F32) for s in outs),
        in_specs=in_specs,
        out_specs=tuple(VMEM for _ in outs),
        scratch_shapes=list(scratch),
        compiler_params=pltpu.CompilerParams(vmem_limit_bytes=limit),
    )


def ring(array, axis, step):
    count = lax.axis_size(axis)
    return lax.ppermute(array, axis, [(i, (i + step) % count) for i in range(count)])


def per_device(
    primal, dual, measured, footprint_weights, pixel_index, bin_index, slot_count,
    dual_kernel, dual_bias, dual_slope, dual_mixing, dual_shift,
    primal_kernel, primal_bias, primal_slope, primal_mixing, primal_shift,
):
    pix = jnp.transpose(pixel_index, (2, 0, 1))
    bins = jnp.transpose(bin_index, (2, 0, 1))

    own = call(pack_kernel, "pack", [(32, 1024)], [VMEM] * 3)(dual, measured, primal)[0]
    left = ring(own, "tile", 1)
    right = ring(own, "tile", -1)

    w_spec = pl.BlockSpec((1, 1, 12, 128, 128), lambda a: (0, a, 0, 0, 0))
    terms = pl.pallas_call(
        project_kernel,
        name="project",
        grid=(16,),
        out_shape=jax.ShapeDtypeStruct((16, 3, 16, 128), F32),
        in_specs=[SMEM, SMEM, SMEM, VMEM, w_spec],
        out_specs=VMEM,
        scratch_shapes=[pltpu.VMEM((16, 16, 128), BF16)] * 3,
        compiler_params=pltpu.CompilerParams(
            vmem_limit_bytes=16 << 20, dimension_semantics=("arbitrary",)
        ),
    )(pix, bins, slot_count, primal, footprint_weights)
    got = lax.all_to_all(terms, "tile", 0, 0, tiled=True)

    sp, sm = call(assemble_kernel, "assemble", [(64, 1024)] * 2, [VMEM] * 5)(
        got, own, left, right, primal
    )
    prev = ring(sp, "plane", 1)
    after = ring(sm, "plane", -1)

    new_dual, send = call(
        dual_kernel_body, "dual_net", [(5, 2, 1, 1024), (16, 8, 4, 128)],
        [VMEM] * 5 + [SMEM] * 3, [pltpu.VMEM((72, 96), F32)],
    )(
        sp, prev, after, jnp.transpose(dual_kernel, (2, 3, 4, 1, 0)), dual_mixing,
        dual_bias, dual_slope, dual_shift,
    )
    leading = lax.all_to_all(send, "tile", 0, 0, tiled=True)

    back, up, down = pl.pallas_call(
        back_kernel,
        name="back",
        grid=(16,),
        out_shape=(
            jax.ShapeDtypeStruct((64, 128), F32),
            jax.ShapeDtypeStruct((16, 128), F32),
            jax.ShapeDtypeStruct((16, 128), F32),
        ),
        in_specs=[SMEM, SMEM, SMEM, pl.BlockSpec((1, 8, 4, 128), lambda a: (a, 0, 0, 0)), w_spec],
        out_specs=(VMEM, VMEM, VMEM),
        scratch_shapes=[
            pltpu.VMEM((8, 128, 128), BF16),
            pltpu.VMEM((17, 16, 128), BF16),
            pltpu.VMEM((128, 256), F32),
        ],
        compiler_params=pltpu.CompilerParams(
            vmem_limit_bytes=16 << 20, dimension_semantics=("arbitrary",)
        ),
    )(pix, bins, slot_count, leading, footprint_weights)
    above = ring(down, "tile", 1)
    below = ring(up, "tile", -1)

    new_primal = call(
        primal_kernel_body, "primal_net", [(5, 2, 4, 512)], [VMEM] * 10 + [SMEM] * 3,
        [
            pltpu.VMEM((96, 384), F32),
            pltpu.VMEM((24, 384), F32),
            pltpu.VMEM((128, 512), F32),
            pltpu.VMEM((32, 512), F32),
        ],
    )(
        sp, sm, prev, after, back, above, below, primal,
        jnp.transpose(primal_kernel, (1, 2, 3, 4, 0)), primal_mixing,
        primal_bias, primal_slope, primal_shift,
    )[0]
    return new_primal, new_dual


def solution(mesh):
    grid = P(None, "plane", "tile", None)
    in_specs = (
        grid, grid, P("plane", "tile", None), P("tile", None, None, None, None),
        P("tile", None, None), P(), P("tile", None),
    ) + (P(),) * 10
    return jax.shard_map(
        per_device, mesh=mesh, in_specs=in_specs, out_specs=(grid, grid), check_vma=False
    )
```

```python
import functools

import jax
import jax.numpy as jnp
from jax import lax
from jax.experimental import pallas as pl
from jax.experimental.pallas import tpu as pltpu
from jax.sharding import PartitionSpec as P


F32 = jnp.float32
BF16 = jnp.bfloat16
VMEM = pl.BlockSpec(memory_space=pltpu.VMEM)
SMEM = pl.BlockSpec(memory_space=pltpu.SMEM)
HBM = pl.BlockSpec(memory_space=pltpu.HBM)


def split(x):
    hi = x.astype(BF16)
    return hi, (x - hi.astype(F32)).astype(BF16)


def dot3(a, b, dims):
    (a_hi, a_lo), (b_hi, b_lo) = a, b
    dot = functools.partial(
        lax.dot_general, dimension_numbers=(dims, ((), ())), preferred_element_type=F32
    )
    return dot(a_hi, b_hi) + dot(a_lo, b_hi) + dot(a_hi, b_lo)


def column(ref, count):
    rows = -(-count // 8) * 8
    index = lax.broadcasted_iota(jnp.int32, (rows, 128), 0)
    out = jnp.zeros((rows, 128), F32)
    for i in range(count):
        out = jnp.where(index == i, ref[i], out)
    return out[:, 0:1]


def shifted_sum(stack):
    left, mid, right = stack
    width = mid.shape[1]
    lane = lax.broadcasted_iota(jnp.int32, mid.shape, 1)
    left = jnp.where(lane == 0, 0.0, pltpu.roll(left, 1, 1))
    right = jnp.where(lane == width - 1, 0.0, pltpu.roll(right, width - 1, 1))
    return left + mid + right


def pack_kernel(dual_hbm, measured_hbm, primal_hbm, out_ref, dual_ref, measured_ref, primal_ref, sem):
    copies = [
        pltpu.make_async_copy(src, dst, sem.at[i])
        for i, (src, dst) in enumerate(
            ((dual_hbm, dual_ref), (measured_hbm, measured_ref), (primal_hbm, primal_ref))
        )
    ]
    for copy in copies:
        copy.start()
    for copy in copies:
        copy.wait()
    zero = jnp.zeros((1, 1024), F32)
    for z in range(2):
        for c in range(5):
            out_ref[z * 8 + c : z * 8 + c + 1, :] = dual_ref[c, z]
        out_ref[z * 8 + 5 : z * 8 + 6, :] = zero
        out_ref[z * 8 + 6 : z * 8 + 7, :] = measured_ref[z]
        out_ref[z * 8 + 7 : z * 8 + 8, :] = zero
    for k, row in enumerate((0, 3)):
        for c in range(5):
            for z in range(2):
                i = 16 + k * 5 + c
                out_ref[i : i + 1, z * 512 : (z + 1) * 512] = primal_ref[c, z, row : row + 1, :]
    out_ref[26:32, :] = jnp.zeros((6, 1024), F32)


def project_kernel(
    pix_hbm, bin_hbm, cnt_hbm, primal_hbm, w_hbm, after_ref,
    out_ref, wh_ref, wl_ref,
    hi_ref, lo_ref, hot_ref, pix_ref, bin_ref, cnt_ref, primal_ref, w_ref, sem, w_sem,
):
    del after_ref
    t = lax.axis_index("tile")
    copies = [
        pltpu.make_async_copy(src, dst, sem.at[i])
        for i, (src, dst) in enumerate(
            (
                (primal_hbm.at[1], primal_ref),
                (pix_hbm, pix_ref),
                (bin_hbm.at[:, pl.ds(t, 1), :], bin_ref),
                (cnt_hbm, cnt_ref),
            )
        )
    ]
    for copy in copies:
        copy.start()

    def fetch(a):
        return pltpu.make_async_copy(w_hbm.at[0, a], w_ref.at[a], w_sem.at[a])

    for a in range(16):
        fetch(a).start()
    row = lax.broadcasted_iota(jnp.int32, (16, 128), 0)
    for b in range(9):
        hot_ref[b] = jnp.where((row & 7) == b, 1.0, 0.0).astype(BF16)
    out_ref[0, 0] = jnp.zeros((16, 128), F32)
    out_ref[15, 2] = jnp.zeros((16, 128), F32)
    for copy in copies:
        copy.wait()
    for q in range(16):
        r, col = q // 4, (q % 4) * 128
        v = jnp.concatenate(
            [
                jnp.broadcast_to(primal_ref[z, r : r + 1, col : col + 128], (8, 128))
                for z in range(2)
            ],
            0,
        )
        hi_ref[q], lo_ref[q] = split(v)

    def angle(a, carry):
        count = cnt_ref[0, a]
        parts = []
        for s in range(12):
            q = pix_ref[s, 0, a]
            b = jnp.where(s < count, bin_ref[s, 0, a], 8)
            hot = hot_ref[b]
            parts.append(jnp.concatenate([hi_ref[q] * hot, lo_ref[q] * hot], 0))
        left = jnp.concatenate(parts, 1)
        fetch(a).wait()
        w_hi, w_lo = split(w_ref[a].reshape(12 * 128, 128))
        wh_ref[a], wl_ref[a] = w_hi, w_lo
        right = jnp.concatenate([w_hi, w_lo], 1)
        d = jnp.dot(left, right, preferred_element_type=F32)
        res = d[0:16, 0:128] + (d[0:16, 128:256] + d[16:32, 0:128])
        out_ref[a, 1] = res

        @pl.when(a > 0)
        def _():
            out_ref[jnp.maximum(a - 1, 0), 2] = res

        @pl.when(a < 15)
        def _():
            out_ref[jnp.minimum(a + 1, 15), 0] = res

        return carry

    lax.fori_loop(0, 16, angle, 0)


def assemble_kernel(got_ref, own_ref, left_ref, right_ref, primal_ref, sp_ref, sm_ref):
    t = lax.axis_index("tile")
    total = got_ref[0]
    for i in range(1, 16):
        total = total + got_ref[i]
    ok = (t > 0, None, t < 15)
    for k, src in enumerate((left_ref, own_ref, right_ref)):
        keep = (lambda v: v) if ok[k] is None else (lambda v, m=ok[k]: jnp.where(m, v, 0.0))
        for z in range(2):
            base = z * 24 + k * 8
            block = keep(src[z * 8 : z * 8 + 8, :])
            for out in (sp_ref, sm_ref):
                out[base : base + 8, :] = block
                for b in range(8):
                    i = z * 8 + b
                    out[base + 5 : base + 6, b * 128 : (b + 1) * 128] = keep(total[k, i : i + 1, :])
    for z, out in ((0, sm_ref), (1, sp_ref)):
        for row in range(6):
            for c in range(5):
                if row == 0:
                    v = jnp.where(ok[0], left_ref[21 + c : 22 + c, z * 512 : (z + 1) * 512], 0.0)
                elif row == 5:
                    v = jnp.where(ok[2], right_ref[16 + c : 17 + c, z * 512 : (z + 1) * 512], 0.0)
                else:
                    v = primal_ref[c, z, row - 1 : row, :]
                i = row * 5 + c
                lane = (i // 16) * 512
                out[48 + i % 16 : 49 + i % 16, lane : lane + 512] = v
        out[62:64, 512:1024] = jnp.zeros((2, 512), F32)


def dual_kernel_body(
    own_ref, prev_ref, next_ref, kern_ref, mix_ref, bias_ref, slope_ref, shift_ref,
    new_ref, send_ref, tt_ref,
):
    p = lax.axis_index("plane")
    tt_ref[...] = jnp.zeros((72, 96), F32)
    for dz in range(3):
        for da in range(3):
            base = dz * 24 + da * 8
            tt_ref[base : base + 7, :] = jnp.concatenate(
                [kern_ref[dz, da, db] for db in range(3)], 1
            )
    x = jnp.concatenate(
        [
            jnp.where(p > 0, prev_ref[0:48, :], 0.0),
            own_ref[0:48, :],
            jnp.where(p < 7, next_ref[0:48, :], 0.0),
        ],
        0,
    )
    x_hi, x_lo = split(x)
    tt = split(tt_ref[...].T)
    bias, slope, shift = column(bias_ref, 32), column(slope_ref, 32), column(shift_ref, 5)
    mix = split(jnp.concatenate([mix_ref[...], jnp.zeros((3, 32), F32)], 0))
    for z in range(4):
        rows = slice(z * 24, z * 24 + 72)
        h = dot3(tt, (x_hi[rows], x_lo[rows]), ((1,), (0,)))
        h = shifted_sum([h[i * 32 : (i + 1) * 32] for i in range(3)]) + bias
        h = jnp.where(h > 0, h, slope * h)
        out = dot3(mix, split(h), ((1,), (0,))) + shift
        out = out + x[(z + 1) * 24 + 8 : (z + 1) * 24 + 16]
        if z in (1, 2):
            for c in range(5):
                new_ref[c, z - 1] = out[c : c + 1, :]
        for b in range(8):
            piece = jnp.broadcast_to(out[0:1, b * 128 : (b + 1) * 128], (16, 128))
            send_ref[:, b, z, :] = piece


def back_kernel(
    pix_ref, bin_ref, cnt_ref, nd_ref, wh_ref, wl_ref,
    out_ref, up_ref, down_ref, tab_ref, hot_ref, acc_ref,
):
    a = pl.program_id(0)
    t = lax.axis_index("tile")

    @pl.when(a == 0)
    def _():
        row = lax.broadcasted_iota(jnp.int32, (16, 128), 0)
        for q in range(17):
            hot_ref[q] = jnp.where(row == q, 1.0, 0.0).astype(BF16)
        acc_ref[...] = jnp.zeros_like(acc_ref)

    for b in range(8):
        hi, lo = split(
            jnp.concatenate(
                [jnp.broadcast_to(nd_ref[a, b, z : z + 1, :], (16, 128)) for z in range(4)], 0
            )
        )
        tab_ref[b, 0:64] = hi
        tab_ref[b, 64:128] = lo
    count = cnt_ref[0, a]
    parts = []
    for s in range(12):
        q = jnp.where(s < count, pix_ref[s, 0, a], 16)
        hot = hot_ref[q]
        parts.append(tab_ref[bin_ref[s, t, a]] * jnp.concatenate([hot] * 8, 0))
    left = jnp.concatenate(parts, 1)
    right = jnp.concatenate(
        [
            jnp.concatenate([w[a, s * 128 : (s + 1) * 128, :] for s in range(12)], 1)
            for w in (wh_ref, wl_ref)
        ],
        0,
    )
    acc_ref[...] += lax.dot_general(
        left, right, (((1,), (1,)), ((), ())), preferred_element_type=F32
    )

    @pl.when(a == 15)
    def _():
        d = acc_ref[...]
        res = d[0:64, 0:128] + (d[0:64, 128:256] + d[64:128, 0:128])
        out_ref[...] = res
        for z in range(4):
            up_ref[z * 4 : z * 4 + 4, :] = res[z * 16 : z * 16 + 4]
            down_ref[z * 4 : z * 4 + 4, :] = res[z * 16 + 12 : z * 16 + 16]


def primal_kernel_body(
    sp_ref, sm_ref, prev_ref, next_ref, back_ref, above_ref, below_ref, primal_ref, kern_ref,
    mix_ref, bias_ref, slope_ref, shift_ref, new_ref, tt_ref, tb_ref, x_ref, y_ref,
):
    p = lax.axis_index("plane")
    t = lax.axis_index("tile")
    keeps = (p > 0, None, None, p < 7)
    for plane, src in enumerate((prev_ref, sm_ref, sp_ref, next_ref)):
        for half in range(2):
            v = src[48:64, half * 512 : (half + 1) * 512]
            if keeps[plane] is not None:
                v = jnp.where(keeps[plane], v, 0.0)
            x_ref[plane * 32 + half * 16 : plane * 32 + half * 16 + 16, :] = v
    y_ref[...] = jnp.zeros((32, 512), F32)
    for plane in range(4):
        for row in range(6):
            for col in range(4):
                if row == 0:
                    v = jnp.where(t > 0, above_ref[plane * 4 + col : plane * 4 + col + 1, :], 0.0)
                elif row == 5:
                    v = jnp.where(t < 15, below_ref[plane * 4 + col : plane * 4 + col + 1, :], 0.0)
                else:
                    i = plane * 16 + (row - 1) * 4 + col
                    v = back_ref[i : i + 1, :]
                if keeps[plane] is not None:
                    v = jnp.where(keeps[plane], v, 0.0)
                y_ref[plane * 8 + row : plane * 8 + row + 1, col * 128 : (col + 1) * 128] = v
    tt_ref[...] = jnp.zeros((96, 384), F32)
    tb_ref[...] = jnp.zeros((24, 384), F32)
    for dz in range(3):
        for dr in range(3):
            rows = [
                jnp.concatenate([kern_ref[c, dz, dr, db : db + 1, :] for db in range(3)], 1)
                for c in range(6)
            ]
            block = jnp.concatenate(rows, 0)
            for r in range(4):
                i = dz * 32 + (r + dr) * 5
                tt_ref[i : i + 5, r * 96 : (r + 1) * 96] = block[0:5]
                i = dz * 8 + r + dr
                tb_ref[i : i + 1, r * 96 : (r + 1) * 96] = block[5:6]
    tt = split(tt_ref[...].T)
    tb = split(tb_ref[...].T)
    x_hi, x_lo = split(x_ref[...])
    y_hi, y_lo = split(y_ref[...])
    bias, slope, shift = column(bias_ref, 32), column(slope_ref, 32), column(shift_ref, 5)
    mix = split(jnp.concatenate([mix_ref[...], jnp.zeros((3, 32), F32)], 0))
    for z in range(2):
        rows = slice(z * 32, z * 32 + 96)
        h = dot3(tt, (x_hi[rows], x_lo[rows]), ((1,), (0,)))
        rows = slice(z * 8, z * 8 + 24)
        h = h + dot3(tb, (y_hi[rows], y_lo[rows]), ((1,), (0,)))
        for r in range(4):
            g = shifted_sum([h[r * 96 + i * 32 : r * 96 + (i + 1) * 32] for i in range(3)]) + bias
            g = jnp.where(g > 0, g, slope * g)
            out = dot3(mix, split(g), ((1,), (0,))) + shift
            for c in range(5):
                new_ref[c, z, r : r + 1, :] = out[c : c + 1, :] + primal_ref[c, z, r : r + 1, :]


def call(body, outs, in_specs, scratch=(), limit=8 << 20):
    return pl.pallas_call(
        body,
        out_shape=tuple(jax.ShapeDtypeStruct(s, F32) for s in outs),
        in_specs=in_specs,
        out_specs=tuple(VMEM for _ in outs),
        scratch_shapes=list(scratch),
        compiler_params=pltpu.CompilerParams(vmem_limit_bytes=limit),
    )


def ring(array, axis, step):
    count = lax.axis_size(axis)
    return lax.ppermute(array, axis, [(i, (i + step) % count) for i in range(count)])


def per_device(
    primal, dual, measured, footprint_weights, pixel_index, bin_index, slot_count,
    dual_kernel, dual_bias, dual_slope, dual_mixing, dual_shift,
    primal_kernel, primal_bias, primal_slope, primal_mixing, primal_shift,
):
    pix = jnp.transpose(pixel_index, (2, 0, 1))
    bins = jnp.transpose(bin_index, (2, 0, 1))
    hbm = lambda x: pltpu.with_memory_space_constraint(x, pltpu.HBM)

    own = call(
        pack_kernel, [(32, 1024)], [HBM] * 3,
        [
            pltpu.VMEM((5, 2, 1, 1024), F32),
            pltpu.VMEM((2, 1, 1024), F32),
            pltpu.VMEM((5, 2, 4, 512), F32),
            pltpu.SemaphoreType.DMA((3,)),
        ],
    )(hbm(dual), hbm(measured), hbm(primal))[0]
    left = ring(own, "tile", 1)
    right = ring(own, "tile", -1)

    terms, w_hi, w_lo = pl.pallas_call(
        project_kernel,
        name="project",
        out_shape=(
            jax.ShapeDtypeStruct((16, 3, 16, 128), F32),
            jax.ShapeDtypeStruct((16, 1536, 128), BF16),
            jax.ShapeDtypeStruct((16, 1536, 128), BF16),
        ),
        in_specs=[HBM] * 5 + [VMEM],
        out_specs=(VMEM, VMEM, VMEM),
        scratch_shapes=[pltpu.VMEM((16, 16, 128), BF16)] * 3
        + [
            pltpu.SMEM((12, 1, 16), jnp.int32),
            pltpu.SMEM((12, 1, 16), jnp.int32),
            pltpu.SMEM((1, 16), jnp.int32),
            pltpu.VMEM((2, 4, 512), F32),
            pltpu.VMEM((16, 12, 128, 128), F32),
            pltpu.SemaphoreType.DMA((4,)),
            pltpu.SemaphoreType.DMA((16,)),
        ],
        compiler_params=pltpu.CompilerParams(vmem_limit_bytes=18 << 20),
        cost_estimate=pl.CostEstimate(flops=1 << 31, bytes_accessed=25 << 20, transcendentals=0),
    )(hbm(pix), hbm(bins), hbm(slot_count), hbm(primal), hbm(footprint_weights), own)
    terms, left, right = lax.optimization_barrier((terms, left, right))
    got = lax.all_to_all(terms, "tile", 0, 0, tiled=True)

    sp, sm = call(assemble_kernel, [(64, 1024)] * 2, [VMEM] * 5)(got, own, left, right, primal)
    prev = ring(sp, "plane", 1)
    after = ring(sm, "plane", -1)

    new_dual, send = call(
        dual_kernel_body, [(5, 2, 1, 1024), (16, 8, 4, 128)],
        [VMEM] * 5 + [SMEM] * 3, [pltpu.VMEM((72, 96), F32)],
    )(
        sp, prev, after, jnp.transpose(dual_kernel, (2, 3, 4, 1, 0)), dual_mixing,
        dual_bias, dual_slope, dual_shift,
    )
    leading = lax.all_to_all(send, "tile", 0, 0, tiled=True)

    back, up, down = pl.pallas_call(
        back_kernel,
        name="back",
        grid=(16,),
        out_shape=(
            jax.ShapeDtypeStruct((64, 128), F32),
            jax.ShapeDtypeStruct((16, 128), F32),
            jax.ShapeDtypeStruct((16, 128), F32),
        ),
        in_specs=[SMEM, SMEM, SMEM, VMEM, VMEM, VMEM],
        out_specs=(VMEM, VMEM, VMEM),
        scratch_shapes=[
            pltpu.VMEM((8, 128, 128), BF16),
            pltpu.VMEM((17, 16, 128), BF16),
            pltpu.VMEM((128, 256), F32),
        ],
        compiler_params=pltpu.CompilerParams(
            vmem_limit_bytes=4 << 20, dimension_semantics=("arbitrary",)
        ),
    )(pix, bins, slot_count, leading, w_hi, w_lo)
    above = ring(down, "tile", 1)
    below = ring(up, "tile", -1)

    new_primal = call(
        primal_kernel_body, [(5, 2, 4, 512)], [VMEM] * 10 + [SMEM] * 3,
        [
            pltpu.VMEM((96, 384), F32),
            pltpu.VMEM((24, 384), F32),
            pltpu.VMEM((128, 512), F32),
            pltpu.VMEM((32, 512), F32),
        ],
    )(
        sp, sm, prev, after, back, above, below, primal,
        jnp.transpose(primal_kernel, (1, 2, 3, 4, 0)), primal_mixing,
        primal_bias, primal_slope, primal_shift,
    )[0]
    return new_primal, new_dual


def solution(mesh):
    grid = P(None, "plane", "tile", None)
    in_specs = (
        grid, grid, P("plane", "tile", None), P("tile", None, None, None, None),
        P("tile", None, None), P(), P("tile", None),
    ) + (P(),) * 10
    return jax.shard_map(
        per_device, mesh=mesh, in_specs=in_specs, out_specs=(grid, grid), check_vma=False
    )
```

```python
import jax
import jax.numpy as jnp
from jax import lax
from jax.experimental import pallas as pl
from jax.experimental.pallas import tpu as pltpu
from jax.sharding import PartitionSpec as P


F32 = jnp.float32
BF16 = jnp.bfloat16
VMEM = pl.BlockSpec(memory_space=pltpu.VMEM)
SMEM = pl.BlockSpec(memory_space=pltpu.SMEM)
HBM = pl.BlockSpec(memory_space=pltpu.HBM)


def split(x):
    hi = x.astype(BF16)
    return hi, (x - hi.astype(F32)).astype(BF16)


def joined(a):
    hi, lo = split(a)
    return jnp.concatenate([hi, lo, hi], 1)


def dot3(left, b):
    hi, lo = split(b)
    return jnp.dot(left, jnp.concatenate([hi, hi, lo], 0), preferred_element_type=F32)


def column(ref, count):
    rows = -(-count // 8) * 8
    index = lax.broadcasted_iota(jnp.int32, (rows, 128), 0)
    out = jnp.zeros((rows, 128), F32)
    for i in range(count):
        out = jnp.where(index == i, ref[i], out)
    return out[:, 0:1]


def shifted_sum(stack):
    left, mid, right = stack
    width = mid.shape[1]
    lane = lax.broadcasted_iota(jnp.int32, mid.shape, 1)
    left = jnp.where(lane == 0, 0.0, pltpu.roll(left, 1, 1))
    right = jnp.where(lane == width - 1, 0.0, pltpu.roll(right, width - 1, 1))
    return left + mid + right


def pack_kernel(dual_hbm, measured_hbm, primal_hbm, out_ref, dual_ref, measured_ref, primal_ref, sem):
    copies = [
        pltpu.make_async_copy(src, dst, sem.at[i])
        for i, (src, dst) in enumerate(
            ((dual_hbm, dual_ref), (measured_hbm, measured_ref), (primal_hbm, primal_ref))
        )
    ]
    for copy in copies:
        copy.start()
    for copy in copies:
        copy.wait()
    zero = jnp.zeros((1, 1024), F32)
    for z in range(2):
        for c in range(5):
            out_ref[z * 8 + c : z * 8 + c + 1, :] = dual_ref[c, z]
        out_ref[z * 8 + 5 : z * 8 + 6, :] = zero
        out_ref[z * 8 + 6 : z * 8 + 7, :] = measured_ref[z]
        out_ref[z * 8 + 7 : z * 8 + 8, :] = zero
    for k, row in enumerate((0, 3)):
        for c in range(5):
            for z in range(2):
                i = 16 + k * 5 + c
                out_ref[i : i + 1, z * 512 : (z + 1) * 512] = primal_ref[c, z, row : row + 1, :]
    out_ref[26:32, :] = jnp.zeros((6, 1024), F32)


def project_kernel(
    pix_hbm, bin_hbm, cnt_hbm, primal_hbm, w_hbm, after_ref,
    final_ref, wh_ref, wl_ref,
    out_ref, hi_ref, lo_ref, hot_ref, pix_ref, bin_ref, cnt_ref, primal_ref, w_ref, sem, w_sem,
):
    del after_ref
    t = lax.axis_index("tile")
    copies = [
        pltpu.make_async_copy(src, dst, sem.at[i])
        for i, (src, dst) in enumerate(
            (
                (primal_hbm.at[1], primal_ref),
                (pix_hbm, pix_ref),
                (bin_hbm.at[:, pl.ds(t, 1), :], bin_ref),
                (cnt_hbm, cnt_ref),
            )
        )
    ]
    for copy in copies:
        copy.start()

    def fetch(i):
        part = pl.ds(i * 2, 2)
        return pltpu.make_async_copy(w_hbm.at[0, part], w_ref.at[part], w_sem.at[i])

    for i in range(8):
        fetch(i).start()
    row = lax.broadcasted_iota(jnp.int32, (16, 128), 0)
    for b in range(9):
        hot_ref[b] = jnp.where((row & 7) == b, 1.0, 0.0).astype(BF16)
    out_ref[1, 0] = jnp.zeros((16, 128), F32)
    out_ref[16, 2] = jnp.zeros((16, 128), F32)
    for copy in copies:
        copy.wait()
    for q in range(16):
        r, col = q // 4, (q % 4) * 128
        v = jnp.concatenate(
            [
                jnp.broadcast_to(primal_ref[z, r : r + 1, col : col + 128], (8, 128))
                for z in range(2)
            ],
            0,
        )
        hi_ref[q], lo_ref[q] = split(v)

    def angle(a):
        count = cnt_ref[0, a]
        parts = []
        for s in range(12):
            q = pix_ref[s, 0, a]
            b = jnp.where(s < count, bin_ref[s, 0, a], 8)
            hot = hot_ref[b]
            parts.append(jnp.concatenate([hi_ref[q] * hot, lo_ref[q] * hot], 0))
        left = jnp.concatenate(parts, 1)
        w_hi, w_lo = split(w_ref[a].reshape(12 * 128, 128))
        wh_ref[a], wl_ref[a] = w_hi, w_lo
        right = jnp.concatenate([w_hi, w_lo], 1)
        d = jnp.dot(left, right, preferred_element_type=F32)
        res = d[0:16, 0:128] + (d[0:16, 128:256] + d[16:32, 0:128])
        out_ref[a + 1, 1] = res
        out_ref[a, 2] = res
        out_ref[a + 2, 0] = res

    def chunk(i, carry):
        fetch(i).wait()
        angle(i * 2)
        angle(i * 2 + 1)
        return carry

    lax.fori_loop(0, 8, chunk, 0)
    final_ref[...] = out_ref[1:17]


def assemble_kernel(got_ref, own_ref, left_ref, right_ref, primal_ref, sp_ref, sm_ref):
    t = lax.axis_index("tile")
    total = got_ref[0]
    for i in range(1, 16):
        total = total + got_ref[i]
    ok = (t > 0, None, t < 15)
    for k, src in enumerate((left_ref, own_ref, right_ref)):
        keep = (lambda v: v) if ok[k] is None else (lambda v, m=ok[k]: jnp.where(m, v, 0.0))
        for z in range(2):
            base = z * 24 + k * 8
            block = keep(src[z * 8 : z * 8 + 8, :])
            for out in (sp_ref, sm_ref):
                out[base : base + 8, :] = block
                for b in range(8):
                    i = z * 8 + b
                    out[base + 5 : base + 6, b * 128 : (b + 1) * 128] = keep(total[k, i : i + 1, :])
    for z, out in ((0, sm_ref), (1, sp_ref)):
        for row in range(6):
            for c in range(5):
                if row == 0:
                    v = jnp.where(ok[0], left_ref[21 + c : 22 + c, z * 512 : (z + 1) * 512], 0.0)
                elif row == 5:
                    v = jnp.where(ok[2], right_ref[16 + c : 17 + c, z * 512 : (z + 1) * 512], 0.0)
                else:
                    v = primal_ref[c, z, row - 1 : row, :]
                i = row * 5 + c
                lane = (i // 16) * 512
                out[48 + i % 16 : 49 + i % 16, lane : lane + 512] = v
        out[62:64, 512:1024] = jnp.zeros((2, 512), F32)


def dual_kernel_body(
    own_ref, prev_ref, next_ref, kern_ref, mix_ref, bias_ref, slope_ref, shift_ref,
    new_ref, send_ref, tt_ref,
):
    p = lax.axis_index("plane")
    tt_ref[...] = jnp.zeros((80, 96), F32)
    for dz in range(3):
        for da in range(3):
            base = dz * 24 + da * 8
            tt_ref[base : base + 7, :] = jnp.concatenate(
                [kern_ref[dz, da, db] for db in range(3)], 1
            )
    x = jnp.concatenate(
        [
            jnp.where(p > 0, prev_ref[0:48, :], 0.0),
            own_ref[0:48, :],
            jnp.where(p < 7, next_ref[0:48, :], 0.0),
            jnp.zeros((8, 1024), F32),
        ],
        0,
    )
    tt = joined(tt_ref[...].T)
    bias, slope, shift = column(bias_ref, 32), column(slope_ref, 32), column(shift_ref, 5)
    mix = joined(jnp.concatenate([mix_ref[...], jnp.zeros((3, 32), F32)], 0))
    for z in range(4):
        h = dot3(tt, x[z * 24 : z * 24 + 80])
        h = shifted_sum([h[i * 32 : (i + 1) * 32] for i in range(3)]) + bias
        h = jnp.where(h > 0, h, slope * h)
        out = dot3(mix, h) + shift
        out = out + x[(z + 1) * 24 + 8 : (z + 1) * 24 + 16]
        if z in (1, 2):
            for c in range(5):
                new_ref[c, z - 1] = out[c : c + 1, :]
        for b in range(8):
            piece = jnp.broadcast_to(out[0:1, b * 128 : (b + 1) * 128], (16, 128))
            send_ref[:, b, z, :] = piece


def back_kernel(
    pix_ref, bin_ref, cnt_ref, nd_ref, wh_ref, wl_ref,
    out_ref, up_ref, down_ref, tab_ref, acc_ref,
):
    t = lax.axis_index("tile")
    for a in range(16):
        for b in range(8):
            v = nd_ref[a, b]
            hi = v.astype(BF16).astype(F32)
            tab_ref[a, b, 0:4] = hi
            tab_ref[a, b, 4:8] = v - hi
    acc_ref[...] = jnp.zeros_like(acc_ref)
    zero = jnp.zeros((8, 128), F32)

    def angle(a):
        count = cnt_ref[0, a]
        for s in range(0, 12, 2):
            one, two = (tab_ref[a, bin_ref[s + i, t, a]] for i in range(2))
            left = jnp.concatenate(
                [jnp.concatenate([one, zero], 1), jnp.concatenate([zero, two], 1)], 0
            ).astype(BF16)
            right = jnp.concatenate(
                [
                    jnp.concatenate(
                        [w[a, (s + i) * 128 : (s + i + 1) * 128, :] for i in range(2)], 1
                    )
                    for w in (wh_ref, wl_ref)
                ],
                0,
            )
            d = lax.dot_general(
                left, right, (((1,), (1,)), ((), ())), preferred_element_type=F32
            )
            d = d[:, 0:128] + d[:, 128:256]
            for i in range(2):
                q = jnp.where(s + i < count, pix_ref[s + i, 0, a], 16)
                acc_ref[q] += d[i * 8 : i * 8 + 8]

    def chunk(i, carry):
        for k in range(4):
            angle(i * 4 + k)
        return carry

    lax.fori_loop(0, 4, chunk, 0)
    for q in range(16):
        v = acc_ref[q, 0:4] + acc_ref[q, 4:8]
        out_ref[q * 4 : q * 4 + 4, :] = v
        if q < 4:
            up_ref[q * 4 : q * 4 + 4, :] = v
        if q >= 12:
            down_ref[q * 4 - 48 : q * 4 - 44, :] = v


def primal_kernel_body(
    sp_ref, sm_ref, prev_ref, next_ref, back_ref, above_ref, below_ref, primal_ref, kern_ref,
    mix_ref, bias_ref, slope_ref, shift_ref, new_ref, tt_ref, tb_ref, x_ref, y_ref,
):
    p = lax.axis_index("plane")
    t = lax.axis_index("tile")
    keeps = (p > 0, None, None, p < 7)
    for plane, src in enumerate((prev_ref, sm_ref, sp_ref, next_ref)):
        for half in range(2):
            v = src[48:64, half * 512 : (half + 1) * 512]
            if keeps[plane] is not None:
                v = jnp.where(keeps[plane], v, 0.0)
            x_ref[plane * 32 + half * 16 : plane * 32 + half * 16 + 16, :] = v
    y_ref[...] = jnp.zeros((40, 512), F32)
    for plane in range(4):
        for row in range(6):
            for col in range(4):
                if row == 0:
                    v = jnp.where(t > 0, above_ref[col * 4 + plane : col * 4 + plane + 1, :], 0.0)
                elif row == 5:
                    v = jnp.where(t < 15, below_ref[col * 4 + plane : col * 4 + plane + 1, :], 0.0)
                else:
                    i = (row * 4 - 4 + col) * 4 + plane
                    v = back_ref[i : i + 1, :]
                if keeps[plane] is not None:
                    v = jnp.where(keeps[plane], v, 0.0)
                y_ref[plane * 8 + row : plane * 8 + row + 1, col * 128 : (col + 1) * 128] = v
    tt_ref[...] = jnp.zeros((96, 384), F32)
    tb_ref[...] = jnp.zeros((32, 384), F32)
    for dz in range(3):
        for dr in range(3):
            rows = [
                jnp.concatenate([kern_ref[c, dz, dr, db : db + 1, :] for db in range(3)], 1)
                for c in range(6)
            ]
            block = jnp.concatenate(rows, 0)
            for r in range(4):
                i = dz * 32 + (r + dr) * 5
                tt_ref[i : i + 5, r * 96 : (r + 1) * 96] = block[0:5]
                i = dz * 8 + r + dr
                tb_ref[i : i + 1, r * 96 : (r + 1) * 96] = block[5:6]
    tt = joined(jnp.concatenate([tt_ref[...], tb_ref[...]], 0).T)
    bias, slope, shift = column(bias_ref, 32), column(slope_ref, 32), column(shift_ref, 5)
    mix = joined(jnp.concatenate([mix_ref[...], jnp.zeros((3, 32), F32)], 0))
    for z in range(2):
        rows = [x_ref[z * 32 : z * 32 + 96], y_ref[z * 8 : z * 8 + 32]]
        h = dot3(tt, jnp.concatenate(rows, 0))
        for r in range(4):
            g = shifted_sum([h[r * 96 + i * 32 : r * 96 + (i + 1) * 32] for i in range(3)]) + bias
            g = jnp.where(g > 0, g, slope * g)
            out = dot3(mix, g) + shift
            for c in range(5):
                new_ref[c, z, r : r + 1, :] = out[c : c + 1, :] + primal_ref[c, z, r : r + 1, :]


def call(body, outs, in_specs, scratch=(), limit=8 << 20):
    return pl.pallas_call(
        body,
        out_shape=tuple(jax.ShapeDtypeStruct(s, F32) for s in outs),
        in_specs=in_specs,
        out_specs=tuple(VMEM for _ in outs),
        scratch_shapes=list(scratch),
        compiler_params=pltpu.CompilerParams(vmem_limit_bytes=limit),
    )


def ring(array, axis, step):
    count = lax.axis_size(axis)
    return lax.ppermute(array, axis, [(i, (i + step) % count) for i in range(count)])


def per_device(
    primal, dual, measured, footprint_weights, pixel_index, bin_index, slot_count,
    dual_kernel, dual_bias, dual_slope, dual_mixing, dual_shift,
    primal_kernel, primal_bias, primal_slope, primal_mixing, primal_shift,
):
    pix = jnp.transpose(pixel_index, (2, 0, 1))
    bins = jnp.transpose(bin_index, (2, 0, 1))
    hbm = lambda x: pltpu.with_memory_space_constraint(x, pltpu.HBM)

    own = call(
        pack_kernel, [(32, 1024)], [HBM] * 3,
        [
            pltpu.VMEM((5, 2, 1, 1024), F32),
            pltpu.VMEM((2, 1, 1024), F32),
            pltpu.VMEM((5, 2, 4, 512), F32),
            pltpu.SemaphoreType.DMA((3,)),
        ],
    )(hbm(dual), hbm(measured), hbm(primal))[0]
    left = ring(own, "tile", 1)
    right = ring(own, "tile", -1)

    terms, w_hi, w_lo = pl.pallas_call(
        project_kernel,
        name="project",
        out_shape=(
            jax.ShapeDtypeStruct((16, 3, 16, 128), F32),
            jax.ShapeDtypeStruct((16, 1536, 128), BF16),
            jax.ShapeDtypeStruct((16, 1536, 128), BF16),
        ),
        in_specs=[HBM] * 5 + [VMEM],
        out_specs=(VMEM, VMEM, VMEM),
        scratch_shapes=[pltpu.VMEM((18, 3, 16, 128), F32)]
        + [pltpu.VMEM((16, 16, 128), BF16)] * 3
        + [
            pltpu.SMEM((12, 1, 16), jnp.int32),
            pltpu.SMEM((12, 1, 16), jnp.int32),
            pltpu.SMEM((1, 16), jnp.int32),
            pltpu.VMEM((2, 4, 512), F32),
            pltpu.VMEM((16, 12, 128, 128), F32),
            pltpu.SemaphoreType.DMA((4,)),
            pltpu.SemaphoreType.DMA((8,)),
        ],
        compiler_params=pltpu.CompilerParams(vmem_limit_bytes=18 << 20),
        cost_estimate=pl.CostEstimate(flops=1 << 31, bytes_accessed=25 << 20, transcendentals=0),
    )(hbm(pix), hbm(bins), hbm(slot_count), hbm(primal), hbm(footprint_weights), own)
    terms, left, right = lax.optimization_barrier((terms, left, right))
    got = lax.all_to_all(terms, "tile", 0, 0, tiled=True)

    sp, sm = call(assemble_kernel, [(64, 1024)] * 2, [VMEM] * 5)(got, own, left, right, primal)
    prev = ring(sp, "plane", 1)
    after = ring(sm, "plane", -1)

    new_dual, send = call(
        dual_kernel_body, [(5, 2, 1, 1024), (16, 8, 4, 128)],
        [VMEM] * 5 + [SMEM] * 3, [pltpu.VMEM((80, 96), F32)],
    )(
        sp, prev, after, jnp.transpose(dual_kernel, (2, 3, 4, 1, 0)), dual_mixing,
        dual_bias, dual_slope, dual_shift,
    )
    leading = lax.all_to_all(send, "tile", 0, 0, tiled=True)

    back, up, down = pl.pallas_call(
        back_kernel,
        name="back",
        out_shape=(
            jax.ShapeDtypeStruct((64, 128), F32),
            jax.ShapeDtypeStruct((16, 128), F32),
            jax.ShapeDtypeStruct((16, 128), F32),
        ),
        in_specs=[SMEM, SMEM, SMEM, VMEM, VMEM, VMEM],
        out_specs=(VMEM, VMEM, VMEM),
        scratch_shapes=[pltpu.VMEM((16, 8, 8, 128), F32), pltpu.VMEM((17, 8, 128), F32)],
        compiler_params=pltpu.CompilerParams(vmem_limit_bytes=4 << 20),
    )(pix, bins, slot_count, leading, w_hi, w_lo)
    above = ring(down, "tile", 1)
    below = ring(up, "tile", -1)

    new_primal = call(
        primal_kernel_body, [(5, 2, 4, 512)], [VMEM] * 10 + [SMEM] * 3,
        [
            pltpu.VMEM((96, 384), F32),
            pltpu.VMEM((32, 384), F32),
            pltpu.VMEM((128, 512), F32),
            pltpu.VMEM((40, 512), F32),
        ],
    )(
        sp, sm, prev, after, back, above, below, primal,
        jnp.transpose(primal_kernel, (1, 2, 3, 4, 0)), primal_mixing,
        primal_bias, primal_slope, primal_shift,
    )[0]
    return new_primal, new_dual


def solution(mesh):
    grid = P(None, "plane", "tile", None)
    in_specs = (
        grid, grid, P("plane", "tile", None), P("tile", None, None, None, None),
        P("tile", None, None), P(), P("tile", None),
    ) + (P(),) * 10
    return jax.shard_map(
        per_device, mesh=mesh, in_specs=in_specs, out_specs=(grid, grid), check_vma=False
    )
```

```python
import jax
import jax.numpy as jnp
from jax import lax
from jax.experimental import pallas as pl
from jax.experimental.pallas import tpu as pltpu
from jax.sharding import PartitionSpec as P


F32 = jnp.float32
BF16 = jnp.bfloat16
VMEM = pl.BlockSpec(memory_space=pltpu.VMEM)
SMEM = pl.BlockSpec(memory_space=pltpu.SMEM)
HBM = pl.BlockSpec(memory_space=pltpu.HBM)


def split(x):
    hi = x.astype(BF16)
    return hi, (x - hi.astype(F32)).astype(BF16)


def joined(a):
    hi, lo = split(a)
    return jnp.concatenate([hi, lo, hi], 1)


def dot3(left, b):
    hi, lo = split(b)
    return jnp.dot(left, jnp.concatenate([hi, hi, lo], 0), preferred_element_type=F32)


def column(ref, count):
    rows = -(-count // 8) * 8
    index = lax.broadcasted_iota(jnp.int32, (rows, 128), 0)
    out = jnp.zeros((rows, 128), F32)
    for i in range(count):
        out = jnp.where(index == i, ref[i], out)
    return out[:, 0:1]


def shifted_sum(stack):
    left, mid, right = stack
    width = mid.shape[1]
    lane = lax.broadcasted_iota(jnp.int32, mid.shape, 1)
    left = jnp.where(lane == 0, 0.0, pltpu.roll(left, 1, 1))
    right = jnp.where(lane == width - 1, 0.0, pltpu.roll(right, width - 1, 1))
    return left + mid + right


def pack_kernel(dual_hbm, measured_hbm, primal_hbm, out_ref, dual_ref, measured_ref, primal_ref, sem):
    copies = [
        pltpu.make_async_copy(src, dst, sem.at[i])
        for i, (src, dst) in enumerate(
            ((dual_hbm, dual_ref), (measured_hbm, measured_ref), (primal_hbm, primal_ref))
        )
    ]
    for copy in copies:
        copy.start()
    for copy in copies:
        copy.wait()
    zero = jnp.zeros((1, 1024), F32)
    for z in range(2):
        for c in range(5):
            out_ref[z * 8 + c : z * 8 + c + 1, :] = dual_ref[c, z]
        out_ref[z * 8 + 5 : z * 8 + 6, :] = zero
        out_ref[z * 8 + 6 : z * 8 + 7, :] = measured_ref[z]
        out_ref[z * 8 + 7 : z * 8 + 8, :] = zero
    for k, row in enumerate((0, 3)):
        for c in range(5):
            for z in range(2):
                i = 16 + k * 5 + c
                out_ref[i : i + 1, z * 512 : (z + 1) * 512] = primal_ref[c, z, row : row + 1, :]
    out_ref[26:32, :] = jnp.zeros((6, 1024), F32)


def project_kernel(
    pix_hbm, bin_hbm, cnt_hbm, primal_hbm, w_hbm, after_ref,
    final_ref, wh_ref, wl_ref,
    out_ref, hi_ref, lo_ref, hot_ref, pix_ref, bin_ref, cnt_ref, primal_ref, w_ref, sem, w_sem,
):
    del after_ref
    t = lax.axis_index("tile")
    copies = [
        pltpu.make_async_copy(src, dst, sem.at[i])
        for i, (src, dst) in enumerate(
            (
                (primal_hbm.at[1], primal_ref),
                (pix_hbm, pix_ref),
                (bin_hbm.at[:, pl.ds(t, 1), :], bin_ref),
                (cnt_hbm, cnt_ref),
            )
        )
    ]
    for copy in copies:
        copy.start()

    def fetch(i):
        part = pl.ds(i * 2, 2)
        return pltpu.make_async_copy(w_hbm.at[0, part], w_ref.at[part], w_sem.at[i])

    for i in range(8):
        fetch(i).start()
    row = lax.broadcasted_iota(jnp.int32, (16, 128), 0)
    for b in range(9):
        hot_ref[b] = jnp.where((row & 7) == b, 1.0, 0.0).astype(BF16)
    out_ref[1, 0] = jnp.zeros((16, 128), F32)
    out_ref[16, 2] = jnp.zeros((16, 128), F32)
    for copy in copies:
        copy.wait()
    for q in range(16):
        r, col = q // 4, (q % 4) * 128
        v = jnp.concatenate(
            [
                jnp.broadcast_to(primal_ref[z, r : r + 1, col : col + 128], (8, 128))
                for z in range(2)
            ],
            0,
        )
        hi_ref[q], lo_ref[q] = split(v)

    def angle(a):
        count = cnt_ref[0, a]
        parts = []
        for s in range(12):
            q = pix_ref[s, 0, a]
            b = jnp.where(s < count, bin_ref[s, 0, a], 8)
            hot = hot_ref[b]
            parts.append(jnp.concatenate([hi_ref[q] * hot, lo_ref[q] * hot], 0))
        left = jnp.concatenate(parts, 1)
        w_hi, w_lo = split(w_ref[a].reshape(12 * 128, 128))
        wh_ref[a], wl_ref[a] = w_hi, w_lo
        right = jnp.concatenate([w_hi, w_lo], 1)
        d = jnp.dot(left, right, preferred_element_type=F32)
        res = d[0:16, 0:128] + (d[0:16, 128:256] + d[16:32, 0:128])
        out_ref[a + 1, 1] = res
        out_ref[a, 2] = res
        out_ref[a + 2, 0] = res

    def chunk(i, carry):
        fetch(i).wait()
        angle(i * 2)
        angle(i * 2 + 1)
        return carry

    lax.fori_loop(0, 8, chunk, 0)
    final_ref[...] = out_ref[1:17]


def rims_kernel(own_ref, left_ref, right_ref, primal_ref, sp_ref, sm_ref):
    t = lax.axis_index("tile")
    ok = (t > 0, None, t < 15)
    for k, src in enumerate((left_ref, own_ref, right_ref)):
        for z in range(2):
            base = z * 24 + k * 8
            block = src[z * 8 : z * 8 + 8, :]
            if ok[k] is not None:
                block = jnp.where(ok[k], block, 0.0)
            for out in (sp_ref, sm_ref):
                out[base : base + 8, :] = block
    for z, out in ((0, sm_ref), (1, sp_ref)):
        for row in range(6):
            for c in range(5):
                if row == 0:
                    v = jnp.where(ok[0], left_ref[21 + c : 22 + c, z * 512 : (z + 1) * 512], 0.0)
                elif row == 5:
                    v = jnp.where(ok[2], right_ref[16 + c : 17 + c, z * 512 : (z + 1) * 512], 0.0)
                else:
                    v = primal_ref[c, z, row - 1 : row, :]
                i = row * 5 + c
                lane = (i // 16) * 512
                out[48 + i % 16 : 49 + i % 16, lane : lane + 512] = v
        out[62:64, 512:1024] = jnp.zeros((2, 512), F32)


def total_kernel(got_ref, out_ref):
    t = lax.axis_index("tile")
    for k, ok in enumerate((t > 0, None, t < 15)):
        total = got_ref[0, k]
        for i in range(1, 16):
            total = total + got_ref[i, k]
        if ok is not None:
            total = jnp.where(ok, total, 0.0)
        out_ref[k * 16 : k * 16 + 16, :] = total


def dual_inputs(own_ref, prev_ref, next_ref):
    p = lax.axis_index("plane")
    return jnp.concatenate(
        [
            jnp.where(p > 0, prev_ref[0:48, :], 0.0),
            own_ref[0:48, :],
            jnp.where(p < 7, next_ref[0:48, :], 0.0),
            jnp.zeros((8, 1024), F32),
        ],
        0,
    )


def dual_known_kernel(
    own_ref, prev_ref, next_ref, kern_ref, bias_ref, known_ref, last_ref, tt_ref, lt_ref
):
    tt_ref[...] = jnp.zeros((80, 96), F32)
    lt_ref[...] = jnp.zeros((80, 128), F32)
    for dz in range(3):
        for da in range(3):
            tiles = [kern_ref[dz, da, db] for db in range(3)]
            base = dz * 24 + da * 8
            tt_ref[base : base + 7, :] = jnp.concatenate(tiles, 1)
            for db in range(3):
                four = jnp.concatenate([tiles[db][5:6]] * 4, 1)
                for z in range(4):
                    i = db * 24 + (z + dz) * 3 + da
                    lt_ref[i : i + 1, z * 32 : (z + 1) * 32] = four[:, z * 32 : (z + 1) * 32]
    last_ref[...] = joined(lt_ref[...].T)
    x = dual_inputs(own_ref, prev_ref, next_ref)
    tt = joined(tt_ref[...].T)
    bias = column(bias_ref, 32)
    for z in range(4):
        h = dot3(tt, x[z * 24 : z * 24 + 80])
        h = shifted_sum([h[i * 32 : (i + 1) * 32] for i in range(3)]) + bias
        known_ref[z * 32 : (z + 1) * 32, :] = h


def spread_columns(y_ref, width):
    mid = y_ref[24:48, :]
    lane = lax.broadcasted_iota(jnp.int32, mid.shape, 1)
    y_ref[0:24, :] = jnp.where(lane == 0, 0.0, pltpu.roll(mid, 1, 1))
    y_ref[48:72, :] = jnp.where(lane == width - 1, 0.0, pltpu.roll(mid, width - 1, 1))


def dual_kernel_body(
    total_ref, tprev_ref, tnext_ref, own_ref, prev_ref, next_ref, known_ref, last_ref,
    mix_ref, slope_ref, shift_ref, new_ref, send_ref, y_ref,
):
    p = lax.axis_index("plane")
    y_ref[...] = jnp.zeros((80, 1024), F32)
    for first, src, keep in ((0, tprev_ref, p > 0), (2, total_ref, None), (4, tnext_ref, p < 7)):
        v = src[...]
        if keep is not None:
            v = jnp.where(keep, v, 0.0)
        for k in range(3):
            for z in range(2):
                row = 24 + (first + z) * 3 + k
                for b in range(8):
                    i = k * 16 + z * 8 + b
                    y_ref[row : row + 1, b * 128 : (b + 1) * 128] = v[i : i + 1]
    spread_columns(y_ref, 1024)
    slope, shift = column(slope_ref, 32), column(shift_ref, 5)
    mix = joined(jnp.concatenate([mix_ref[...], jnp.zeros((3, 32), F32)], 0))
    h = dot3(last_ref[...], y_ref[...]) + known_ref[...]
    dual_rows = (
        jnp.where(p > 0, prev_ref[32:40, :], 0.0), own_ref[8:16, :], own_ref[32:40, :],
        jnp.where(p < 7, next_ref[8:16, :], 0.0),
    )
    for z in range(4):
        g = h[z * 32 : (z + 1) * 32]
        g = jnp.where(g > 0, g, slope * g)
        out = dot3(mix, g) + shift + dual_rows[z]
        if z in (1, 2):
            for c in range(5):
                new_ref[c, z - 1] = out[c : c + 1, :]
        for b in range(8):
            piece = jnp.broadcast_to(out[0:1, b * 128 : (b + 1) * 128], (16, 128))
            send_ref[:, b, z, :] = piece


def back_kernel(
    pix_ref, bin_ref, cnt_ref, nd_ref, wh_ref, wl_ref,
    out_ref, up_ref, down_ref, tab_ref, acc_ref,
):
    t = lax.axis_index("tile")
    for a in range(16):
        for b in range(8):
            v = nd_ref[a, b]
            hi = v.astype(BF16).astype(F32)
            tab_ref[a, b, 0:4] = hi
            tab_ref[a, b, 4:8] = v - hi
    acc_ref[...] = jnp.zeros_like(acc_ref)
    zero = jnp.zeros((8, 128), F32)

    def angle(a):
        count = cnt_ref[0, a]
        for s in range(0, 12, 2):
            one, two = (tab_ref[a, bin_ref[s + i, t, a]] for i in range(2))
            left = jnp.concatenate(
                [jnp.concatenate([one, zero], 1), jnp.concatenate([zero, two], 1)], 0
            ).astype(BF16)
            right = jnp.concatenate(
                [
                    jnp.concatenate(
                        [w[a, (s + i) * 128 : (s + i + 1) * 128, :] for i in range(2)], 1
                    )
                    for w in (wh_ref, wl_ref)
                ],
                0,
            )
            d = lax.dot_general(
                left, right, (((1,), (1,)), ((), ())), preferred_element_type=F32
            )
            d = d[:, 0:128] + d[:, 128:256]
            for i in range(2):
                q = jnp.where(s + i < count, pix_ref[s + i, 0, a], 16)
                acc_ref[q] += d[i * 8 : i * 8 + 8]

    def chunk(i, carry):
        for k in range(4):
            angle(i * 4 + k)
        return carry

    lax.fori_loop(0, 4, chunk, 0)
    for q in range(16):
        v = acc_ref[q, 0:4] + acc_ref[q, 4:8]
        out_ref[q * 4 : q * 4 + 4, :] = v
        if q < 4:
            up_ref[q * 4 : q * 4 + 4, :] = v
        if q >= 12:
            down_ref[q * 4 - 48 : q * 4 - 44, :] = v


def primal_known_kernel(
    sp_ref, sm_ref, prev_ref, next_ref, kern_ref, bias_ref, known_ref, last_ref,
    tt_ref, lt_ref, x_ref,
):
    p = lax.axis_index("plane")
    keeps = (p > 0, None, None, p < 7)
    for plane, src in enumerate((prev_ref, sm_ref, sp_ref, next_ref)):
        for half in range(2):
            v = src[48:64, half * 512 : (half + 1) * 512]
            if keeps[plane] is not None:
                v = jnp.where(keeps[plane], v, 0.0)
            x_ref[plane * 32 + half * 16 : plane * 32 + half * 16 + 16, :] = v
    tt_ref[...] = jnp.zeros((96, 384), F32)
    lt_ref[...] = jnp.zeros((80, 256), F32)
    for dz in range(3):
        for dr in range(3):
            block = jnp.concatenate(
                [
                    jnp.concatenate([kern_ref[c, dz, dr, db : db + 1, :] for db in range(3)], 1)
                    for c in range(5)
                ],
                0,
            )
            for r in range(4):
                i = dz * 32 + (r + dr) * 5
                tt_ref[i : i + 5, r * 96 : (r + 1) * 96] = block
            for db in range(3):
                four = jnp.concatenate([kern_ref[5, dz, dr, db : db + 1, :]] * 4, 1)
                for z in range(2):
                    for r in range(4):
                        i = db * 24 + (z + dz) * 6 + r + dr
                        lane = z * 128 + r * 32
                        lt_ref[i : i + 1, lane : lane + 32] = four[:, r * 32 : (r + 1) * 32]
    last_ref[...] = joined(lt_ref[...].T)
    tt = joined(tt_ref[...].T)
    bias = column(bias_ref, 32)
    for z in range(2):
        h = dot3(tt, x_ref[z * 32 : z * 32 + 96])
        for r in range(4):
            g = shifted_sum([h[r * 96 + i * 32 : r * 96 + (i + 1) * 32] for i in range(3)]) + bias
            i = (z * 4 + r) * 32
            known_ref[i : i + 32, :] = g


def primal_kernel_body(
    back_ref, above_ref, below_ref, known_ref, last_ref, primal_ref,
    mix_ref, slope_ref, shift_ref, new_ref, y_ref,
):
    p = lax.axis_index("plane")
    t = lax.axis_index("tile")
    keeps = (p > 0, None, None, p < 7)
    y_ref[...] = jnp.zeros((80, 512), F32)
    for plane in range(4):
        for row in range(6):
            for col in range(4):
                if row == 0:
                    i = col * 4 + plane
                    v = jnp.where(t > 0, above_ref[i : i + 1, :], 0.0)
                elif row == 5:
                    i = col * 4 + plane
                    v = jnp.where(t < 15, below_ref[i : i + 1, :], 0.0)
                else:
                    i = (row * 4 - 4 + col) * 4 + plane
                    v = back_ref[i : i + 1, :]
                if keeps[plane] is not None:
                    v = jnp.where(keeps[plane], v, 0.0)
                i = 24 + plane * 6 + row
                y_ref[i : i + 1, col * 128 : (col + 1) * 128] = v
    spread_columns(y_ref, 512)
    slope, shift = column(slope_ref, 32), column(shift_ref, 5)
    mix = joined(jnp.concatenate([mix_ref[...], jnp.zeros((3, 32), F32)], 0))
    h = dot3(last_ref[...], y_ref[...]) + known_ref[...]
    for z in range(2):
        for r in range(4):
            i = (z * 4 + r) * 32
            g = h[i : i + 32]
            g = jnp.where(g > 0, g, slope * g)
            out = dot3(mix, g) + shift
            for c in range(5):
                new_ref[c, z, r : r + 1, :] = out[c : c + 1, :] + primal_ref[c, z, r : r + 1, :]


def call(body, outs, in_specs, scratch=(), limit=8 << 20):
    return pl.pallas_call(
        body,
        out_shape=tuple(jax.ShapeDtypeStruct(s[0], s[1]) for s in outs),
        in_specs=in_specs,
        out_specs=tuple(VMEM for _ in outs),
        scratch_shapes=list(scratch),
        compiler_params=pltpu.CompilerParams(vmem_limit_bytes=limit),
    )


def ring(array, axis, step):
    count = lax.axis_size(axis)
    return lax.ppermute(array, axis, [(i, (i + step) % count) for i in range(count)])


def per_device(
    primal, dual, measured, footprint_weights, pixel_index, bin_index, slot_count,
    dual_kernel, dual_bias, dual_slope, dual_mixing, dual_shift,
    primal_kernel, primal_bias, primal_slope, primal_mixing, primal_shift,
):
    pix = jnp.transpose(pixel_index, (2, 0, 1))
    bins = jnp.transpose(bin_index, (2, 0, 1))
    hbm = lambda x: pltpu.with_memory_space_constraint(x, pltpu.HBM)

    own = call(
        pack_kernel, [((32, 1024), F32)], [HBM] * 3,
        [
            pltpu.VMEM((5, 2, 1, 1024), F32),
            pltpu.VMEM((2, 1, 1024), F32),
            pltpu.VMEM((5, 2, 4, 512), F32),
            pltpu.SemaphoreType.DMA((3,)),
        ],
    )(hbm(dual), hbm(measured), hbm(primal))[0]
    left = ring(own, "tile", 1)
    right = ring(own, "tile", -1)

    terms, w_hi, w_lo = pl.pallas_call(
        project_kernel,
        name="project",
        out_shape=(
            jax.ShapeDtypeStruct((16, 3, 16, 128), F32),
            jax.ShapeDtypeStruct((16, 1536, 128), BF16),
            jax.ShapeDtypeStruct((16, 1536, 128), BF16),
        ),
        in_specs=[HBM] * 5 + [VMEM],
        out_specs=(VMEM, VMEM, VMEM),
        scratch_shapes=[pltpu.VMEM((18, 3, 16, 128), F32)]
        + [pltpu.VMEM((16, 16, 128), BF16)] * 3
        + [
            pltpu.SMEM((12, 1, 16), jnp.int32),
            pltpu.SMEM((12, 1, 16), jnp.int32),
            pltpu.SMEM((1, 16), jnp.int32),
            pltpu.VMEM((2, 4, 512), F32),
            pltpu.VMEM((16, 12, 128, 128), F32),
            pltpu.SemaphoreType.DMA((4,)),
            pltpu.SemaphoreType.DMA((8,)),
        ],
        compiler_params=pltpu.CompilerParams(vmem_limit_bytes=18 << 20),
        cost_estimate=pl.CostEstimate(flops=1 << 31, bytes_accessed=25 << 20, transcendentals=0),
    )(hbm(pix), hbm(bins), hbm(slot_count), hbm(primal), hbm(footprint_weights), own)
    sp, sm = call(rims_kernel, [((64, 1024), F32)] * 2, [VMEM] * 4)(own, left, right, primal)
    prev = ring(sp, "plane", 1)
    after = ring(sm, "plane", -1)
    got = lax.all_to_all(terms, "tile", 0, 0, tiled=True)
    total = call(total_kernel, [((48, 128), F32)], [VMEM])(got)[0]
    tprev = ring(total, "plane", 1)
    tnext = ring(total, "plane", -1)

    known, last = call(
        dual_known_kernel, [((128, 1024), F32), ((128, 240), BF16)],
        [VMEM] * 4 + [SMEM],
        [pltpu.VMEM((80, 96), F32), pltpu.VMEM((80, 128), F32)],
    )(sp, prev, after, jnp.transpose(dual_kernel, (2, 3, 4, 1, 0)), dual_bias)

    new_dual, send = call(
        dual_kernel_body, [((5, 2, 1, 1024), F32), ((16, 8, 4, 128), F32)],
        [VMEM] * 9 + [SMEM] * 2, [pltpu.VMEM((80, 1024), F32)],
    )(
        total, tprev, tnext, sp, prev, after, known, last, dual_mixing,
        dual_slope, dual_shift,
    )
    leading = lax.all_to_all(send, "tile", 0, 0, tiled=True)

    back, up, down = pl.pallas_call(
        back_kernel,
        name="back",
        out_shape=(
            jax.ShapeDtypeStruct((64, 128), F32),
            jax.ShapeDtypeStruct((16, 128), F32),
            jax.ShapeDtypeStruct((16, 128), F32),
        ),
        in_specs=[SMEM, SMEM, SMEM, VMEM, VMEM, VMEM],
        out_specs=(VMEM, VMEM, VMEM),
        scratch_shapes=[pltpu.VMEM((16, 8, 8, 128), F32), pltpu.VMEM((17, 8, 128), F32)],
        compiler_params=pltpu.CompilerParams(vmem_limit_bytes=4 << 20),
    )(pix, bins, slot_count, leading, w_hi, w_lo)
    above = ring(down, "tile", 1)
    below = ring(up, "tile", -1)

    known, last = call(
        primal_known_kernel, [((256, 512), F32), ((256, 240), BF16)],
        [VMEM] * 5 + [SMEM],
        [pltpu.VMEM((96, 384), F32), pltpu.VMEM((80, 256), F32), pltpu.VMEM((128, 512), F32)],
    )(sp, sm, prev, after, jnp.transpose(primal_kernel, (1, 2, 3, 4, 0)), primal_bias)

    new_primal = call(
        primal_kernel_body, [((5, 2, 4, 512), F32)], [VMEM] * 7 + [SMEM] * 2,
        [pltpu.VMEM((80, 512), F32)],
    )(
        back, above, below, known, last, primal, primal_mixing, primal_slope, primal_shift,
    )[0]
    return new_primal, new_dual


def solution(mesh):
    grid = P(None, "plane", "tile", None)
    in_specs = (
        grid, grid, P("plane", "tile", None), P("tile", None, None, None, None),
        P("tile", None, None), P(), P("tile", None),
    ) + (P(),) * 10
    return jax.shard_map(
        per_device, mesh=mesh, in_specs=in_specs, out_specs=(grid, grid), check_vma=False
    )
```

```python
import jax
import jax.numpy as jnp
from jax import lax
from jax.experimental import pallas as pl
from jax.experimental.pallas import tpu as pltpu
from jax.sharding import PartitionSpec as P


F32 = jnp.float32
BF16 = jnp.bfloat16
VMEM = pl.BlockSpec(memory_space=pltpu.VMEM)
SMEM = pl.BlockSpec(memory_space=pltpu.SMEM)
HBM = pl.BlockSpec(memory_space=pltpu.HBM)


def split(x):
    hi = x.astype(BF16)
    return hi, (x - hi.astype(F32)).astype(BF16)


def is_even(axis):
    return (lax.axis_index(axis) & 1) == 0


def joined(a):
    hi, lo = split(a)
    return jnp.concatenate([hi, lo, hi], 1)


def dot3(left, b):
    hi, lo = split(b)
    return jnp.dot(left, jnp.concatenate([hi, hi, lo], 0), preferred_element_type=F32)


def column(ref, count):
    rows = -(-count // 8) * 8
    index = lax.broadcasted_iota(jnp.int32, (rows, 128), 0)
    out = jnp.zeros((rows, 128), F32)
    for i in range(count):
        out = jnp.where(index == i, ref[i], out)
    return out[:, 0:1]


def shifted_sum(stack):
    left, mid, right = stack
    width = mid.shape[1]
    lane = lax.broadcasted_iota(jnp.int32, mid.shape, 1)
    left = jnp.where(lane == 0, 0.0, pltpu.roll(left, 1, 1))
    right = jnp.where(lane == width - 1, 0.0, pltpu.roll(right, width - 1, 1))
    return left + mid + right


def pack_kernel(dual_hbm, measured_hbm, primal_hbm, out_ref, dual_ref, measured_ref, primal_ref, sem):
    copies = [
        pltpu.make_async_copy(src, dst, sem.at[i])
        for i, (src, dst) in enumerate(
            ((dual_hbm, dual_ref), (measured_hbm, measured_ref), (primal_hbm, primal_ref))
        )
    ]
    for copy in copies:
        copy.start()
    for copy in copies:
        copy.wait()
    zero = jnp.zeros((1, 1024), F32)
    for z in range(2):
        for c in range(5):
            out_ref[z * 8 + c : z * 8 + c + 1, :] = dual_ref[c, z]
        out_ref[z * 8 + 5 : z * 8 + 6, :] = zero
        out_ref[z * 8 + 6 : z * 8 + 7, :] = measured_ref[z]
        out_ref[z * 8 + 7 : z * 8 + 8, :] = zero
    for k, row in enumerate((0, 3)):
        for c in range(5):
            for z in range(2):
                i = 16 + k * 5 + c
                out_ref[i : i + 1, z * 512 : (z + 1) * 512] = primal_ref[c, z, row : row + 1, :]
    out_ref[26:32, :] = jnp.zeros((6, 1024), F32)


def project_kernel(
    pix_hbm, bin_hbm, cnt_hbm, primal_hbm, w_hbm, after_ref,
    final_ref, wh_ref, wl_ref,
    out_ref, hi_ref, lo_ref, hot_ref, pix_ref, bin_ref, cnt_ref, primal_ref, w_ref, sem, w_sem,
):
    del after_ref
    t = lax.axis_index("tile")
    copies = [
        pltpu.make_async_copy(src, dst, sem.at[i])
        for i, (src, dst) in enumerate(
            (
                (primal_hbm.at[1], primal_ref),
                (pix_hbm, pix_ref),
                (bin_hbm.at[:, pl.ds(t, 1), :], bin_ref),
                (cnt_hbm, cnt_ref),
            )
        )
    ]
    for copy in copies:
        copy.start()

    def fetch(i):
        part = pl.ds(i * 2, 2)
        return pltpu.make_async_copy(w_hbm.at[0, part], w_ref.at[part], w_sem.at[i])

    for i in range(8):
        fetch(i).start()
    row = lax.broadcasted_iota(jnp.int32, (16, 128), 0)
    for b in range(9):
        hot_ref[b] = jnp.where((row & 7) == b, 1.0, 0.0).astype(BF16)
    out_ref[1, 0] = jnp.zeros((16, 128), F32)
    out_ref[16, 2] = jnp.zeros((16, 128), F32)
    for copy in copies:
        copy.wait()
    for q in range(16):
        r, col = q // 4, (q % 4) * 128
        v = jnp.concatenate(
            [
                jnp.broadcast_to(primal_ref[z, r : r + 1, col : col + 128], (8, 128))
                for z in range(2)
            ],
            0,
        )
        hi_ref[q], lo_ref[q] = split(v)

    def angle(a):
        count = cnt_ref[0, a]
        parts = []
        for s in range(12):
            q = pix_ref[s, 0, a]
            b = jnp.where(s < count, bin_ref[s, 0, a], 8)
            hot = hot_ref[b]
            parts.append(jnp.concatenate([hi_ref[q] * hot, lo_ref[q] * hot], 0))
        left = jnp.concatenate(parts, 1)
        w_hi, w_lo = split(w_ref[a].reshape(12 * 128, 128))
        wh_ref[a], wl_ref[a] = w_hi, w_lo
        right = jnp.concatenate([w_hi, w_lo], 1)
        d = jnp.dot(left, right, preferred_element_type=F32)
        res = d[0:16, 0:128] + (d[0:16, 128:256] + d[16:32, 0:128])
        out_ref[a + 1, 1] = res
        out_ref[a, 2] = res
        out_ref[a + 2, 0] = res

    def chunk(i, carry):
        fetch(i).wait()
        angle(i * 2)
        angle(i * 2 + 1)
        return carry

    lax.fori_loop(0, 8, chunk, 0)
    final_ref[...] = out_ref[1:17]


def rims_kernel(own_ref, first_ref, second_ref, primal_ref, sp_ref, sm_ref, a_ref, b_ref):
    t = lax.axis_index("tile")
    even, even_plane = is_even("tile"), is_even("plane")

    def left(rows, lanes):
        return jnp.where(even, second_ref[rows, lanes], first_ref[rows, lanes])

    def right(rows, lanes):
        return jnp.where(even, first_ref[rows, lanes], second_ref[rows, lanes])

    every = slice(None)
    for z in range(2):
        rows = slice(z * 8, z * 8 + 8)
        blocks = (
            jnp.where(t > 0, left(rows, every), 0.0),
            own_ref[rows, :],
            jnp.where(t < 15, right(rows, every), 0.0),
        )
        for k, block in enumerate(blocks):
            base = z * 24 + k * 8
            for out in (sp_ref, sm_ref, a_ref, b_ref):
                out[base : base + 8, :] = block
    for z, out in ((0, sm_ref), (1, sp_ref)):
        half = slice(z * 512, (z + 1) * 512)
        for row in range(6):
            for c in range(5):
                if row == 0:
                    v = jnp.where(t > 0, left(slice(21 + c, 22 + c), half), 0.0)
                elif row == 5:
                    v = jnp.where(t < 15, right(slice(16 + c, 17 + c), half), 0.0)
                else:
                    v = primal_ref[c, z, row - 1 : row, :]
                i = row * 5 + c
                lane = (i // 16) * 512
                out[48 + i % 16 : 49 + i % 16, lane : lane + 512] = v
        out[62:64, 512:1024] = jnp.zeros((2, 512), F32)
    up, down = sp_ref[48:64, :], sm_ref[48:64, :]
    a_ref[48:64, :] = jnp.where(even_plane, up, down)
    b_ref[48:64, :] = jnp.where(even_plane, down, up)


def total_kernel(got_ref, out_ref):
    t = lax.axis_index("tile")
    for k, ok in enumerate((t > 0, None, t < 15)):
        total = got_ref[0, k]
        for i in range(1, 16):
            total = total + got_ref[i, k]
        if ok is not None:
            total = jnp.where(ok, total, 0.0)
        out_ref[k * 16 : k * 16 + 16, :] = total


def plane_sides(first_ref, second_ref, rows):
    p = lax.axis_index("plane")
    even = is_even("plane")
    first, second = first_ref[rows, :], second_ref[rows, :]
    before = jnp.where(p > 0, jnp.where(even, second, first), 0.0)
    return before, jnp.where(p < 7, jnp.where(even, first, second), 0.0)


def dual_inputs(own_ref, first_ref, second_ref):
    before, after = plane_sides(first_ref, second_ref, slice(0, 48))
    return jnp.concatenate(
        [
            before,
            own_ref[0:48, :],
            after,
            jnp.zeros((8, 1024), F32),
        ],
        0,
    )


def dual_known_kernel(
    own_ref, first_ref, second_ref, kern_ref, bias_ref, known_ref, last_ref, tt_ref, lt_ref
):
    tt_ref[...] = jnp.zeros((80, 96), F32)
    lt_ref[...] = jnp.zeros((80, 128), F32)
    for dz in range(3):
        for da in range(3):
            tiles = [kern_ref[dz, da, db] for db in range(3)]
            base = dz * 24 + da * 8
            tt_ref[base : base + 7, :] = jnp.concatenate(tiles, 1)
            for db in range(3):
                four = jnp.concatenate([tiles[db][5:6]] * 4, 1)
                for z in range(4):
                    i = db * 24 + (z + dz) * 3 + da
                    lt_ref[i : i + 1, z * 32 : (z + 1) * 32] = four[:, z * 32 : (z + 1) * 32]
    last_ref[...] = joined(lt_ref[...].T)
    x = dual_inputs(own_ref, first_ref, second_ref)
    tt = joined(tt_ref[...].T)
    bias = column(bias_ref, 32)
    for z in range(4):
        h = dot3(tt, x[z * 24 : z * 24 + 80])
        h = shifted_sum([h[i * 32 : (i + 1) * 32] for i in range(3)]) + bias
        known_ref[z * 32 : (z + 1) * 32, :] = h


def spread_columns(y_ref, width):
    mid = y_ref[24:48, :]
    lane = lax.broadcasted_iota(jnp.int32, mid.shape, 1)
    y_ref[0:24, :] = jnp.where(lane == 0, 0.0, pltpu.roll(mid, 1, 1))
    y_ref[48:72, :] = jnp.where(lane == width - 1, 0.0, pltpu.roll(mid, width - 1, 1))


def dual_kernel_body(
    total_ref, ta_ref, tb_ref, own_ref, first_ref, second_ref, known_ref, last_ref,
    mix_ref, slope_ref, shift_ref, new_ref, send_ref, y_ref,
):
    y_ref[...] = jnp.zeros((80, 1024), F32)
    before, after = plane_sides(ta_ref, tb_ref, slice(0, 48))
    for start, v in ((0, before), (2, total_ref[...]), (4, after)):
        for k in range(3):
            for z in range(2):
                row = 24 + (start + z) * 3 + k
                for b in range(8):
                    i = k * 16 + z * 8 + b
                    y_ref[row : row + 1, b * 128 : (b + 1) * 128] = v[i : i + 1]
    spread_columns(y_ref, 1024)
    slope, shift = column(slope_ref, 32), column(shift_ref, 5)
    mix = joined(jnp.concatenate([mix_ref[...], jnp.zeros((3, 32), F32)], 0))
    h = dot3(last_ref[...], y_ref[...]) + known_ref[...]
    dual_rows = (
        plane_sides(first_ref, second_ref, slice(32, 40))[0],
        own_ref[8:16, :],
        own_ref[32:40, :],
        plane_sides(first_ref, second_ref, slice(8, 16))[1],
    )
    for z in range(4):
        g = h[z * 32 : (z + 1) * 32]
        g = jnp.where(g > 0, g, slope * g)
        out = dot3(mix, g) + shift + dual_rows[z]
        if z in (1, 2):
            for c in range(5):
                new_ref[c, z - 1] = out[c : c + 1, :]
        for b in range(8):
            piece = jnp.broadcast_to(out[0:1, b * 128 : (b + 1) * 128], (16, 128))
            send_ref[:, b, z, :] = piece


def back_kernel(
    pix_ref, bin_ref, cnt_ref, nd_ref, wh_ref, wl_ref, new_ref,
    out_ref, first_ref, second_ref, new_hbm, tab_ref, acc_ref, sem,
):
    t = lax.axis_index("tile")
    even = is_even("tile")
    copy = pltpu.make_async_copy(new_ref, new_hbm, sem)
    copy.start()
    for a in range(16):
        for b in range(8):
            v = nd_ref[a, b]
            hi = v.astype(BF16).astype(F32)
            tab_ref[a, b, 0:4] = hi
            tab_ref[a, b, 4:8] = v - hi
    acc_ref[...] = jnp.zeros_like(acc_ref)
    zero = jnp.zeros((8, 128), F32)

    def angle(a):
        count = cnt_ref[0, a]
        for s in range(0, 12, 2):
            one, two = (tab_ref[a, bin_ref[s + i, t, a]] for i in range(2))
            left = jnp.concatenate(
                [jnp.concatenate([one, zero], 1), jnp.concatenate([zero, two], 1)], 0
            ).astype(BF16)
            right = jnp.concatenate(
                [
                    jnp.concatenate(
                        [w[a, (s + i) * 128 : (s + i + 1) * 128, :] for i in range(2)], 1
                    )
                    for w in (wh_ref, wl_ref)
                ],
                0,
            )
            d = lax.dot_general(
                left, right, (((1,), (1,)), ((), ())), preferred_element_type=F32
            )
            d = d[:, 0:128] + d[:, 128:256]
            for i in range(2):
                q = jnp.where(s + i < count, pix_ref[s + i, 0, a], 16)
                acc_ref[q] += d[i * 8 : i * 8 + 8]

    def chunk(i, carry):
        for k in range(4):
            angle(i * 4 + k)
        return carry

    lax.fori_loop(0, 4, chunk, 0)
    for q in range(16):
        v = acc_ref[q, 0:4] + acc_ref[q, 4:8]
        out_ref[q * 4 : q * 4 + 4, :] = v
    up, down = out_ref[0:16, :], out_ref[48:64, :]
    first_ref[...] = jnp.where(even, down, up)
    second_ref[...] = jnp.where(even, up, down)
    copy.wait()


def primal_known_kernel(
    sp_ref, sm_ref, first_ref, second_ref, kern_ref, bias_ref, known_ref, last_ref,
    tt_ref, lt_ref, x_ref,
):
    before, after = plane_sides(first_ref, second_ref, slice(48, 64))
    for plane, v in enumerate((before, sm_ref[48:64, :], sp_ref[48:64, :], after)):
        for half in range(2):
            i = plane * 32 + half * 16
            x_ref[i : i + 16, :] = v[:, half * 512 : (half + 1) * 512]
    tt_ref[...] = jnp.zeros((96, 384), F32)
    lt_ref[...] = jnp.zeros((80, 256), F32)
    for dz in range(3):
        for dr in range(3):
            block = jnp.concatenate(
                [
                    jnp.concatenate([kern_ref[c, dz, dr, db : db + 1, :] for db in range(3)], 1)
                    for c in range(5)
                ],
                0,
            )
            for r in range(4):
                i = dz * 32 + (r + dr) * 5
                tt_ref[i : i + 5, r * 96 : (r + 1) * 96] = block
            for db in range(3):
                four = jnp.concatenate([kern_ref[5, dz, dr, db : db + 1, :]] * 4, 1)
                for z in range(2):
                    for r in range(4):
                        i = db * 24 + (z + dz) * 6 + r + dr
                        lane = z * 128 + r * 32
                        lt_ref[i : i + 1, lane : lane + 32] = four[:, r * 32 : (r + 1) * 32]
    last_ref[...] = joined(lt_ref[...].T)
    tt = joined(tt_ref[...].T)
    bias = column(bias_ref, 32)
    for z in range(2):
        h = dot3(tt, x_ref[z * 32 : z * 32 + 96])
        for r in range(4):
            g = shifted_sum([h[r * 96 + i * 32 : r * 96 + (i + 1) * 32] for i in range(3)]) + bias
            i = (z * 4 + r) * 32
            known_ref[i : i + 32, :] = g


def primal_kernel_body(
    back_ref, first_ref, second_ref, known_ref, last_ref, primal_ref,
    mix_ref, slope_ref, shift_ref, new_ref, y_ref,
):
    p = lax.axis_index("plane")
    t = lax.axis_index("tile")
    keeps = (p > 0, None, None, p < 7)
    even = is_even("tile")
    first, second = first_ref[...], second_ref[...]
    above = jnp.where(t > 0, jnp.where(even, second, first), 0.0)
    below = jnp.where(t < 15, jnp.where(even, first, second), 0.0)
    y_ref[...] = jnp.zeros((80, 512), F32)
    for plane in range(4):
        for row in range(6):
            for col in range(4):
                if row == 0:
                    i = col * 4 + plane
                    v = above[i : i + 1]
                elif row == 5:
                    i = col * 4 + plane
                    v = below[i : i + 1]
                else:
                    i = (row * 4 - 4 + col) * 4 + plane
                    v = back_ref[i : i + 1, :]
                if keeps[plane] is not None:
                    v = jnp.where(keeps[plane], v, 0.0)
                i = 24 + plane * 6 + row
                y_ref[i : i + 1, col * 128 : (col + 1) * 128] = v
    spread_columns(y_ref, 512)
    slope, shift = column(slope_ref, 32), column(shift_ref, 5)
    mix = joined(jnp.concatenate([mix_ref[...], jnp.zeros((3, 32), F32)], 0))
    h = dot3(last_ref[...], y_ref[...]) + known_ref[...]
    for z in range(2):
        for r in range(4):
            i = (z * 4 + r) * 32
            g = h[i : i + 32]
            g = jnp.where(g > 0, g, slope * g)
            out = dot3(mix, g) + shift
            for c in range(5):
                new_ref[c, z, r : r + 1, :] = out[c : c + 1, :] + primal_ref[c, z, r : r + 1, :]


def call(body, outs, in_specs, scratch=(), limit=8 << 20):
    return pl.pallas_call(
        body,
        out_shape=tuple(jax.ShapeDtypeStruct(s[0], s[1]) for s in outs),
        in_specs=in_specs,
        out_specs=tuple(VMEM for _ in outs),
        scratch_shapes=list(scratch),
        compiler_params=pltpu.CompilerParams(vmem_limit_bytes=limit),
    )


def swaps(first, second, axis):
    count = lax.axis_size(axis)
    a = lax.ppermute(first, axis, [(i, i ^ 1) for i in range(count)])
    pairs = [(i, (i - 1 if i % 2 == 0 else i + 1) % count) for i in range(count)]
    b = lax.ppermute(second, axis, pairs)
    return a, b


def per_device(
    primal, dual, measured, footprint_weights, pixel_index, bin_index, slot_count,
    dual_kernel, dual_bias, dual_slope, dual_mixing, dual_shift,
    primal_kernel, primal_bias, primal_slope, primal_mixing, primal_shift,
):
    pix = jnp.transpose(pixel_index, (2, 0, 1))
    bins = jnp.transpose(bin_index, (2, 0, 1))
    hbm = lambda x: pltpu.with_memory_space_constraint(x, pltpu.HBM)

    own = call(
        pack_kernel, [((32, 1024), F32)], [HBM] * 3,
        [
            pltpu.VMEM((5, 2, 1, 1024), F32),
            pltpu.VMEM((2, 1, 1024), F32),
            pltpu.VMEM((5, 2, 4, 512), F32),
            pltpu.SemaphoreType.DMA((3,)),
        ],
    )(hbm(dual), hbm(measured), hbm(primal))[0]
    near = swaps(own, own, "tile")

    terms, w_hi, w_lo = pl.pallas_call(
        project_kernel,
        name="project",
        out_shape=(
            jax.ShapeDtypeStruct((16, 3, 16, 128), F32),
            jax.ShapeDtypeStruct((16, 1536, 128), BF16),
            jax.ShapeDtypeStruct((16, 1536, 128), BF16),
        ),
        in_specs=[HBM] * 5 + [VMEM],
        out_specs=(VMEM, VMEM, VMEM),
        scratch_shapes=[pltpu.VMEM((18, 3, 16, 128), F32)]
        + [pltpu.VMEM((16, 16, 128), BF16)] * 3
        + [
            pltpu.SMEM((12, 1, 16), jnp.int32),
            pltpu.SMEM((12, 1, 16), jnp.int32),
            pltpu.SMEM((1, 16), jnp.int32),
            pltpu.VMEM((2, 4, 512), F32),
            pltpu.VMEM((16, 12, 128, 128), F32),
            pltpu.SemaphoreType.DMA((4,)),
            pltpu.SemaphoreType.DMA((8,)),
        ],
        compiler_params=pltpu.CompilerParams(vmem_limit_bytes=18 << 20),
        cost_estimate=pl.CostEstimate(flops=1 << 31, bytes_accessed=25 << 20, transcendentals=0),
    )(hbm(pix), hbm(bins), hbm(slot_count), hbm(primal), hbm(footprint_weights), own)
    terms, near = lax.optimization_barrier((terms, near))
    sp, sm, side_a, side_b = call(
        rims_kernel, [((64, 1024), F32)] * 4, [VMEM] * 4
    )(own, *near, primal)
    sides = swaps(side_a, side_b, "plane")
    got = lax.all_to_all(terms, "tile", 0, 0, tiled=True)
    total = call(total_kernel, [((48, 128), F32)], [VMEM])(got)[0]
    rows = swaps(total, total, "plane")

    known, last = call(
        dual_known_kernel, [((128, 1024), F32), ((128, 240), BF16)],
        [VMEM] * 4 + [SMEM],
        [pltpu.VMEM((80, 96), F32), pltpu.VMEM((80, 128), F32)],
    )(sp, *sides, jnp.transpose(dual_kernel, (2, 3, 4, 1, 0)), dual_bias)

    new_rows, send = call(
        dual_kernel_body, [((5, 2, 1, 1024), F32), ((16, 8, 4, 128), F32)],
        [VMEM] * 9 + [SMEM] * 2, [pltpu.VMEM((80, 1024), F32)],
    )(
        total, *rows, sp, *sides, known, last, dual_mixing,
        dual_slope, dual_shift,
    )
    leading = lax.all_to_all(send, "tile", 0, 0, tiled=True)

    back, edge_a, edge_b, new_dual = pl.pallas_call(
        back_kernel,
        name="back",
        out_shape=(
            jax.ShapeDtypeStruct((64, 128), F32),
            jax.ShapeDtypeStruct((16, 128), F32),
            jax.ShapeDtypeStruct((16, 128), F32),
            jax.ShapeDtypeStruct((5, 2, 1, 1024), F32),
        ),
        in_specs=[SMEM, SMEM, SMEM, VMEM, VMEM, VMEM, VMEM],
        out_specs=(VMEM, VMEM, VMEM, HBM),
        scratch_shapes=[
            pltpu.VMEM((16, 8, 8, 128), F32),
            pltpu.VMEM((17, 8, 128), F32),
            pltpu.SemaphoreType.DMA,
        ],
        compiler_params=pltpu.CompilerParams(vmem_limit_bytes=4 << 20),
    )(pix, bins, slot_count, leading, w_hi, w_lo, new_rows)
    edges = swaps(edge_a, edge_b, "tile")

    known, last = call(
        primal_known_kernel, [((256, 512), F32), ((256, 240), BF16)],
        [VMEM] * 5 + [SMEM],
        [pltpu.VMEM((96, 384), F32), pltpu.VMEM((80, 256), F32), pltpu.VMEM((128, 512), F32)],
    )(sp, sm, *sides, jnp.transpose(primal_kernel, (1, 2, 3, 4, 0)), primal_bias)

    new_primal = call(
        primal_kernel_body, [((5, 2, 4, 512), F32)], [VMEM] * 7 + [SMEM] * 2,
        [pltpu.VMEM((80, 512), F32)],
    )(
        back, *edges, known, last, primal, primal_mixing, primal_slope, primal_shift,
    )[0]
    return new_primal, new_dual


def solution(mesh):
    grid = P(None, "plane", "tile", None)
    in_specs = (
        grid, grid, P("plane", "tile", None), P("tile", None, None, None, None),
        P("tile", None, None), P(), P("tile", None),
    ) + (P(),) * 10
    return jax.shard_map(
        per_device, mesh=mesh, in_specs=in_specs, out_specs=(grid, grid), check_vma=False
    )
```

```python
import jax
import jax.numpy as jnp
from jax import lax
from jax.experimental import pallas as pl
from jax.experimental.pallas import tpu as pltpu
from jax.sharding import PartitionSpec as P


F32 = jnp.float32
BF16 = jnp.bfloat16
VMEM = pl.BlockSpec(memory_space=pltpu.VMEM)
SMEM = pl.BlockSpec(memory_space=pltpu.SMEM)
HBM = pl.BlockSpec(memory_space=pltpu.HBM)


def split(x):
    hi = x.astype(BF16)
    return hi, (x - hi.astype(F32)).astype(BF16)


def is_even(axis):
    return (lax.axis_index(axis) & 1) == 0


def joined(a):
    hi, lo = split(a)
    return jnp.concatenate([hi, lo, hi], 1)


def dot3(left, b):
    hi, lo = split(b)
    return jnp.dot(left, jnp.concatenate([hi, hi, lo], 0), preferred_element_type=F32)


def column(ref, count):
    rows = -(-count // 8) * 8
    index = lax.broadcasted_iota(jnp.int32, (rows, 128), 0)
    out = jnp.zeros((rows, 128), F32)
    for i in range(count):
        out = jnp.where(index == i, ref[i], out)
    return out[:, 0:1]


def shifted_sum(stack):
    left, mid, right = stack
    width = mid.shape[1]
    lane = lax.broadcasted_iota(jnp.int32, mid.shape, 1)
    left = jnp.where(lane == 0, 0.0, pltpu.roll(left, 1, 1))
    right = jnp.where(lane == width - 1, 0.0, pltpu.roll(right, width - 1, 1))
    return left + mid + right


HEAD = 4


def pack_kernel(
    dual_hbm, measured_hbm, primal_hbm, w_hbm,
    out_ref, head_ref, dual_ref, measured_ref, primal_ref, sem,
):
    head = pltpu.make_async_copy(w_hbm.at[0, pl.ds(0, HEAD)], head_ref, sem.at[3])
    copies = [
        pltpu.make_async_copy(src, dst, sem.at[i])
        for i, (src, dst) in enumerate(
            ((dual_hbm, dual_ref), (measured_hbm, measured_ref), (primal_hbm, primal_ref))
        )
    ]
    for copy in copies:
        copy.start()
    head.start()
    for copy in copies:
        copy.wait()
    zero = jnp.zeros((1, 1024), F32)
    for z in range(2):
        for c in range(5):
            out_ref[z * 8 + c : z * 8 + c + 1, :] = dual_ref[c, z]
        out_ref[z * 8 + 5 : z * 8 + 6, :] = zero
        out_ref[z * 8 + 6 : z * 8 + 7, :] = measured_ref[z]
        out_ref[z * 8 + 7 : z * 8 + 8, :] = zero
    for k, row in enumerate((0, 3)):
        for c in range(5):
            for z in range(2):
                i = 16 + k * 5 + c
                out_ref[i : i + 1, z * 512 : (z + 1) * 512] = primal_ref[c, z, row : row + 1, :]
    out_ref[26:32, :] = jnp.zeros((6, 1024), F32)
    head.wait()


def index_copies(pix_hbm, bin_hbm, cnt_hbm, pix_ref, bin_ref, cnt_ref, sem):
    t = lax.axis_index("tile")
    return [
        pltpu.make_async_copy(pix_hbm, pix_ref, sem.at[0]),
        pltpu.make_async_copy(bin_hbm.at[:, pl.ds(t, 1), :], bin_ref, sem.at[1]),
        pltpu.make_async_copy(cnt_hbm, cnt_ref, sem.at[2]),
    ]


def project_kernel(
    pix_hbm, bin_hbm, cnt_hbm, primal_hbm, w_hbm, head_ref,
    final_ref, wh_ref, wl_ref,
    out_ref, hi_ref, lo_ref, hot_ref, pix_ref, bin_ref, cnt_ref, primal_ref, w_ref, sem, w_sem,
):
    copies = index_copies(pix_hbm, bin_hbm, cnt_hbm, pix_ref, bin_ref, cnt_ref, sem)
    copies.append(pltpu.make_async_copy(primal_hbm.at[1], primal_ref, sem.at[3]))
    for copy in copies:
        copy.start()

    def fetch(i):
        return pltpu.make_async_copy(
            w_hbm.at[0, pl.ds(HEAD + i * 2, 2)], w_ref.at[pl.ds(i * 2, 2)], w_sem.at[i]
        )

    rest = (16 - HEAD) // 2
    for i in range(rest):
        fetch(i).start()
    row = lax.broadcasted_iota(jnp.int32, (16, 128), 0)
    for b in range(9):
        hot_ref[b] = jnp.where((row & 7) == b, 1.0, 0.0).astype(BF16)
    out_ref[1, 0] = jnp.zeros((16, 128), F32)
    out_ref[16, 2] = jnp.zeros((16, 128), F32)
    for copy in copies:
        copy.wait()
    for q in range(16):
        r, col = q // 4, (q % 4) * 128
        v = jnp.concatenate(
            [
                jnp.broadcast_to(primal_ref[z, r : r + 1, col : col + 128], (8, 128))
                for z in range(2)
            ],
            0,
        )
        hi_ref[q], lo_ref[q] = split(v)

    def angle(a, source, at):
        count = cnt_ref[0, a]
        parts = []
        for s in range(12):
            q = pix_ref[s, 0, a]
            b = jnp.where(s < count, bin_ref[s, 0, a], 8)
            hot = hot_ref[b]
            parts.append(jnp.concatenate([hi_ref[q] * hot, lo_ref[q] * hot], 0))
        left = jnp.concatenate(parts, 1)
        w_hi, w_lo = split(source[at].reshape(12 * 128, 128))
        wh_ref[a], wl_ref[a] = w_hi, w_lo
        right = jnp.concatenate([w_hi, w_lo], 1)
        d = jnp.dot(left, right, preferred_element_type=F32)
        res = d[0:16, 0:128] + (d[0:16, 128:256] + d[16:32, 0:128])
        out_ref[a + 1, 1] = res
        out_ref[a, 2] = res
        out_ref[a + 2, 0] = res

    def first(i, carry):
        for k in (i * 2, i * 2 + 1):
            angle(k, head_ref, k)
        return carry

    def chunk(i, carry):
        fetch(i).wait()
        for k in (i * 2, i * 2 + 1):
            angle(HEAD + k, w_ref, k)
        return carry

    lax.fori_loop(0, HEAD // 2, first, 0)
    lax.fori_loop(0, rest, chunk, 0)
    final_ref[...] = out_ref[1:17]


def rims_kernel(own_ref, first_ref, second_ref, primal_ref, sp_ref, sm_ref, a_ref, b_ref):
    t = lax.axis_index("tile")
    even, even_plane = is_even("tile"), is_even("plane")

    def left(rows, lanes):
        return jnp.where(even, second_ref[rows, lanes], first_ref[rows, lanes])

    def right(rows, lanes):
        return jnp.where(even, first_ref[rows, lanes], second_ref[rows, lanes])

    every = slice(None)
    for z in range(2):
        rows = slice(z * 8, z * 8 + 8)
        blocks = (
            jnp.where(t > 0, left(rows, every), 0.0),
            own_ref[rows, :],
            jnp.where(t < 15, right(rows, every), 0.0),
        )
        for k, block in enumerate(blocks):
            base = z * 24 + k * 8
            for out in (sp_ref, sm_ref, a_ref, b_ref):
                out[base : base + 8, :] = block
    for z, out in ((0, sm_ref), (1, sp_ref)):
        half = slice(z * 512, (z + 1) * 512)
        for row in range(6):
            for c in range(5):
                if row == 0:
                    v = jnp.where(t > 0, left(slice(21 + c, 22 + c), half), 0.0)
                elif row == 5:
                    v = jnp.where(t < 15, right(slice(16 + c, 17 + c), half), 0.0)
                else:
                    v = primal_ref[c, z, row - 1 : row, :]
                i = row * 5 + c
                lane = (i // 16) * 512
                out[48 + i % 16 : 49 + i % 16, lane : lane + 512] = v
        out[62:64, 512:1024] = jnp.zeros((2, 512), F32)
    up, down = sp_ref[48:64, :], sm_ref[48:64, :]
    a_ref[48:64, :] = jnp.where(even_plane, up, down)
    b_ref[48:64, :] = jnp.where(even_plane, down, up)


def total_kernel(got_ref, out_ref):
    t = lax.axis_index("tile")
    for k, ok in enumerate((t > 0, None, t < 15)):
        total = got_ref[0, k]
        for i in range(1, 16):
            total = total + got_ref[i, k]
        if ok is not None:
            total = jnp.where(ok, total, 0.0)
        out_ref[k * 16 : k * 16 + 16, :] = total


def plane_sides(first_ref, second_ref, rows):
    p = lax.axis_index("plane")
    even = is_even("plane")
    first, second = first_ref[rows, :], second_ref[rows, :]
    before = jnp.where(p > 0, jnp.where(even, second, first), 0.0)
    return before, jnp.where(p < 7, jnp.where(even, first, second), 0.0)


def dual_inputs(own_ref, first_ref, second_ref):
    before, after = plane_sides(first_ref, second_ref, slice(0, 48))
    return jnp.concatenate(
        [
            before,
            own_ref[0:48, :],
            after,
            jnp.zeros((8, 1024), F32),
        ],
        0,
    )


def dual_known_kernel(
    own_ref, first_ref, second_ref, kern_ref, bias_ref, known_ref, last_ref, tt_ref, lt_ref
):
    tt_ref[...] = jnp.zeros((80, 96), F32)
    lt_ref[...] = jnp.zeros((80, 128), F32)
    for dz in range(3):
        for da in range(3):
            tiles = [kern_ref[dz, da, db] for db in range(3)]
            base = dz * 24 + da * 8
            tt_ref[base : base + 7, :] = jnp.concatenate(tiles, 1)
            for db in range(3):
                four = jnp.concatenate([tiles[db][5:6]] * 4, 1)
                for z in range(4):
                    i = db * 24 + (z + dz) * 3 + da
                    lt_ref[i : i + 1, z * 32 : (z + 1) * 32] = four[:, z * 32 : (z + 1) * 32]
    last_ref[...] = joined(lt_ref[...].T)
    x = dual_inputs(own_ref, first_ref, second_ref)
    tt = joined(tt_ref[...].T)
    bias = column(bias_ref, 32)
    for z in range(4):
        h = dot3(tt, x[z * 24 : z * 24 + 80])
        h = shifted_sum([h[i * 32 : (i + 1) * 32] for i in range(3)]) + bias
        known_ref[z * 32 : (z + 1) * 32, :] = h


def spread_columns(y_ref, width):
    mid = y_ref[24:48, :]
    lane = lax.broadcasted_iota(jnp.int32, mid.shape, 1)
    y_ref[0:24, :] = jnp.where(lane == 0, 0.0, pltpu.roll(mid, 1, 1))
    y_ref[48:72, :] = jnp.where(lane == width - 1, 0.0, pltpu.roll(mid, width - 1, 1))


def dual_kernel_body(
    total_ref, ta_ref, tb_ref, own_ref, first_ref, second_ref, known_ref, last_ref,
    mix_ref, slope_ref, shift_ref, new_ref, send_ref, y_ref,
):
    y_ref[...] = jnp.zeros((80, 1024), F32)
    before, after = plane_sides(ta_ref, tb_ref, slice(0, 48))
    for start, v in ((0, before), (2, total_ref[...]), (4, after)):
        for k in range(3):
            for z in range(2):
                row = 24 + (start + z) * 3 + k
                for b in range(8):
                    i = k * 16 + z * 8 + b
                    y_ref[row : row + 1, b * 128 : (b + 1) * 128] = v[i : i + 1]
    spread_columns(y_ref, 1024)
    slope, shift = column(slope_ref, 32), column(shift_ref, 5)
    mix = joined(jnp.concatenate([mix_ref[...], jnp.zeros((3, 32), F32)], 0))
    h = dot3(last_ref[...], y_ref[...]) + known_ref[...]
    dual_rows = (
        plane_sides(first_ref, second_ref, slice(32, 40))[0],
        own_ref[8:16, :],
        own_ref[32:40, :],
        plane_sides(first_ref, second_ref, slice(8, 16))[1],
    )
    for z in range(4):
        g = h[z * 32 : (z + 1) * 32]
        g = jnp.where(g > 0, g, slope * g)
        out = dot3(mix, g) + shift + dual_rows[z]
        if z in (1, 2):
            for c in range(5):
                new_ref[c, z - 1] = out[c : c + 1, :]
        for b in range(8):
            piece = jnp.broadcast_to(out[0:1, b * 128 : (b + 1) * 128], (16, 128))
            send_ref[:, b, z, :] = piece


def back_kernel(
    pix_hbm, bin_hbm, cnt_hbm, nd_ref, wh_ref, wl_ref, new_ref,
    out_ref, first_ref, second_ref, new_hbm, tab_ref, acc_ref, pix_ref, bin_ref, cnt_ref, sem,
):
    even = is_even("tile")
    copies = index_copies(pix_hbm, bin_hbm, cnt_hbm, pix_ref, bin_ref, cnt_ref, sem)
    for copy in copies:
        copy.start()
    out_copy = pltpu.make_async_copy(new_ref, new_hbm, sem.at[3])
    out_copy.start()
    for a in range(16):
        for b in range(8):
            v = nd_ref[a, b]
            hi = v.astype(BF16).astype(F32)
            tab_ref[a, b, 0:4] = hi
            tab_ref[a, b, 4:8] = v - hi
    acc_ref[...] = jnp.zeros_like(acc_ref)
    zero = jnp.zeros((8, 128), F32)
    for copy in copies:
        copy.wait()

    def angle(a):
        count = cnt_ref[0, a]
        for s in range(0, 12, 2):
            one, two = (tab_ref[a, bin_ref[s + i, 0, a]] for i in range(2))
            left = jnp.concatenate(
                [jnp.concatenate([one, zero], 1), jnp.concatenate([zero, two], 1)], 0
            ).astype(BF16)
            right = jnp.concatenate(
                [
                    jnp.concatenate(
                        [w[a, (s + i) * 128 : (s + i + 1) * 128, :] for i in range(2)], 1
                    )
                    for w in (wh_ref, wl_ref)
                ],
                0,
            )
            d = lax.dot_general(
                left, right, (((1,), (1,)), ((), ())), preferred_element_type=F32
            )
            d = d[:, 0:128] + d[:, 128:256]
            for i in range(2):
                q = jnp.where(s + i < count, pix_ref[s + i, 0, a], 16)
                acc_ref[q] += d[i * 8 : i * 8 + 8]

    def chunk(i, carry):
        for k in range(4):
            angle(i * 4 + k)
        return carry

    lax.fori_loop(0, 4, chunk, 0)
    for q in range(16):
        v = acc_ref[q, 0:4] + acc_ref[q, 4:8]
        out_ref[q * 4 : q * 4 + 4, :] = v
    up, down = out_ref[0:16, :], out_ref[48:64, :]
    first_ref[...] = jnp.where(even, down, up)
    second_ref[...] = jnp.where(even, up, down)
    out_copy.wait()


def primal_known_kernel(
    sp_ref, sm_ref, first_ref, second_ref, kern_ref, bias_ref, known_ref, last_ref,
    tt_ref, lt_ref, x_ref,
):
    before, after = plane_sides(first_ref, second_ref, slice(48, 64))
    for plane, v in enumerate((before, sm_ref[48:64, :], sp_ref[48:64, :], after)):
        for half in range(2):
            i = plane * 32 + half * 16
            x_ref[i : i + 16, :] = v[:, half * 512 : (half + 1) * 512]
    tt_ref[...] = jnp.zeros((96, 384), F32)
    lt_ref[...] = jnp.zeros((80, 256), F32)
    for dz in range(3):
        for dr in range(3):
            block = jnp.concatenate(
                [
                    jnp.concatenate([kern_ref[c, dz, dr, db : db + 1, :] for db in range(3)], 1)
                    for c in range(5)
                ],
                0,
            )
            for r in range(4):
                i = dz * 32 + (r + dr) * 5
                tt_ref[i : i + 5, r * 96 : (r + 1) * 96] = block
            for db in range(3):
                four = jnp.concatenate([kern_ref[5, dz, dr, db : db + 1, :]] * 4, 1)
                for z in range(2):
                    for r in range(4):
                        i = db * 24 + (z + dz) * 6 + r + dr
                        lane = z * 128 + r * 32
                        lt_ref[i : i + 1, lane : lane + 32] = four[:, r * 32 : (r + 1) * 32]
    last_ref[...] = joined(lt_ref[...].T)
    tt = joined(tt_ref[...].T)
    bias = column(bias_ref, 32)
    for z in range(2):
        h = dot3(tt, x_ref[z * 32 : z * 32 + 96])
        for r in range(4):
            g = shifted_sum([h[r * 96 + i * 32 : r * 96 + (i + 1) * 32] for i in range(3)]) + bias
            i = (z * 4 + r) * 32
            known_ref[i : i + 32, :] = g


def primal_kernel_body(
    back_ref, first_ref, second_ref, known_ref, last_ref, primal_ref,
    mix_ref, slope_ref, shift_ref, new_ref, y_ref,
):
    p = lax.axis_index("plane")
    t = lax.axis_index("tile")
    keeps = (p > 0, None, None, p < 7)
    even = is_even("tile")
    first, second = first_ref[...], second_ref[...]
    above = jnp.where(t > 0, jnp.where(even, second, first), 0.0)
    below = jnp.where(t < 15, jnp.where(even, first, second), 0.0)
    y_ref[...] = jnp.zeros((80, 512), F32)
    for plane in range(4):
        for row in range(6):
            for col in range(4):
                if row == 0:
                    i = col * 4 + plane
                    v = above[i : i + 1]
                elif row == 5:
                    i = col * 4 + plane
                    v = below[i : i + 1]
                else:
                    i = (row * 4 - 4 + col) * 4 + plane
                    v = back_ref[i : i + 1, :]
                if keeps[plane] is not None:
                    v = jnp.where(keeps[plane], v, 0.0)
                i = 24 + plane * 6 + row
                y_ref[i : i + 1, col * 128 : (col + 1) * 128] = v
    spread_columns(y_ref, 512)
    slope, shift = column(slope_ref, 32), column(shift_ref, 5)
    mix = joined(jnp.concatenate([mix_ref[...], jnp.zeros((3, 32), F32)], 0))
    h = dot3(last_ref[...], y_ref[...]) + known_ref[...]
    for z in range(2):
        for r in range(4):
            i = (z * 4 + r) * 32
            g = h[i : i + 32]
            g = jnp.where(g > 0, g, slope * g)
            out = dot3(mix, g) + shift
            for c in range(5):
                new_ref[c, z, r : r + 1, :] = out[c : c + 1, :] + primal_ref[c, z, r : r + 1, :]


def call(body, outs, in_specs, scratch=(), limit=8 << 20):
    return pl.pallas_call(
        body,
        out_shape=tuple(jax.ShapeDtypeStruct(s[0], s[1]) for s in outs),
        in_specs=in_specs,
        out_specs=tuple(VMEM for _ in outs),
        scratch_shapes=list(scratch),
        compiler_params=pltpu.CompilerParams(vmem_limit_bytes=limit),
    )


def swaps(first, second, axis):
    count = lax.axis_size(axis)
    a = lax.ppermute(first, axis, [(i, i ^ 1) for i in range(count)])
    pairs = [(i, (i - 1 if i % 2 == 0 else i + 1) % count) for i in range(count)]
    b = lax.ppermute(second, axis, pairs)
    return a, b


def per_device(
    primal, dual, measured, footprint_weights, pixel_index, bin_index, slot_count,
    dual_kernel, dual_bias, dual_slope, dual_mixing, dual_shift,
    primal_kernel, primal_bias, primal_slope, primal_mixing, primal_shift,
):
    pix = jnp.transpose(pixel_index, (2, 0, 1))
    bins = jnp.transpose(bin_index, (2, 0, 1))
    hbm = lambda x: pltpu.with_memory_space_constraint(x, pltpu.HBM)

    own, head = call(
        pack_kernel, [((32, 1024), F32), ((HEAD, 12, 128, 128), F32)], [HBM] * 4,
        [
            pltpu.VMEM((5, 2, 1, 1024), F32),
            pltpu.VMEM((2, 1, 1024), F32),
            pltpu.VMEM((5, 2, 4, 512), F32),
            pltpu.SemaphoreType.DMA((4,)),
        ],
        4 << 20,
    )(hbm(dual), hbm(measured), hbm(primal), hbm(footprint_weights))
    near = swaps(own, own, "tile")

    terms, w_hi, w_lo = pl.pallas_call(
        project_kernel,
        name="project",
        out_shape=(
            jax.ShapeDtypeStruct((16, 3, 16, 128), F32),
            jax.ShapeDtypeStruct((16, 1536, 128), BF16),
            jax.ShapeDtypeStruct((16, 1536, 128), BF16),
        ),
        in_specs=[HBM] * 5 + [VMEM],
        out_specs=(VMEM, VMEM, VMEM),
        scratch_shapes=[pltpu.VMEM((18, 3, 16, 128), F32)]
        + [pltpu.VMEM((16, 16, 128), BF16)] * 3
        + [
            pltpu.SMEM((12, 1, 16), jnp.int32),
            pltpu.SMEM((12, 1, 16), jnp.int32),
            pltpu.SMEM((1, 16), jnp.int32),
            pltpu.VMEM((2, 4, 512), F32),
            pltpu.VMEM((16 - HEAD, 12, 128, 128), F32),
            pltpu.SemaphoreType.DMA((4,)),
            pltpu.SemaphoreType.DMA((8,)),
        ],
        compiler_params=pltpu.CompilerParams(vmem_limit_bytes=18 << 20),
        cost_estimate=pl.CostEstimate(flops=1 << 31, bytes_accessed=25 << 20, transcendentals=0),
    )(hbm(pix), hbm(bins), hbm(slot_count), hbm(primal), hbm(footprint_weights), head)
    terms, near = lax.optimization_barrier((terms, near))
    sp, sm, side_a, side_b = call(
        rims_kernel, [((64, 1024), F32)] * 4, [VMEM] * 4
    )(own, *near, primal)
    sides = swaps(side_a, side_b, "plane")
    got = lax.all_to_all(terms, "tile", 0, 0, tiled=True)
    total = call(total_kernel, [((48, 128), F32)], [VMEM])(got)[0]
    rows = swaps(total, total, "plane")

    known, last = call(
        dual_known_kernel, [((128, 1024), F32), ((128, 240), BF16)],
        [VMEM] * 4 + [SMEM],
        [pltpu.VMEM((80, 96), F32), pltpu.VMEM((80, 128), F32)],
    )(sp, *sides, jnp.transpose(dual_kernel, (2, 3, 4, 1, 0)), dual_bias)

    new_rows, send = call(
        dual_kernel_body, [((5, 2, 1, 1024), F32), ((16, 8, 4, 128), F32)],
        [VMEM] * 9 + [SMEM] * 2, [pltpu.VMEM((80, 1024), F32)],
    )(
        total, *rows, sp, *sides, known, last, dual_mixing,
        dual_slope, dual_shift,
    )
    leading = lax.all_to_all(send, "tile", 0, 0, tiled=True)

    back, edge_a, edge_b, new_dual = pl.pallas_call(
        back_kernel,
        name="back",
        out_shape=(
            jax.ShapeDtypeStruct((64, 128), F32),
            jax.ShapeDtypeStruct((16, 128), F32),
            jax.ShapeDtypeStruct((16, 128), F32),
            jax.ShapeDtypeStruct((5, 2, 1, 1024), F32),
        ),
        in_specs=[HBM, HBM, HBM, VMEM, VMEM, VMEM, VMEM],
        out_specs=(VMEM, VMEM, VMEM, HBM),
        scratch_shapes=[
            pltpu.VMEM((16, 8, 8, 128), F32),
            pltpu.VMEM((17, 8, 128), F32),
            pltpu.SMEM((12, 1, 16), jnp.int32),
            pltpu.SMEM((12, 1, 16), jnp.int32),
            pltpu.SMEM((1, 16), jnp.int32),
            pltpu.SemaphoreType.DMA((4,)),
        ],
        compiler_params=pltpu.CompilerParams(vmem_limit_bytes=4 << 20),
    )(
        hbm(pix), hbm(bins), hbm(slot_count), leading, w_hi, w_lo, new_rows,
    )
    edges = swaps(edge_a, edge_b, "tile")

    known, last = call(
        primal_known_kernel, [((256, 512), F32), ((256, 240), BF16)],
        [VMEM] * 5 + [SMEM],
        [pltpu.VMEM((96, 384), F32), pltpu.VMEM((80, 256), F32), pltpu.VMEM((128, 512), F32)],
    )(sp, sm, *sides, jnp.transpose(primal_kernel, (1, 2, 3, 4, 0)), primal_bias)

    new_primal = call(
        primal_kernel_body, [((5, 2, 4, 512), F32)], [VMEM] * 7 + [SMEM] * 2,
        [pltpu.VMEM((80, 512), F32)],
    )(
        back, *edges, known, last, primal, primal_mixing, primal_slope, primal_shift,
    )[0]
    return new_primal, new_dual


def solution(mesh):
    grid = P(None, "plane", "tile", None)
    in_specs = (
        grid, grid, P("plane", "tile", None), P("tile", None, None, None, None),
        P("tile", None, None), P(), P("tile", None),
    ) + (P(),) * 10
    return jax.shard_map(
        per_device, mesh=mesh, in_specs=in_specs, out_specs=(grid, grid), check_vma=False
    )
```

```python
import jax
import jax.numpy as jnp
from jax import lax
from jax.experimental import pallas as pl
from jax.experimental.pallas import tpu as pltpu
from jax.sharding import PartitionSpec as P


F32 = jnp.float32
BF16 = jnp.bfloat16
VMEM = pl.BlockSpec(memory_space=pltpu.VMEM)
SMEM = pl.BlockSpec(memory_space=pltpu.SMEM)
HBM = pl.BlockSpec(memory_space=pltpu.HBM)


def split(x):
    hi = x.astype(BF16)
    return hi, (x - hi.astype(F32)).astype(BF16)


def is_even(axis):
    return (lax.axis_index(axis) & 1) == 0


def joined(a):
    hi, lo = split(a)
    return jnp.concatenate([hi, lo, hi], 1)


def dot3(left, b):
    hi, lo = split(b)
    return jnp.dot(left, jnp.concatenate([hi, hi, lo], 0), preferred_element_type=F32)


def column(ref, count):
    rows = -(-count // 8) * 8
    index = lax.broadcasted_iota(jnp.int32, (rows, 128), 0)
    out = jnp.zeros((rows, 128), F32)
    for i in range(count):
        out = jnp.where(index == i, ref[i], out)
    return out[:, 0:1]


def shifted_sum(stack):
    left, mid, right = stack
    width = mid.shape[1]
    lane = lax.broadcasted_iota(jnp.int32, mid.shape, 1)
    left = jnp.where(lane == 0, 0.0, pltpu.roll(left, 1, 1))
    right = jnp.where(lane == width - 1, 0.0, pltpu.roll(right, width - 1, 1))
    return left + mid + right


CHUNK = 8
ROOM = 96 + CHUNK
SURE = 48


def pack_kernel(dual_hbm, measured_hbm, primal_hbm, out_ref, dual_ref, measured_ref, primal_ref, sem):
    copies = [
        pltpu.make_async_copy(src, dst, sem.at[i])
        for i, (src, dst) in enumerate(
            ((dual_hbm, dual_ref), (measured_hbm, measured_ref), (primal_hbm, primal_ref))
        )
    ]
    for copy in copies:
        copy.start()
    for copy in copies:
        copy.wait()
    zero = jnp.zeros((1, 1024), F32)
    for z in range(2):
        for c in range(5):
            out_ref[z * 8 + c : z * 8 + c + 1, :] = dual_ref[c, z]
        out_ref[z * 8 + 5 : z * 8 + 6, :] = zero
        out_ref[z * 8 + 6 : z * 8 + 7, :] = measured_ref[z]
        out_ref[z * 8 + 7 : z * 8 + 8, :] = zero
    for k, row in enumerate((0, 3)):
        for c in range(5):
            for z in range(2):
                i = 16 + k * 5 + c
                out_ref[i : i + 1, z * 512 : (z + 1) * 512] = primal_ref[c, z, row : row + 1, :]
    out_ref[26:32, :] = jnp.zeros((6, 1024), F32)


def index_copies(pix_hbm, bin_hbm, cnt_hbm, pix_ref, bin_ref, cnt_ref, sem):
    t = lax.axis_index("tile")
    return [
        pltpu.make_async_copy(pix_hbm, pix_ref, sem.at[0]),
        pltpu.make_async_copy(bin_hbm.at[:, pl.ds(t, 1), :], bin_ref, sem.at[1]),
        pltpu.make_async_copy(cnt_hbm, cnt_ref, sem.at[2]),
    ]


def list_pairs(cnt_ref, list_ref):
    base = 0
    for a in range(16):
        for k in range(3):
            list_ref[base + k] = a * 8 + 3 + k
        base = base + ((cnt_ref[0, a] - 5) >> 1)
    for k in range(CHUNK):
        list_ref[base + k] = 128 + 3
    return (base + CHUNK - 1) // CHUNK


def pair_at(list_ref, cnt_ref, i):
    code = list_ref[i]
    a, k = (code >> 3) & 15, code & 7
    return a, k, jnp.where(code < 128, cnt_ref[0, a], 0)


def project_kernel(
    pix_hbm, bin_hbm, cnt_hbm, primal_hbm, w_hbm, after_ref,
    out_ref, wh_ref, wl_ref,
    acc_ref, hi_ref, lo_ref, hot_ref, pix_ref, bin_ref, cnt_ref, list_ref, primal_ref, w_ref,
    sem, sure_sem, w_sem,
):
    del after_ref
    copies = index_copies(pix_hbm, bin_hbm, cnt_hbm, pix_ref, bin_ref, cnt_ref, sem)
    copies.append(pltpu.make_async_copy(primal_hbm.at[1], primal_ref, sem.at[3]))
    for copy in copies[::-1]:
        copy.start()

    def fetch_sure(a):
        return pltpu.make_async_copy(
            w_hbm.at[a, pl.ds(0, 3)], w_ref.at[pl.ds(a * 3, 3)], sure_sem.at[a]
        )

    def fetch(i):
        a, k, _ = pair_at(list_ref, cnt_ref, i)
        return pltpu.make_async_copy(w_hbm.at[a, k], w_ref.at[SURE + i], w_sem.at[i])

    for a in range(16):
        fetch_sure(a).start()
    copies[2].wait()
    steps = list_pairs(cnt_ref, list_ref)
    for c in range(6):

        @pl.when(c < steps)
        def _():
            for j in range(CHUNK):
                fetch(c * CHUNK + j).start()

    row = lax.broadcasted_iota(jnp.int32, (16, 128), 0)
    for b in range(9):
        hot_ref[b] = jnp.where((row & 7) == b, 1.0, 0.0).astype(BF16)
    copies[3].wait()
    for q in range(16):
        r, col = q // 4, (q % 4) * 128
        v = jnp.concatenate(
            [
                jnp.broadcast_to(primal_ref[z, r : r + 1, col : col + 128], (8, 128))
                for z in range(2)
            ],
            0,
        )
        hi_ref[q], lo_ref[q] = split(v)
    copies[0].wait()
    copies[1].wait()

    def operands(i, a, k, count):
        parts = []
        for s in (k * 2, k * 2 + 1):
            q, b = pix_ref[s, 0, a], bin_ref[s, 0, a]
            hot = hot_ref[b if count is None else jnp.where(s < count, b, 8)]
            parts.append(jnp.concatenate([hi_ref[q] * hot, lo_ref[q] * hot], 0))
        w_hi, w_lo = split(w_ref[i])
        wh_ref[i], wl_ref[i] = w_hi, w_lo
        return jnp.concatenate(parts, 1), jnp.concatenate([w_hi, w_lo], 1)

    def product(left, right):
        d = jnp.dot(left, right, preferred_element_type=F32)
        return d[0:16, 0:128] + (d[0:16, 128:256] + d[16:32, 0:128])

    def sure_step(c, carry):
        for j in range(4):
            fetch_sure(c * 4 + j).wait()
        for j in range(4):
            a = c * 4 + j
            lefts, rights = zip(*(operands(a * 3 + k, a, k, None) for k in range(3)))
            acc_ref[a] = product(jnp.concatenate(lefts, 1), jnp.concatenate(rights, 0))
        return carry

    def step(c, carry):
        for j in range(CHUNK):
            fetch(c * CHUNK + j).wait()
        for j in range(CHUNK):
            i = c * CHUNK + j
            a, k, count = pair_at(list_ref, cnt_ref, i)
            acc_ref[a] += product(*operands(SURE + i, a, k, count))
        return carry

    lax.fori_loop(0, 4, sure_step, 0)
    lax.fori_loop(0, steps, step, 0)
    zero = jnp.zeros((16, 128), F32)
    for a in range(16):
        for k in range(3):
            out_ref[a, k] = acc_ref[a + k - 1] if 0 <= a + k - 1 < 16 else zero


def rims_kernel(own_ref, first_ref, second_ref, primal_ref, sp_ref, sm_ref, a_ref, b_ref):
    t = lax.axis_index("tile")
    even, even_plane = is_even("tile"), is_even("plane")

    def left(rows, lanes):
        return jnp.where(even, second_ref[rows, lanes], first_ref[rows, lanes])

    def right(rows, lanes):
        return jnp.where(even, first_ref[rows, lanes], second_ref[rows, lanes])

    every = slice(None)
    for z in range(2):
        rows = slice(z * 8, z * 8 + 8)
        blocks = (
            jnp.where(t > 0, left(rows, every), 0.0),
            own_ref[rows, :],
            jnp.where(t < 15, right(rows, every), 0.0),
        )
        for k, block in enumerate(blocks):
            base = z * 24 + k * 8
            for out in (sp_ref, sm_ref, a_ref, b_ref):
                out[base : base + 8, :] = block
    for z, out in ((0, sm_ref), (1, sp_ref)):
        half = slice(z * 512, (z + 1) * 512)
        for row in range(6):
            for c in range(5):
                if row == 0:
                    v = jnp.where(t > 0, left(slice(21 + c, 22 + c), half), 0.0)
                elif row == 5:
                    v = jnp.where(t < 15, right(slice(16 + c, 17 + c), half), 0.0)
                else:
                    v = primal_ref[c, z, row - 1 : row, :]
                i = row * 5 + c
                lane = (i // 16) * 512
                out[48 + i % 16 : 49 + i % 16, lane : lane + 512] = v
        out[62:64, 512:1024] = jnp.zeros((2, 512), F32)
    up, down = sp_ref[48:64, :], sm_ref[48:64, :]
    a_ref[48:64, :] = jnp.where(even_plane, up, down)
    b_ref[48:64, :] = jnp.where(even_plane, down, up)


def total_kernel(got_ref, out_ref):
    t = lax.axis_index("tile")
    for k, ok in enumerate((t > 0, None, t < 15)):
        total = got_ref[0, k]
        for i in range(1, 16):
            total = total + got_ref[i, k]
        if ok is not None:
            total = jnp.where(ok, total, 0.0)
        out_ref[k * 16 : k * 16 + 16, :] = total


def plane_sides(first_ref, second_ref, rows):
    p = lax.axis_index("plane")
    even = is_even("plane")
    first, second = first_ref[rows, :], second_ref[rows, :]
    before = jnp.where(p > 0, jnp.where(even, second, first), 0.0)
    return before, jnp.where(p < 7, jnp.where(even, first, second), 0.0)


def dual_inputs(own_ref, first_ref, second_ref):
    before, after = plane_sides(first_ref, second_ref, slice(0, 48))
    return jnp.concatenate(
        [
            before,
            own_ref[0:48, :],
            after,
            jnp.zeros((8, 1024), F32),
        ],
        0,
    )


def dual_known_kernel(
    own_ref, first_ref, second_ref, kern_ref, bias_ref, known_ref, last_ref, tt_ref, lt_ref
):
    tt_ref[...] = jnp.zeros((80, 96), F32)
    lt_ref[...] = jnp.zeros((80, 128), F32)
    for dz in range(3):
        for da in range(3):
            tiles = [kern_ref[dz, da, db] for db in range(3)]
            base = dz * 24 + da * 8
            tt_ref[base : base + 7, :] = jnp.concatenate(tiles, 1)
            for db in range(3):
                four = jnp.concatenate([tiles[db][5:6]] * 4, 1)
                for z in range(4):
                    i = db * 24 + (z + dz) * 3 + da
                    lt_ref[i : i + 1, z * 32 : (z + 1) * 32] = four[:, z * 32 : (z + 1) * 32]
    last_ref[...] = joined(lt_ref[...].T)
    x = dual_inputs(own_ref, first_ref, second_ref)
    tt = joined(tt_ref[...].T)
    bias = column(bias_ref, 32)
    for z in range(4):
        h = dot3(tt, x[z * 24 : z * 24 + 80])
        h = shifted_sum([h[i * 32 : (i + 1) * 32] for i in range(3)]) + bias
        known_ref[z * 32 : (z + 1) * 32, :] = h


def spread_columns(y_ref, width):
    mid = y_ref[24:48, :]
    lane = lax.broadcasted_iota(jnp.int32, mid.shape, 1)
    y_ref[0:24, :] = jnp.where(lane == 0, 0.0, pltpu.roll(mid, 1, 1))
    y_ref[48:72, :] = jnp.where(lane == width - 1, 0.0, pltpu.roll(mid, width - 1, 1))


def dual_kernel_body(
    total_ref, ta_ref, tb_ref, own_ref, first_ref, second_ref, known_ref, last_ref,
    mix_ref, slope_ref, shift_ref, new_ref, send_ref, y_ref,
):
    y_ref[...] = jnp.zeros((80, 1024), F32)
    before, after = plane_sides(ta_ref, tb_ref, slice(0, 48))
    for start, v in ((0, before), (2, total_ref[...]), (4, after)):
        for k in range(3):
            for z in range(2):
                row = 24 + (start + z) * 3 + k
                for b in range(8):
                    i = k * 16 + z * 8 + b
                    y_ref[row : row + 1, b * 128 : (b + 1) * 128] = v[i : i + 1]
    spread_columns(y_ref, 1024)
    slope, shift = column(slope_ref, 32), column(shift_ref, 5)
    mix = joined(jnp.concatenate([mix_ref[...], jnp.zeros((3, 32), F32)], 0))
    h = dot3(last_ref[...], y_ref[...]) + known_ref[...]
    dual_rows = (
        plane_sides(first_ref, second_ref, slice(32, 40))[0],
        own_ref[8:16, :],
        own_ref[32:40, :],
        plane_sides(first_ref, second_ref, slice(8, 16))[1],
    )
    for z in range(4):
        g = h[z * 32 : (z + 1) * 32]
        g = jnp.where(g > 0, g, slope * g)
        out = dot3(mix, g) + shift + dual_rows[z]
        if z in (1, 2):
            for c in range(5):
                new_ref[c, z - 1] = out[c : c + 1, :]
        for b in range(8):
            piece = jnp.broadcast_to(out[0:1, b * 128 : (b + 1) * 128], (16, 128))
            send_ref[:, b, z, :] = piece


def back_kernel(
    pix_hbm, bin_hbm, cnt_hbm, nd_ref, wh_ref, wl_ref, new_ref,
    out_ref, first_ref, second_ref, new_hbm, tab_ref, acc_ref, pix_ref, bin_ref, cnt_ref, list_ref,
    sem,
):
    even = is_even("tile")
    copies = index_copies(pix_hbm, bin_hbm, cnt_hbm, pix_ref, bin_ref, cnt_ref, sem)
    for copy in copies:
        copy.start()
    out_copy = pltpu.make_async_copy(new_ref, new_hbm, sem.at[3])
    out_copy.start()
    for a in range(16):
        for b in range(8):
            v = nd_ref[a, b]
            hi = v.astype(BF16).astype(F32)
            tab_ref[a, b, 0:4] = hi
            tab_ref[a, b, 4:8] = v - hi
    acc_ref[...] = jnp.zeros_like(acc_ref)
    zero = jnp.zeros((8, 128), F32)
    for copy in copies:
        copy.wait()

    steps = list_pairs(cnt_ref, list_ref)

    def pair(i, a, k, count):
        slots = (k * 2, k * 2 + 1)
        one, two = (tab_ref[a, bin_ref[s, 0, a]] for s in slots)
        left = jnp.concatenate(
            [jnp.concatenate([one, zero], 1), jnp.concatenate([zero, two], 1)], 0
        ).astype(BF16)
        right = jnp.concatenate(
            [jnp.concatenate([w[i, 0:128, :], w[i, 128:256, :]], 1) for w in (wh_ref, wl_ref)], 0
        )
        d = lax.dot_general(left, right, (((1,), (1,)), ((), ())), preferred_element_type=F32)
        d = d[:, 0:128] + d[:, 128:256]
        for n, s in enumerate(slots):
            q = pix_ref[s, 0, a]
            acc_ref[q if count is None else jnp.where(s < count, q, 16)] += d[n * 8 : n * 8 + 8]

    def sure_step(c, carry):
        for j in range(4):
            for k in range(3):
                a = c * 4 + j
                pair(a * 3 + k, a, k, None)
        return carry

    def step(c, carry):
        for j in range(CHUNK):
            i = c * CHUNK + j
            pair(SURE + i, *pair_at(list_ref, cnt_ref, i))
        return carry

    lax.fori_loop(0, 4, sure_step, 0)
    lax.fori_loop(0, steps, step, 0)
    for q in range(16):
        v = acc_ref[q, 0:4] + acc_ref[q, 4:8]
        out_ref[q * 4 : q * 4 + 4, :] = v
    up, down = out_ref[0:16, :], out_ref[48:64, :]
    first_ref[...] = jnp.where(even, down, up)
    second_ref[...] = jnp.where(even, up, down)
    out_copy.wait()


def primal_known_kernel(
    sp_ref, sm_ref, first_ref, second_ref, kern_ref, bias_ref, known_ref, last_ref,
    tt_ref, lt_ref, x_ref,
):
    before, after = plane_sides(first_ref, second_ref, slice(48, 64))
    for plane, v in enumerate((before, sm_ref[48:64, :], sp_ref[48:64, :], after)):
        for half in range(2):
            i = plane * 32 + half * 16
            x_ref[i : i + 16, :] = v[:, half * 512 : (half + 1) * 512]
    tt_ref[...] = jnp.zeros((96, 384), F32)
    lt_ref[...] = jnp.zeros((80, 256), F32)
    for dz in range(3):
        for dr in range(3):
            block = jnp.concatenate(
                [
                    jnp.concatenate([kern_ref[c, dz, dr, db : db + 1, :] for db in range(3)], 1)
                    for c in range(5)
                ],
                0,
            )
            for r in range(4):
                i = dz * 32 + (r + dr) * 5
                tt_ref[i : i + 5, r * 96 : (r + 1) * 96] = block
            for db in range(3):
                four = jnp.concatenate([kern_ref[5, dz, dr, db : db + 1, :]] * 4, 1)
                for z in range(2):
                    for r in range(4):
                        i = db * 24 + (z + dz) * 6 + r + dr
                        lane = z * 128 + r * 32
                        lt_ref[i : i + 1, lane : lane + 32] = four[:, r * 32 : (r + 1) * 32]
    last_ref[...] = joined(lt_ref[...].T)
    tt = joined(tt_ref[...].T)
    bias = column(bias_ref, 32)
    for z in range(2):
        h = dot3(tt, x_ref[z * 32 : z * 32 + 96])
        for r in range(4):
            g = shifted_sum([h[r * 96 + i * 32 : r * 96 + (i + 1) * 32] for i in range(3)]) + bias
            i = (z * 4 + r) * 32
            known_ref[i : i + 32, :] = g


def primal_kernel_body(
    back_ref, first_ref, second_ref, known_ref, last_ref, primal_ref,
    mix_ref, slope_ref, shift_ref, new_ref, y_ref,
):
    p = lax.axis_index("plane")
    t = lax.axis_index("tile")
    keeps = (p > 0, None, None, p < 7)
    even = is_even("tile")
    first, second = first_ref[...], second_ref[...]
    above = jnp.where(t > 0, jnp.where(even, second, first), 0.0)
    below = jnp.where(t < 15, jnp.where(even, first, second), 0.0)
    y_ref[...] = jnp.zeros((80, 512), F32)
    for plane in range(4):
        for row in range(6):
            for col in range(4):
                if row == 0:
                    i = col * 4 + plane
                    v = above[i : i + 1]
                elif row == 5:
                    i = col * 4 + plane
                    v = below[i : i + 1]
                else:
                    i = (row * 4 - 4 + col) * 4 + plane
                    v = back_ref[i : i + 1, :]
                if keeps[plane] is not None:
                    v = jnp.where(keeps[plane], v, 0.0)
                i = 24 + plane * 6 + row
                y_ref[i : i + 1, col * 128 : (col + 1) * 128] = v
    spread_columns(y_ref, 512)
    slope, shift = column(slope_ref, 32), column(shift_ref, 5)
    mix = joined(jnp.concatenate([mix_ref[...], jnp.zeros((3, 32), F32)], 0))
    h = dot3(last_ref[...], y_ref[...]) + known_ref[...]
    for z in range(2):
        for r in range(4):
            i = (z * 4 + r) * 32
            g = h[i : i + 32]
            g = jnp.where(g > 0, g, slope * g)
            out = dot3(mix, g) + shift
            for c in range(5):
                new_ref[c, z, r : r + 1, :] = out[c : c + 1, :] + primal_ref[c, z, r : r + 1, :]


def call(body, outs, in_specs, scratch=(), limit=8 << 20):
    return pl.pallas_call(
        body,
        out_shape=tuple(jax.ShapeDtypeStruct(s[0], s[1]) for s in outs),
        in_specs=in_specs,
        out_specs=tuple(VMEM for _ in outs),
        scratch_shapes=list(scratch),
        compiler_params=pltpu.CompilerParams(vmem_limit_bytes=limit),
    )


def swaps(first, second, axis):
    count = lax.axis_size(axis)
    a = lax.ppermute(first, axis, [(i, i ^ 1) for i in range(count)])
    pairs = [(i, (i - 1 if i % 2 == 0 else i + 1) % count) for i in range(count)]
    b = lax.ppermute(second, axis, pairs)
    return a, b


def per_device(
    primal, dual, measured, footprint_weights, pixel_index, bin_index, slot_count,
    dual_kernel, dual_bias, dual_slope, dual_mixing, dual_shift,
    primal_kernel, primal_bias, primal_slope, primal_mixing, primal_shift,
):
    pix = jnp.transpose(pixel_index, (2, 0, 1))
    bins = jnp.transpose(bin_index, (2, 0, 1))
    hbm = lambda x: pltpu.with_memory_space_constraint(x, pltpu.HBM)

    own = call(
        pack_kernel, [((32, 1024), F32)], [HBM] * 3,
        [
            pltpu.VMEM((5, 2, 1, 1024), F32),
            pltpu.VMEM((2, 1, 1024), F32),
            pltpu.VMEM((5, 2, 4, 512), F32),
            pltpu.SemaphoreType.DMA((3,)),
        ],
    )(hbm(dual), hbm(measured), hbm(primal))[0]
    pairs = footprint_weights.reshape(16, 6, 256, 128)

    near = swaps(own, own, "tile")

    terms, w_hi, w_lo = pl.pallas_call(
        project_kernel,
        name="project",
        out_shape=(
            jax.ShapeDtypeStruct((16, 3, 16, 128), F32),
            jax.ShapeDtypeStruct((ROOM, 256, 128), BF16),
            jax.ShapeDtypeStruct((ROOM, 256, 128), BF16),
        ),
        in_specs=[HBM] * 5 + [VMEM],
        out_specs=(VMEM, VMEM, VMEM),
        scratch_shapes=[pltpu.VMEM((16, 16, 128), F32)]
        + [pltpu.VMEM((16, 16, 128), BF16)] * 3
        + [
            pltpu.SMEM((12, 1, 16), jnp.int32),
            pltpu.SMEM((12, 1, 16), jnp.int32),
            pltpu.SMEM((1, 16), jnp.int32),
            pltpu.SMEM((128,), jnp.int32),
            pltpu.VMEM((2, 4, 512), F32),
            pltpu.VMEM((ROOM, 256, 128), F32),
            pltpu.SemaphoreType.DMA((4,)),
            pltpu.SemaphoreType.DMA((16,)),
            pltpu.SemaphoreType.DMA((ROOM - SURE,)),
        ],
        compiler_params=pltpu.CompilerParams(vmem_limit_bytes=18 << 20),
        cost_estimate=pl.CostEstimate(flops=1 << 31, bytes_accessed=25 << 20, transcendentals=0),
    )(hbm(pix), hbm(bins), hbm(slot_count), hbm(primal), hbm(pairs), own)
    terms, near = lax.optimization_barrier((terms, near))
    sp, sm, side_a, side_b = call(
        rims_kernel, [((64, 1024), F32)] * 4, [VMEM] * 4
    )(own, *near, primal)
    sides = swaps(side_a, side_b, "plane")
    got = lax.all_to_all(terms, "tile", 0, 0, tiled=True)
    total = call(total_kernel, [((48, 128), F32)], [VMEM])(got)[0]
    rows = swaps(total, total, "plane")

    known, last = call(
        dual_known_kernel, [((128, 1024), F32), ((128, 240), BF16)],
        [VMEM] * 4 + [SMEM],
        [pltpu.VMEM((80, 96), F32), pltpu.VMEM((80, 128), F32)],
    )(sp, *sides, jnp.transpose(dual_kernel, (2, 3, 4, 1, 0)), dual_bias)

    new_rows, send = call(
        dual_kernel_body, [((5, 2, 1, 1024), F32), ((16, 8, 4, 128), F32)],
        [VMEM] * 9 + [SMEM] * 2, [pltpu.VMEM((80, 1024), F32)],
    )(
        total, *rows, sp, *sides, known, last, dual_mixing,
        dual_slope, dual_shift,
    )
    leading = lax.all_to_all(send, "tile", 0, 0, tiled=True)

    back, edge_a, edge_b, new_dual = pl.pallas_call(
        back_kernel,
        name="back",
        out_shape=(
            jax.ShapeDtypeStruct((64, 128), F32),
            jax.ShapeDtypeStruct((16, 128), F32),
            jax.ShapeDtypeStruct((16, 128), F32),
            jax.ShapeDtypeStruct((5, 2, 1, 1024), F32),
        ),
        in_specs=[HBM, HBM, HBM, VMEM, VMEM, VMEM, VMEM],
        out_specs=(VMEM, VMEM, VMEM, HBM),
        scratch_shapes=[
            pltpu.VMEM((16, 8, 8, 128), F32),
            pltpu.VMEM((17, 8, 128), F32),
            pltpu.SMEM((12, 1, 16), jnp.int32),
            pltpu.SMEM((12, 1, 16), jnp.int32),
            pltpu.SMEM((1, 16), jnp.int32),
            pltpu.SMEM((128,), jnp.int32),
            pltpu.SemaphoreType.DMA((4,)),
        ],
        compiler_params=pltpu.CompilerParams(vmem_limit_bytes=4 << 20),
    )(
        hbm(pix), hbm(bins), hbm(slot_count), leading, w_hi, w_lo, new_rows,
    )
    edges = swaps(edge_a, edge_b, "tile")

    known, last = call(
        primal_known_kernel, [((256, 512), F32), ((256, 240), BF16)],
        [VMEM] * 5 + [SMEM],
        [pltpu.VMEM((96, 384), F32), pltpu.VMEM((80, 256), F32), pltpu.VMEM((128, 512), F32)],
    )(sp, sm, *sides, jnp.transpose(primal_kernel, (1, 2, 3, 4, 0)), primal_bias)

    new_primal = call(
        primal_kernel_body, [((5, 2, 4, 512), F32)], [VMEM] * 7 + [SMEM] * 2,
        [pltpu.VMEM((80, 512), F32)],
    )(
        back, *edges, known, last, primal, primal_mixing, primal_slope, primal_shift,
    )[0]
    return new_primal, new_dual


def solution(mesh):
    grid = P(None, "plane", "tile", None)
    in_specs = (
        grid, grid, P("plane", "tile", None), P("tile", None, None, None, None),
        P("tile", None, None), P(), P("tile", None),
    ) + (P(),) * 10
    return jax.shard_map(
        per_device, mesh=mesh, in_specs=in_specs, out_specs=(grid, grid), check_vma=False
    )
```

```python
import jax
import jax.numpy as jnp
from jax import lax
from jax.experimental import pallas as pl
from jax.experimental.pallas import tpu as pltpu
from jax.sharding import PartitionSpec as P


F32 = jnp.float32
BF16 = jnp.bfloat16
VMEM = pl.BlockSpec(memory_space=pltpu.VMEM)
SMEM = pl.BlockSpec(memory_space=pltpu.SMEM)
HBM = pl.BlockSpec(memory_space=pltpu.HBM)


def split(x):
    hi = x.astype(BF16)
    return hi, (x - hi.astype(F32)).astype(BF16)


def is_even(axis):
    return (lax.axis_index(axis) & 1) == 0


def joined(a):
    hi, lo = split(a)
    return jnp.concatenate([hi, lo, hi], 1)


def dot3(left, b):
    hi, lo = split(b)
    return jnp.dot(left, jnp.concatenate([hi, hi, lo], 0), preferred_element_type=F32)


def column(ref, count):
    rows = -(-count // 8) * 8
    index = lax.broadcasted_iota(jnp.int32, (rows, 128), 0)
    out = jnp.zeros((rows, 128), F32)
    for i in range(count):
        out = jnp.where(index == i, ref[i], out)
    return out[:, 0:1]


def shifted_sum(stack):
    left, mid, right = stack
    width = mid.shape[1]
    lane = lax.broadcasted_iota(jnp.int32, mid.shape, 1)
    left = jnp.where(lane == 0, 0.0, pltpu.roll(left, 1, 1))
    right = jnp.where(lane == width - 1, 0.0, pltpu.roll(right, width - 1, 1))
    return left + mid + right


CHUNK = 8
ROOM = 96 + CHUNK
SURE = 48


def pack_kernel(dual_hbm, measured_hbm, primal_hbm, out_ref, dual_ref, measured_ref, primal_ref, sem):
    copies = [
        pltpu.make_async_copy(src, dst, sem.at[i])
        for i, (src, dst) in enumerate(
            ((dual_hbm, dual_ref), (measured_hbm, measured_ref), (primal_hbm, primal_ref))
        )
    ]
    for copy in copies:
        copy.start()
    for copy in copies:
        copy.wait()
    zero = jnp.zeros((1, 1024), F32)
    for z in range(2):
        for c in range(5):
            out_ref[z * 8 + c : z * 8 + c + 1, :] = dual_ref[c, z]
        out_ref[z * 8 + 5 : z * 8 + 6, :] = zero
        out_ref[z * 8 + 6 : z * 8 + 7, :] = measured_ref[z]
        out_ref[z * 8 + 7 : z * 8 + 8, :] = zero
    for k, row in enumerate((0, 3)):
        for c in range(5):
            for z in range(2):
                i = 16 + k * 5 + c
                out_ref[i : i + 1, z * 512 : (z + 1) * 512] = primal_ref[c, z, row : row + 1, :]
    out_ref[26:32, :] = jnp.zeros((6, 1024), F32)


def index_copies(pix_hbm, bin_hbm, cnt_hbm, pix_ref, bin_ref, cnt_ref, sem):
    t = lax.axis_index("tile")
    return [
        pltpu.make_async_copy(pix_hbm, pix_ref, sem.at[0]),
        pltpu.make_async_copy(bin_hbm.at[:, pl.ds(t, 1), :], bin_ref, sem.at[1]),
        pltpu.make_async_copy(cnt_hbm, cnt_ref, sem.at[2]),
    ]


def list_pairs(cnt_ref, list_ref):
    base = 0
    for a in range(16):
        for k in range(3):
            list_ref[base + k] = a * 8 + 3 + k
        base = base + ((cnt_ref[0, a] - 5) >> 1)
    for k in range(CHUNK):
        list_ref[base + k] = 128 + 3
    return (base + CHUNK - 1) // CHUNK


def pair_at(list_ref, cnt_ref, i):
    code = list_ref[i]
    a, k = (code >> 3) & 15, code & 7
    return a, k, jnp.where(code < 128, cnt_ref[0, a], 0)


def project_kernel(
    pix_hbm, bin_hbm, cnt_hbm, primal_hbm, w_hbm, after_ref,
    out_ref, wh_ref, wl_ref,
    acc_ref, hi_ref, lo_ref, hot_ref, pix_ref, bin_ref, cnt_ref, list_ref, primal_ref, w_ref,
    sem, sure_sem, w_sem,
):
    del after_ref
    copies = index_copies(pix_hbm, bin_hbm, cnt_hbm, pix_ref, bin_ref, cnt_ref, sem)
    copies.append(pltpu.make_async_copy(primal_hbm.at[1], primal_ref, sem.at[3]))
    for copy in copies[::-1]:
        copy.start()

    def fetch_sure(a):
        return pltpu.make_async_copy(
            w_hbm.at[a, pl.ds(0, 3)], w_ref.at[pl.ds(a * 3, 3)], sure_sem.at[a]
        )

    def fetch(i):
        a, k, _ = pair_at(list_ref, cnt_ref, i)
        return pltpu.make_async_copy(w_hbm.at[a, k], w_ref.at[SURE + i], w_sem.at[i])

    for a in range(16):
        fetch_sure(a).start()
    copies[2].wait()
    steps = list_pairs(cnt_ref, list_ref)
    for c in range(6):

        @pl.when(c < steps)
        def _():
            for j in range(CHUNK):
                fetch(c * CHUNK + j).start()

    row = lax.broadcasted_iota(jnp.int32, (16, 128), 0)
    for b in range(9):
        hot_ref[b] = jnp.where((row & 7) == b, 1.0, 0.0).astype(BF16)
    copies[3].wait()
    for q in range(16):
        r, col = q // 4, (q % 4) * 128
        v = jnp.concatenate(
            [
                jnp.broadcast_to(primal_ref[z, r : r + 1, col : col + 128], (8, 128))
                for z in range(2)
            ],
            0,
        )
        hi_ref[q], lo_ref[q] = split(v)
    copies[0].wait()
    copies[1].wait()

    def operands(i, a, k, count):
        parts = []
        for s in (k * 2, k * 2 + 1):
            q, b = pix_ref[s, 0, a], bin_ref[s, 0, a]
            hot = hot_ref[b if count is None else jnp.where(s < count, b, 8)]
            parts.append(jnp.concatenate([hi_ref[q] * hot, lo_ref[q] * hot], 0))
        w_hi, w_lo = split(w_ref[i])
        wh_ref[i], wl_ref[i] = w_hi, w_lo
        return jnp.concatenate(parts, 1), jnp.concatenate([w_hi, w_lo], 1)

    def product(left, right):
        d = jnp.dot(left, right, preferred_element_type=F32)
        return d[0:16, 0:128] + (d[0:16, 128:256] + d[16:32, 0:128])

    def sure_step(c, carry):
        for j in range(4):
            fetch_sure(c * 4 + j).wait()
        for j in range(4):
            a = c * 4 + j
            lefts, rights = zip(*(operands(a * 3 + k, a, k, None) for k in range(3)))
            acc_ref[a] = product(jnp.concatenate(lefts, 1), jnp.concatenate(rights, 0))
        return carry

    def step(c, carry):
        for j in range(CHUNK):
            fetch(c * CHUNK + j).wait()
        for j in range(CHUNK):
            i = c * CHUNK + j
            a, k, count = pair_at(list_ref, cnt_ref, i)
            acc_ref[a] += product(*operands(SURE + i, a, k, count))
        return carry

    lax.fori_loop(0, 4, sure_step, 0)
    lax.fori_loop(0, steps, step, 0)
    zero = jnp.zeros((16, 128), F32)
    for a in range(16):
        for k in range(3):
            out_ref[a, k] = acc_ref[a + k - 1] if 0 <= a + k - 1 < 16 else zero


def rims_kernel(own_ref, first_ref, second_ref, primal_ref, sp_ref, sm_ref, a_ref, b_ref):
    t = lax.axis_index("tile")
    even, even_plane = is_even("tile"), is_even("plane")

    def left(rows, lanes):
        return jnp.where(even, second_ref[rows, lanes], first_ref[rows, lanes])

    def right(rows, lanes):
        return jnp.where(even, first_ref[rows, lanes], second_ref[rows, lanes])

    every = slice(None)
    for z in range(2):
        rows = slice(z * 8, z * 8 + 8)
        blocks = (
            jnp.where(t > 0, left(rows, every), 0.0),
            own_ref[rows, :],
            jnp.where(t < 15, right(rows, every), 0.0),
        )
        for k, block in enumerate(blocks):
            base = z * 24 + k * 8
            for out in (sp_ref, sm_ref, a_ref, b_ref):
                out[base : base + 8, :] = block
    for z, out in ((0, sm_ref), (1, sp_ref)):
        half = slice(z * 512, (z + 1) * 512)
        for row in range(6):
            for c in range(5):
                if row == 0:
                    v = jnp.where(t > 0, left(slice(21 + c, 22 + c), half), 0.0)
                elif row == 5:
                    v = jnp.where(t < 15, right(slice(16 + c, 17 + c), half), 0.0)
                else:
                    v = primal_ref[c, z, row - 1 : row, :]
                i = row * 5 + c
                lane = (i // 16) * 512
                out[48 + i % 16 : 49 + i % 16, lane : lane + 512] = v
        out[62:64, 512:1024] = jnp.zeros((2, 512), F32)
    up, down = sp_ref[48:64, :], sm_ref[48:64, :]
    a_ref[48:64, :] = jnp.where(even_plane, up, down)
    b_ref[48:64, :] = jnp.where(even_plane, down, up)


def total_kernel(got_ref, out_ref):
    t = lax.axis_index("tile")
    for k, ok in enumerate((t > 0, None, t < 15)):
        total = got_ref[0, k]
        for i in range(1, 16):
            total = total + got_ref[i, k]
        if ok is not None:
            total = jnp.where(ok, total, 0.0)
        out_ref[k * 16 : k * 16 + 16, :] = total


def plane_sides(first_ref, second_ref, rows):
    p = lax.axis_index("plane")
    even = is_even("plane")
    first, second = first_ref[rows, :], second_ref[rows, :]
    before = jnp.where(p > 0, jnp.where(even, second, first), 0.0)
    return before, jnp.where(p < 7, jnp.where(even, first, second), 0.0)


def dual_inputs(own_ref, first_ref, second_ref):
    before, after = plane_sides(first_ref, second_ref, slice(0, 48))
    return jnp.concatenate(
        [
            before,
            own_ref[0:48, :],
            after,
            jnp.zeros((8, 1024), F32),
        ],
        0,
    )


def dual_known_kernel(
    own_ref, first_ref, second_ref, kern_ref, bias_ref, known_ref, last_ref, tt_ref, lt_ref
):
    tt_ref[...] = jnp.zeros((80, 96), F32)
    lt_ref[...] = jnp.zeros((80, 128), F32)
    for dz in range(3):
        for da in range(3):
            tiles = [kern_ref[dz, da, db] for db in range(3)]
            base = dz * 24 + da * 8
            tt_ref[base : base + 7, :] = jnp.concatenate(tiles, 1)
            for db in range(3):
                four = jnp.concatenate([tiles[db][5:6]] * 4, 1)
                for z in range(4):
                    i = db * 24 + (z + dz) * 3 + da
                    lt_ref[i : i + 1, z * 32 : (z + 1) * 32] = four[:, z * 32 : (z + 1) * 32]
    last_ref[...] = joined(lt_ref[...].T)
    x = dual_inputs(own_ref, first_ref, second_ref)
    tt = joined(tt_ref[...].T)
    bias = column(bias_ref, 32)
    for z in range(4):
        h = dot3(tt, x[z * 24 : z * 24 + 80])
        h = shifted_sum([h[i * 32 : (i + 1) * 32] for i in range(3)]) + bias
        known_ref[z * 32 : (z + 1) * 32, :] = h


def spread_columns(y_ref, width):
    mid = y_ref[24:48, :]
    lane = lax.broadcasted_iota(jnp.int32, mid.shape, 1)
    y_ref[0:24, :] = jnp.where(lane == 0, 0.0, pltpu.roll(mid, 1, 1))
    y_ref[48:72, :] = jnp.where(lane == width - 1, 0.0, pltpu.roll(mid, width - 1, 1))


def dual_kernel_body(
    total_ref, ta_ref, tb_ref, own_ref, first_ref, second_ref, known_ref, last_ref,
    mix_ref, slope_ref, shift_ref, new_ref, send_ref, y_ref,
):
    y_ref[...] = jnp.zeros((80, 1024), F32)
    before, after = plane_sides(ta_ref, tb_ref, slice(0, 48))
    for start, v in ((0, before), (2, total_ref[...]), (4, after)):
        for k in range(3):
            for z in range(2):
                row = 24 + (start + z) * 3 + k
                for b in range(8):
                    i = k * 16 + z * 8 + b
                    y_ref[row : row + 1, b * 128 : (b + 1) * 128] = v[i : i + 1]
    spread_columns(y_ref, 1024)
    slope, shift = column(slope_ref, 32), column(shift_ref, 5)
    mix = joined(jnp.concatenate([mix_ref[...], jnp.zeros((3, 32), F32)], 0))
    h = dot3(last_ref[...], y_ref[...]) + known_ref[...]
    dual_rows = (
        plane_sides(first_ref, second_ref, slice(32, 40))[0],
        own_ref[8:16, :],
        own_ref[32:40, :],
        plane_sides(first_ref, second_ref, slice(8, 16))[1],
    )
    for z in range(4):
        g = h[z * 32 : (z + 1) * 32]
        g = jnp.where(g > 0, g, slope * g)
        out = dot3(mix, g) + shift + dual_rows[z]
        if z in (1, 2):
            for c in range(5):
                new_ref[c, z - 1] = out[c : c + 1, :]
        for b in range(8):
            piece = jnp.broadcast_to(out[0:1, b * 128 : (b + 1) * 128], (16, 128))
            send_ref[:, b, z, :] = piece


def back_kernel(
    pix_hbm, bin_hbm, cnt_hbm, nd_ref, wh_ref, wl_ref, new_ref,
    out_ref, first_ref, second_ref, new_hbm, tab_ref, acc_ref, pix_ref, bin_ref, cnt_ref, list_ref,
    sem,
):
    even = is_even("tile")
    copies = index_copies(pix_hbm, bin_hbm, cnt_hbm, pix_ref, bin_ref, cnt_ref, sem)
    for copy in copies:
        copy.start()
    out_copy = pltpu.make_async_copy(new_ref, new_hbm, sem.at[3])
    out_copy.start()
    for a in range(16):
        for b in range(8):
            v = nd_ref[a, b]
            hi = v.astype(BF16).astype(F32)
            tab_ref[a, b, 0:4] = hi
            tab_ref[a, b, 4:8] = v - hi
    acc_ref[...] = jnp.zeros_like(acc_ref)
    zero = jnp.zeros((8, 128), F32)
    for copy in copies:
        copy.wait()

    steps = list_pairs(cnt_ref, list_ref)

    def pair(i, a, k, count):
        slots = (k * 2, k * 2 + 1)
        one, two = (tab_ref[a, bin_ref[s, 0, a]] for s in slots)
        left = jnp.concatenate(
            [jnp.concatenate([one, zero], 1), jnp.concatenate([zero, two], 1)], 0
        ).astype(BF16)
        right = jnp.concatenate(
            [jnp.concatenate([w[i, 0:128, :], w[i, 128:256, :]], 1) for w in (wh_ref, wl_ref)], 0
        )
        d = lax.dot_general(left, right, (((1,), (1,)), ((), ())), preferred_element_type=F32)
        d = d[:, 0:128] + d[:, 128:256]
        for n, s in enumerate(slots):
            q = pix_ref[s, 0, a]
            acc_ref[q if count is None else jnp.where(s < count, q, 16)] += d[n * 8 : n * 8 + 8]

    def sure_step(c, carry):
        for j in range(4):
            for k in range(3):
                a = c * 4 + j
                pair(a * 3 + k, a, k, None)
        return carry

    def step(c, carry):
        for j in range(CHUNK):
            i = c * CHUNK + j
            pair(SURE + i, *pair_at(list_ref, cnt_ref, i))
        return carry

    lax.fori_loop(0, 4, sure_step, 0)
    lax.fori_loop(0, steps, step, 0)
    for q in range(16):
        v = acc_ref[q, 0:4] + acc_ref[q, 4:8]
        out_ref[q * 4 : q * 4 + 4, :] = v
    up, down = out_ref[0:16, :], out_ref[48:64, :]
    first_ref[...] = jnp.where(even, down, up)
    second_ref[...] = jnp.where(even, up, down)
    out_copy.wait()


def finish(g, mix, slope, shift):
    g = jnp.where(g > 0, g, slope * g)
    return dot3(mix, g) + shift


def primal_inner_kernel(
    sp_ref, sm_ref, first_ref, second_ref, back_ref, primal_ref, kern_ref, mix_ref,
    bias_ref, slope_ref, shift_ref, part_ref, rim_ref, out_hbm,
    tt_ref, lt_ref, lr_ref, x_ref, y_ref, out_ref, sem,
):
    p = lax.axis_index("plane")
    keeps = (p > 0, None, None, p < 7)
    before, after = plane_sides(first_ref, second_ref, slice(48, 64))
    for plane, v in enumerate((before, sm_ref[48:64, :], sp_ref[48:64, :], after)):
        for half in range(2):
            i = plane * 32 + half * 16
            x_ref[i : i + 16, :] = v[:, half * 512 : (half + 1) * 512]
    y_ref[...] = jnp.zeros((80, 512), F32)
    for plane in range(4):
        for row in range(1, 5):
            for col in range(4):
                i = (row * 4 - 4 + col) * 4 + plane
                v = back_ref[i : i + 1, :]
                if keeps[plane] is not None:
                    v = jnp.where(keeps[plane], v, 0.0)
                i = 24 + plane * 6 + row
                y_ref[i : i + 1, col * 128 : (col + 1) * 128] = v
    spread_columns(y_ref, 512)
    tt_ref[...] = jnp.zeros((96, 384), F32)
    lt_ref[...] = jnp.zeros((80, 256), F32)
    lr_ref[...] = jnp.zeros((32, 128), F32)
    for dz in range(3):
        for dr in range(3):
            block = jnp.concatenate(
                [
                    jnp.concatenate([kern_ref[c, dz, dr, db : db + 1, :] for db in range(3)], 1)
                    for c in range(5)
                ],
                0,
            )
            for r in range(4):
                i = dz * 32 + (r + dr) * 5
                tt_ref[i : i + 5, r * 96 : (r + 1) * 96] = block
            for db in range(3):
                four = jnp.concatenate([kern_ref[5, dz, dr, db : db + 1, :]] * 4, 1)
                for z in range(2):
                    for r in range(4):
                        i = db * 24 + (z + dz) * 6 + r + dr
                        lane = z * 128 + r * 32
                        lt_ref[i : i + 1, lane : lane + 32] = four[:, r * 32 : (r + 1) * 32]
                    if dr != 1:
                        i = db * 8 + (z + dz) * 2 + dr // 2
                        k = z * 2 + dr // 2
                        lr_ref[i : i + 1, k * 32 : (k + 1) * 32] = four[:, k * 32 : (k + 1) * 32]
    rim_ref[...] = joined(lr_ref[...].T)
    tt = joined(tt_ref[...].T)
    bias, slope, shift = column(bias_ref, 32), column(slope_ref, 32), column(shift_ref, 5)
    mix = joined(jnp.concatenate([mix_ref[...], jnp.zeros((3, 32), F32)], 0))
    own = dot3(joined(lt_ref[...].T), y_ref[...])
    for z in range(2):
        h = dot3(tt, x_ref[z * 32 : z * 32 + 96])
        for r in range(4):
            g = shifted_sum([h[r * 96 + i * 32 : r * 96 + (i + 1) * 32] for i in range(3)]) + bias
            i = (z * 4 + r) * 32
            g = g + own[i : i + 32]
            if r in (0, 3):
                i = (z * 2 + r // 3) * 32
                part_ref[i : i + 32, :] = g
            else:
                out = finish(g, mix, slope, shift)
                for c in range(5):
                    out_ref[c, z, r - 1 : r, :] = out[c : c + 1] + primal_ref[c, z, r : r + 1, :]
    copy = pltpu.make_async_copy(out_ref, out_hbm.at[:, :, 1:3, :], sem)
    copy.start()
    copy.wait()


def primal_outer_kernel(
    first_ref, second_ref, part_ref, rim_ref, primal_ref, mix_ref, slope_ref, shift_ref,
    inner_hbm, out_hbm, y_ref, out_ref, sem,
):
    del inner_hbm
    p = lax.axis_index("plane")
    t = lax.axis_index("tile")
    keeps = (p > 0, None, None, p < 7)
    even = is_even("tile")
    first, second = first_ref[...], second_ref[...]
    above = jnp.where(t > 0, jnp.where(even, second, first), 0.0)
    below = jnp.where(t < 15, jnp.where(even, first, second), 0.0)
    for plane in range(4):
        for rim, src in enumerate((above, below)):
            for col in range(4):
                i = col * 4 + plane
                v = src[i : i + 1]
                if keeps[plane] is not None:
                    v = jnp.where(keeps[plane], v, 0.0)
                i = 8 + plane * 2 + rim
                y_ref[i : i + 1, col * 128 : (col + 1) * 128] = v
    mid = y_ref[8:16, :]
    lane = lax.broadcasted_iota(jnp.int32, mid.shape, 1)
    y_ref[0:8, :] = jnp.where(lane == 0, 0.0, pltpu.roll(mid, 1, 1))
    y_ref[16:24, :] = jnp.where(lane == 511, 0.0, pltpu.roll(mid, 511, 1))
    y_ref[24:32, :] = jnp.zeros((8, 512), F32)
    slope, shift = column(slope_ref, 32), column(shift_ref, 5)
    mix = joined(jnp.concatenate([mix_ref[...], jnp.zeros((3, 32), F32)], 0))
    h = dot3(rim_ref[...], y_ref[...]) + part_ref[...]
    copies = []
    for rim, row in enumerate((0, 3)):
        for z in range(2):
            i = (z * 2 + rim) * 32
            out = finish(h[i : i + 32], mix, slope, shift)
            for c in range(5):
                out_ref[rim, c, z] = out[c : c + 1] + primal_ref[c, z, row : row + 1, :]
        copies.append(
            pltpu.make_async_copy(
                out_ref.at[rim], out_hbm.at[:, :, row : row + 1, :], sem.at[rim]
            )
        )
        copies[-1].start()
    for copy in copies:
        copy.wait()


def call(body, outs, in_specs, scratch=(), limit=8 << 20):
    return pl.pallas_call(
        body,
        out_shape=tuple(jax.ShapeDtypeStruct(s[0], s[1]) for s in outs),
        in_specs=in_specs,
        out_specs=tuple(VMEM for _ in outs),
        scratch_shapes=list(scratch),
        compiler_params=pltpu.CompilerParams(vmem_limit_bytes=limit),
    )


def swaps(first, second, axis):
    count = lax.axis_size(axis)
    a = lax.ppermute(first, axis, [(i, i ^ 1) for i in range(count)])
    pairs = [(i, (i - 1 if i % 2 == 0 else i + 1) % count) for i in range(count)]
    b = lax.ppermute(second, axis, pairs)
    return a, b


def per_device(
    primal, dual, measured, footprint_weights, pixel_index, bin_index, slot_count,
    dual_kernel, dual_bias, dual_slope, dual_mixing, dual_shift,
    primal_kernel, primal_bias, primal_slope, primal_mixing, primal_shift,
):
    pix = jnp.transpose(pixel_index, (2, 0, 1))
    bins = jnp.transpose(bin_index, (2, 0, 1))
    hbm = lambda x: pltpu.with_memory_space_constraint(x, pltpu.HBM)

    own = call(
        pack_kernel, [((32, 1024), F32)], [HBM] * 3,
        [
            pltpu.VMEM((5, 2, 1, 1024), F32),
            pltpu.VMEM((2, 1, 1024), F32),
            pltpu.VMEM((5, 2, 4, 512), F32),
            pltpu.SemaphoreType.DMA((3,)),
        ],
    )(hbm(dual), hbm(measured), hbm(primal))[0]
    pairs = footprint_weights.reshape(16, 6, 256, 128)

    near = swaps(own, own, "tile")

    terms, w_hi, w_lo = pl.pallas_call(
        project_kernel,
        name="project",
        out_shape=(
            jax.ShapeDtypeStruct((16, 3, 16, 128), F32),
            jax.ShapeDtypeStruct((ROOM, 256, 128), BF16),
            jax.ShapeDtypeStruct((ROOM, 256, 128), BF16),
        ),
        in_specs=[HBM] * 5 + [VMEM],
        out_specs=(VMEM, VMEM, VMEM),
        scratch_shapes=[pltpu.VMEM((16, 16, 128), F32)]
        + [pltpu.VMEM((16, 16, 128), BF16)] * 3
        + [
            pltpu.SMEM((12, 1, 16), jnp.int32),
            pltpu.SMEM((12, 1, 16), jnp.int32),
            pltpu.SMEM((1, 16), jnp.int32),
            pltpu.SMEM((128,), jnp.int32),
            pltpu.VMEM((2, 4, 512), F32),
            pltpu.VMEM((ROOM, 256, 128), F32),
            pltpu.SemaphoreType.DMA((4,)),
            pltpu.SemaphoreType.DMA((16,)),
            pltpu.SemaphoreType.DMA((ROOM - SURE,)),
        ],
        compiler_params=pltpu.CompilerParams(vmem_limit_bytes=18 << 20),
        cost_estimate=pl.CostEstimate(flops=1 << 31, bytes_accessed=25 << 20, transcendentals=0),
    )(hbm(pix), hbm(bins), hbm(slot_count), hbm(primal), hbm(pairs), own)
    terms, near = lax.optimization_barrier((terms, near))
    sp, sm, side_a, side_b = call(
        rims_kernel, [((64, 1024), F32)] * 4, [VMEM] * 4
    )(own, *near, primal)
    sides = swaps(side_a, side_b, "plane")
    got = lax.all_to_all(terms, "tile", 0, 0, tiled=True)
    total = call(total_kernel, [((48, 128), F32)], [VMEM])(got)[0]
    rows = swaps(total, total, "plane")

    known, last = call(
        dual_known_kernel, [((128, 1024), F32), ((128, 240), BF16)],
        [VMEM] * 4 + [SMEM],
        [pltpu.VMEM((80, 96), F32), pltpu.VMEM((80, 128), F32)],
    )(sp, *sides, jnp.transpose(dual_kernel, (2, 3, 4, 1, 0)), dual_bias)

    new_rows, send = call(
        dual_kernel_body, [((5, 2, 1, 1024), F32), ((16, 8, 4, 128), F32)],
        [VMEM] * 9 + [SMEM] * 2, [pltpu.VMEM((80, 1024), F32)],
    )(
        total, *rows, sp, *sides, known, last, dual_mixing,
        dual_slope, dual_shift,
    )
    leading = lax.all_to_all(send, "tile", 0, 0, tiled=True)

    back, edge_a, edge_b, new_dual = pl.pallas_call(
        back_kernel,
        name="back",
        out_shape=(
            jax.ShapeDtypeStruct((64, 128), F32),
            jax.ShapeDtypeStruct((16, 128), F32),
            jax.ShapeDtypeStruct((16, 128), F32),
            jax.ShapeDtypeStruct((5, 2, 1, 1024), F32),
        ),
        in_specs=[HBM, HBM, HBM, VMEM, VMEM, VMEM, VMEM],
        out_specs=(VMEM, VMEM, VMEM, HBM),
        scratch_shapes=[
            pltpu.VMEM((16, 8, 8, 128), F32),
            pltpu.VMEM((17, 8, 128), F32),
            pltpu.SMEM((12, 1, 16), jnp.int32),
            pltpu.SMEM((12, 1, 16), jnp.int32),
            pltpu.SMEM((1, 16), jnp.int32),
            pltpu.SMEM((128,), jnp.int32),
            pltpu.SemaphoreType.DMA((4,)),
        ],
        compiler_params=pltpu.CompilerParams(vmem_limit_bytes=4 << 20),
    )(
        hbm(pix), hbm(bins), hbm(slot_count), leading, w_hi, w_lo, new_rows,
    )
    edges = swaps(edge_a, edge_b, "tile")

    part, rim, inner = pl.pallas_call(
        primal_inner_kernel,
        name="primal_inner",
        out_shape=(
            jax.ShapeDtypeStruct((128, 512), F32),
            jax.ShapeDtypeStruct((128, 96), BF16),
            jax.ShapeDtypeStruct((5, 2, 4, 512), F32),
        ),
        in_specs=[VMEM] * 8 + [SMEM] * 3,
        out_specs=(VMEM, VMEM, HBM),
        scratch_shapes=[
            pltpu.VMEM((96, 384), F32),
            pltpu.VMEM((80, 256), F32),
            pltpu.VMEM((32, 128), F32),
            pltpu.VMEM((128, 512), F32),
            pltpu.VMEM((80, 512), F32),
            pltpu.VMEM((5, 2, 2, 512), F32),
            pltpu.SemaphoreType.DMA,
        ],
        compiler_params=pltpu.CompilerParams(vmem_limit_bytes=8 << 20),
    )(
        sp, sm, *sides, back, primal, jnp.transpose(primal_kernel, (1, 2, 3, 4, 0)),
        primal_mixing, primal_bias, primal_slope, primal_shift,
    )

    new_primal = pl.pallas_call(
        primal_outer_kernel,
        name="primal_outer",
        out_shape=jax.ShapeDtypeStruct((5, 2, 4, 512), F32),
        in_specs=[VMEM] * 6 + [SMEM] * 2 + [HBM],
        out_specs=HBM,
        scratch_shapes=[
            pltpu.VMEM((32, 512), F32),
            pltpu.VMEM((2, 5, 2, 1, 512), F32),
            pltpu.SemaphoreType.DMA((2,)),
        ],
        input_output_aliases={8: 0},
        compiler_params=pltpu.CompilerParams(vmem_limit_bytes=8 << 20),
    )(
        *edges, part, rim, primal, primal_mixing, primal_slope, primal_shift, hbm(inner),
    )
    return new_primal, new_dual


def solution(mesh):
    grid = P(None, "plane", "tile", None)
    in_specs = (
        grid, grid, P("plane", "tile", None), P("tile", None, None, None, None),
        P("tile", None, None), P(), P("tile", None),
    ) + (P(),) * 10
    return jax.shard_map(
        per_device, mesh=mesh, in_specs=in_specs, out_specs=(grid, grid), check_vma=False
    )
```

```python
import jax
import jax.numpy as jnp
from jax import lax
from jax.experimental import pallas as pl
from jax.experimental.pallas import tpu as pltpu
from jax.sharding import PartitionSpec as P


F32 = jnp.float32
BF16 = jnp.bfloat16
VMEM = pl.BlockSpec(memory_space=pltpu.VMEM)
SMEM = pl.BlockSpec(memory_space=pltpu.SMEM)
HBM = pl.BlockSpec(memory_space=pltpu.HBM)


def split(x):
    hi = x.astype(BF16)
    return hi, (x - hi.astype(F32)).astype(BF16)


def is_even(axis):
    return (lax.axis_index(axis) & 1) == 0


def joined(a):
    hi, lo = split(a)
    return jnp.concatenate([hi, lo, hi], 1)


def dot3(left, b):
    hi, lo = split(b)
    return jnp.dot(left, jnp.concatenate([hi, hi, lo], 0), preferred_element_type=F32)


def column(ref, count):
    rows = -(-count // 8) * 8
    index = lax.broadcasted_iota(jnp.int32, (rows, 128), 0)
    out = jnp.zeros((rows, 128), F32)
    for i in range(count):
        out = jnp.where(index == i, ref[i], out)
    return out


def tail_weights(mix_ref, slope_ref, shift_ref, cols_ref, mix_out_ref):
    cols_ref[0:32, :] = column(slope_ref, 32)
    cols_ref[32:40, :] = column(shift_ref, 5)
    mix_out_ref[...] = joined(jnp.concatenate([mix_ref[...], jnp.zeros((3, 32), F32)], 0))


def shifted_sum(stack):
    left, mid, right = stack
    width = mid.shape[1]
    lane = lax.broadcasted_iota(jnp.int32, mid.shape, 1)
    left = jnp.where(lane == 0, 0.0, pltpu.roll(left, 1, 1))
    right = jnp.where(lane == width - 1, 0.0, pltpu.roll(right, width - 1, 1))
    return left + mid + right


CHUNK = 8
ROOM = 96 + CHUNK
SURE = 48


def pack_kernel(dual_hbm, measured_hbm, primal_hbm, out_ref, dual_ref, measured_ref, primal_ref, sem):
    copies = [
        pltpu.make_async_copy(src, dst, sem.at[i])
        for i, (src, dst) in enumerate(
            ((dual_hbm, dual_ref), (measured_hbm, measured_ref), (primal_hbm, primal_ref))
        )
    ]
    for copy in copies:
        copy.start()
    for copy in copies:
        copy.wait()
    zero = jnp.zeros((1, 1024), F32)
    for z in range(2):
        for c in range(5):
            out_ref[z * 8 + c : z * 8 + c + 1, :] = dual_ref[c, z]
        out_ref[z * 8 + 5 : z * 8 + 6, :] = zero
        out_ref[z * 8 + 6 : z * 8 + 7, :] = measured_ref[z]
        out_ref[z * 8 + 7 : z * 8 + 8, :] = zero
    for k, row in enumerate((0, 3)):
        for c in range(5):
            for z in range(2):
                i = 16 + k * 5 + c
                out_ref[i : i + 1, z * 512 : (z + 1) * 512] = primal_ref[c, z, row : row + 1, :]
    out_ref[26:32, :] = jnp.zeros((6, 1024), F32)


def index_copies(pix_hbm, bin_hbm, cnt_hbm, pix_ref, bin_ref, cnt_ref, sem):
    t = lax.axis_index("tile")
    return [
        pltpu.make_async_copy(pix_hbm, pix_ref, sem.at[0]),
        pltpu.make_async_copy(bin_hbm.at[:, pl.ds(t, 1), :], bin_ref, sem.at[1]),
        pltpu.make_async_copy(cnt_hbm, cnt_ref, sem.at[2]),
    ]


def list_pairs(cnt_ref, list_ref):
    base = 0
    for a in range(16):
        for k in range(3):
            list_ref[base + k] = a * 8 + 3 + k
        base = base + ((cnt_ref[0, a] - 5) >> 1)
    for k in range(CHUNK):
        list_ref[base + k] = 128 + 3
    return (base + CHUNK - 1) // CHUNK


def pair_at(list_ref, cnt_ref, i):
    code = list_ref[i]
    a, k = (code >> 3) & 15, code & 7
    return a, k, jnp.where(code < 128, cnt_ref[0, a], 0)


def project_kernel(
    pix_hbm, bin_hbm, cnt_hbm, primal_hbm, w_hbm, after_ref,
    out_ref, wh_ref, wl_ref,
    acc_ref, hi_ref, lo_ref, hot_ref, pix_ref, bin_ref, cnt_ref, list_ref, primal_ref, w_ref,
    sem, sure_sem, w_sem,
):
    del after_ref
    copies = index_copies(pix_hbm, bin_hbm, cnt_hbm, pix_ref, bin_ref, cnt_ref, sem)
    copies.append(pltpu.make_async_copy(primal_hbm.at[1], primal_ref, sem.at[3]))
    for copy in copies[::-1]:
        copy.start()

    def fetch_sure(a):
        return pltpu.make_async_copy(
            w_hbm.at[a, pl.ds(0, 3)], w_ref.at[pl.ds(a * 3, 3)], sure_sem.at[a]
        )

    def fetch(i):
        a, k, _ = pair_at(list_ref, cnt_ref, i)
        return pltpu.make_async_copy(w_hbm.at[a, k], w_ref.at[SURE + i], w_sem.at[i])

    for a in range(16):
        fetch_sure(a).start()
    copies[2].wait()
    steps = list_pairs(cnt_ref, list_ref)
    for c in range(6):

        @pl.when(c < steps)
        def _():
            for j in range(CHUNK):
                fetch(c * CHUNK + j).start()

    row = lax.broadcasted_iota(jnp.int32, (16, 128), 0)
    for b in range(9):
        hot_ref[b] = jnp.where((row & 7) == b, 1.0, 0.0).astype(BF16)
    copies[3].wait()
    for q in range(16):
        r, col = q // 4, (q % 4) * 128
        v = jnp.concatenate(
            [
                jnp.broadcast_to(primal_ref[z, r : r + 1, col : col + 128], (8, 128))
                for z in range(2)
            ],
            0,
        )
        hi_ref[q], lo_ref[q] = split(v)
    copies[0].wait()
    copies[1].wait()

    def operands(i, a, k, count):
        parts = []
        for s in (k * 2, k * 2 + 1):
            q, b = pix_ref[s, 0, a], bin_ref[s, 0, a]
            hot = hot_ref[b if count is None else jnp.where(s < count, b, 8)]
            parts.append(jnp.concatenate([hi_ref[q] * hot, lo_ref[q] * hot], 0))
        w_hi, w_lo = split(w_ref[i])
        wh_ref[i], wl_ref[i] = w_hi, w_lo
        return jnp.concatenate(parts, 1), jnp.concatenate([w_hi, w_lo], 1)

    def product(left, right):
        d = jnp.dot(left, right, preferred_element_type=F32)
        return d[0:16, 0:128] + (d[0:16, 128:256] + d[16:32, 0:128])

    def sure_step(c, carry):
        for j in range(4):
            fetch_sure(c * 4 + j).wait()
        for j in range(4):
            a = c * 4 + j
            lefts, rights = zip(*(operands(a * 3 + k, a, k, None) for k in range(3)))
            acc_ref[a] = product(jnp.concatenate(lefts, 1), jnp.concatenate(rights, 0))
        return carry

    def step(c, carry):
        for j in range(CHUNK):
            fetch(c * CHUNK + j).wait()
        for j in range(CHUNK):
            i = c * CHUNK + j
            a, k, count = pair_at(list_ref, cnt_ref, i)
            acc_ref[a] += product(*operands(SURE + i, a, k, count))
        return carry

    lax.fori_loop(0, 4, sure_step, 0)
    lax.fori_loop(0, steps, step, 0)
    zero = jnp.zeros((16, 128), F32)
    for a in range(16):
        for k in range(3):
            out_ref[a, k] = acc_ref[a + k - 1] if 0 <= a + k - 1 < 16 else zero


def rims_kernel(own_ref, first_ref, second_ref, primal_ref, sp_ref, sm_ref, a_ref, b_ref):
    t = lax.axis_index("tile")
    even, even_plane = is_even("tile"), is_even("plane")

    def left(rows, lanes):
        return jnp.where(even, second_ref[rows, lanes], first_ref[rows, lanes])

    def right(rows, lanes):
        return jnp.where(even, first_ref[rows, lanes], second_ref[rows, lanes])

    every = slice(None)
    for z in range(2):
        rows = slice(z * 8, z * 8 + 8)
        blocks = (
            jnp.where(t > 0, left(rows, every), 0.0),
            own_ref[rows, :],
            jnp.where(t < 15, right(rows, every), 0.0),
        )
        for k, block in enumerate(blocks):
            base = z * 24 + k * 8
            for out in (sp_ref, sm_ref, a_ref, b_ref):
                out[base : base + 8, :] = block
    for z, out in ((0, sm_ref), (1, sp_ref)):
        half = slice(z * 512, (z + 1) * 512)
        for row in range(6):
            for c in range(5):
                if row == 0:
                    v = jnp.where(t > 0, left(slice(21 + c, 22 + c), half), 0.0)
                elif row == 5:
                    v = jnp.where(t < 15, right(slice(16 + c, 17 + c), half), 0.0)
                else:
                    v = primal_ref[c, z, row - 1 : row, :]
                i = row * 5 + c
                lane = (i // 16) * 512
                out[48 + i % 16 : 49 + i % 16, lane : lane + 512] = v
        out[62:64, 512:1024] = jnp.zeros((2, 512), F32)
    up, down = sp_ref[48:64, :], sm_ref[48:64, :]
    a_ref[48:64, :] = jnp.where(even_plane, up, down)
    b_ref[48:64, :] = jnp.where(even_plane, down, up)


def total_kernel(got_ref, out_ref):
    t = lax.axis_index("tile")
    for k, ok in enumerate((t > 0, None, t < 15)):
        total = got_ref[0, k]
        for i in range(1, 16):
            total = total + got_ref[i, k]
        if ok is not None:
            total = jnp.where(ok, total, 0.0)
        out_ref[k * 16 : k * 16 + 16, :] = total


def plane_sides(first_ref, second_ref, rows):
    p = lax.axis_index("plane")
    even = is_even("plane")
    first, second = first_ref[rows, :], second_ref[rows, :]
    before = jnp.where(p > 0, jnp.where(even, second, first), 0.0)
    return before, jnp.where(p < 7, jnp.where(even, first, second), 0.0)


def dual_inputs(own_ref, first_ref, second_ref):
    before, after = plane_sides(first_ref, second_ref, slice(0, 48))
    return jnp.concatenate(
        [
            before,
            own_ref[0:48, :],
            after,
            jnp.zeros((8, 1024), F32),
        ],
        0,
    )


def dual_known_kernel(
    own_ref, first_ref, second_ref, kern_ref, mix_ref, bias_ref, slope_ref, shift_ref,
    known_ref, last_ref, cols_ref, mix_out_ref, tt_ref, lt_ref,
):
    tail_weights(mix_ref, slope_ref, shift_ref, cols_ref, mix_out_ref)
    tt_ref[...] = jnp.zeros((80, 96), F32)
    lt_ref[...] = jnp.zeros((80, 128), F32)
    for dz in range(3):
        for da in range(3):
            tiles = [kern_ref[dz, da, db] for db in range(3)]
            base = dz * 24 + da * 8
            tt_ref[base : base + 7, :] = jnp.concatenate(tiles, 1)
            for db in range(3):
                four = jnp.concatenate([tiles[db][5:6]] * 4, 1)
                for z in range(4):
                    i = db * 24 + (z + dz) * 3 + da
                    lt_ref[i : i + 1, z * 32 : (z + 1) * 32] = four[:, z * 32 : (z + 1) * 32]
    last_ref[...] = joined(lt_ref[...].T)
    x = dual_inputs(own_ref, first_ref, second_ref)
    tt = joined(tt_ref[...].T)
    bias = column(bias_ref, 32)[:, 0:1]
    for z in range(4):
        h = dot3(tt, x[z * 24 : z * 24 + 80])
        h = shifted_sum([h[i * 32 : (i + 1) * 32] for i in range(3)]) + bias
        known_ref[z * 32 : (z + 1) * 32, :] = h


def spread_columns(y_ref, width):
    mid = y_ref[24:48, :]
    lane = lax.broadcasted_iota(jnp.int32, mid.shape, 1)
    y_ref[0:24, :] = jnp.where(lane == 0, 0.0, pltpu.roll(mid, 1, 1))
    y_ref[48:72, :] = jnp.where(lane == width - 1, 0.0, pltpu.roll(mid, width - 1, 1))


def dual_kernel_body(
    total_ref, ta_ref, tb_ref, own_ref, first_ref, second_ref, known_ref, last_ref,
    cols_ref, mix_ref, new_ref, send_ref, y_ref,
):
    y_ref[...] = jnp.zeros((80, 1024), F32)
    before, after = plane_sides(ta_ref, tb_ref, slice(0, 48))
    for start, v in ((0, before), (2, total_ref[...]), (4, after)):
        for k in range(3):
            for z in range(2):
                row = 24 + (start + z) * 3 + k
                for b in range(8):
                    i = k * 16 + z * 8 + b
                    y_ref[row : row + 1, b * 128 : (b + 1) * 128] = v[i : i + 1]
    spread_columns(y_ref, 1024)
    slope, shift, mix = cols_ref[0:32, 0:1], cols_ref[32:40, 0:1], mix_ref[...]
    h = dot3(last_ref[...], y_ref[...]) + known_ref[...]
    dual_rows = (
        plane_sides(first_ref, second_ref, slice(32, 40))[0],
        own_ref[8:16, :],
        own_ref[32:40, :],
        plane_sides(first_ref, second_ref, slice(8, 16))[1],
    )
    for z in range(4):
        g = h[z * 32 : (z + 1) * 32]
        g = jnp.where(g > 0, g, slope * g)
        out = dot3(mix, g) + shift + dual_rows[z]
        if z in (1, 2):
            for c in range(5):
                new_ref[c, z - 1] = out[c : c + 1, :]
        for b in range(8):
            piece = jnp.broadcast_to(out[0:1, b * 128 : (b + 1) * 128], (16, 128))
            send_ref[:, b, z, :] = piece


def back_kernel(
    pix_hbm, bin_hbm, cnt_hbm, nd_ref, wh_ref, wl_ref, new_ref,
    out_ref, first_ref, second_ref, new_hbm, tab_ref, acc_ref, pix_ref, bin_ref, cnt_ref, list_ref,
    sem,
):
    even = is_even("tile")
    copies = index_copies(pix_hbm, bin_hbm, cnt_hbm, pix_ref, bin_ref, cnt_ref, sem)
    for copy in copies:
        copy.start()
    out_copy = pltpu.make_async_copy(new_ref, new_hbm, sem.at[3])
    out_copy.start()
    for a in range(16):
        for b in range(8):
            v = nd_ref[a, b]
            hi = v.astype(BF16).astype(F32)
            tab_ref[a, b, 0:4] = hi
            tab_ref[a, b, 4:8] = v - hi
    acc_ref[...] = jnp.zeros_like(acc_ref)
    zero = jnp.zeros((8, 128), F32)
    for copy in copies:
        copy.wait()

    steps = list_pairs(cnt_ref, list_ref)

    def pair(i, a, k, count):
        slots = (k * 2, k * 2 + 1)
        one, two = (tab_ref[a, bin_ref[s, 0, a]] for s in slots)
        left = jnp.concatenate(
            [jnp.concatenate([one, zero], 1), jnp.concatenate([zero, two], 1)], 0
        ).astype(BF16)
        right = jnp.concatenate(
            [jnp.concatenate([w[i, 0:128, :], w[i, 128:256, :]], 1) for w in (wh_ref, wl_ref)], 0
        )
        d = lax.dot_general(left, right, (((1,), (1,)), ((), ())), preferred_element_type=F32)
        d = d[:, 0:128] + d[:, 128:256]
        for n, s in enumerate(slots):
            q = pix_ref[s, 0, a]
            acc_ref[q if count is None else jnp.where(s < count, q, 16)] += d[n * 8 : n * 8 + 8]

    def sure_step(c, carry):
        for j in range(4):
            for k in range(3):
                a = c * 4 + j
                pair(a * 3 + k, a, k, None)
        return carry

    def step(c, carry):
        for j in range(CHUNK):
            i = c * CHUNK + j
            pair(SURE + i, *pair_at(list_ref, cnt_ref, i))
        return carry

    lax.fori_loop(0, 4, sure_step, 0)
    lax.fori_loop(0, steps, step, 0)
    for q in range(16):
        v = acc_ref[q, 0:4] + acc_ref[q, 4:8]
        out_ref[q * 4 : q * 4 + 4, :] = v
    up, down = out_ref[0:16, :], out_ref[48:64, :]
    first_ref[...] = jnp.where(even, down, up)
    second_ref[...] = jnp.where(even, up, down)
    out_copy.wait()


def finish(g, mix, slope, shift):
    g = jnp.where(g > 0, g, slope * g)
    return dot3(mix, g) + shift


def primal_inner_kernel(
    sp_ref, sm_ref, first_ref, second_ref, back_ref, primal_ref, kern_ref, mix_ref,
    bias_ref, slope_ref, shift_ref, part_ref, rim_ref, out_ref, cols_ref, mix_out_ref,
    tt_ref, lt_ref, lr_ref, x_ref, y_ref,
):
    p = lax.axis_index("plane")
    keeps = (p > 0, None, None, p < 7)
    before, after = plane_sides(first_ref, second_ref, slice(48, 64))
    for plane, v in enumerate((before, sm_ref[48:64, :], sp_ref[48:64, :], after)):
        for half in range(2):
            i = plane * 32 + half * 16
            x_ref[i : i + 16, :] = v[:, half * 512 : (half + 1) * 512]
    y_ref[...] = jnp.zeros((80, 512), F32)
    for plane in range(4):
        for row in range(1, 5):
            for col in range(4):
                i = (row * 4 - 4 + col) * 4 + plane
                v = back_ref[i : i + 1, :]
                if keeps[plane] is not None:
                    v = jnp.where(keeps[plane], v, 0.0)
                i = 24 + plane * 6 + row
                y_ref[i : i + 1, col * 128 : (col + 1) * 128] = v
    spread_columns(y_ref, 512)
    tt_ref[...] = jnp.zeros((96, 384), F32)
    lt_ref[...] = jnp.zeros((80, 256), F32)
    lr_ref[...] = jnp.zeros((32, 128), F32)
    for dz in range(3):
        for dr in range(3):
            block = jnp.concatenate(
                [
                    jnp.concatenate([kern_ref[c, dz, dr, db : db + 1, :] for db in range(3)], 1)
                    for c in range(5)
                ],
                0,
            )
            for r in range(4):
                i = dz * 32 + (r + dr) * 5
                tt_ref[i : i + 5, r * 96 : (r + 1) * 96] = block
            for db in range(3):
                four = jnp.concatenate([kern_ref[5, dz, dr, db : db + 1, :]] * 4, 1)
                for z in range(2):
                    for r in range(4):
                        i = db * 24 + (z + dz) * 6 + r + dr
                        lane = z * 128 + r * 32
                        lt_ref[i : i + 1, lane : lane + 32] = four[:, r * 32 : (r + 1) * 32]
                    if dr != 1:
                        i = db * 8 + (z + dz) * 2 + dr // 2
                        k = z * 2 + dr // 2
                        lr_ref[i : i + 1, k * 32 : (k + 1) * 32] = four[:, k * 32 : (k + 1) * 32]
    rim_ref[...] = joined(lr_ref[...].T)
    tt = joined(tt_ref[...].T)
    tail_weights(mix_ref, slope_ref, shift_ref, cols_ref, mix_out_ref)
    bias = column(bias_ref, 32)[:, 0:1]
    slope, shift, mix = cols_ref[0:32, 0:1], cols_ref[32:40, 0:1], mix_out_ref[...]
    own = dot3(joined(lt_ref[...].T), y_ref[...])
    for z in range(2):
        h = dot3(tt, x_ref[z * 32 : z * 32 + 96])
        for r in range(4):
            g = shifted_sum([h[r * 96 + i * 32 : r * 96 + (i + 1) * 32] for i in range(3)]) + bias
            i = (z * 4 + r) * 32
            g = g + own[i : i + 32]
            if r in (0, 3):
                i = (z * 2 + r // 3) * 32
                part_ref[i : i + 32, :] = g
            else:
                out = finish(g, mix, slope, shift)
                for c in range(5):
                    out_ref[c, z, r : r + 1, :] = out[c : c + 1] + primal_ref[c, z, r : r + 1, :]
    for z in range(2):
        for c in range(5):
            for r in (0, 3):
                out_ref[c, z, r : r + 1, :] = primal_ref[c, z, r : r + 1, :]


def primal_outer_kernel(
    first_ref, second_ref, part_ref, rim_ref, inner_ref, cols_ref, mix_ref,
    out_hbm, y_ref, out_ref, sem,
):
    out_ref[...] = inner_ref[...]
    p = lax.axis_index("plane")
    t = lax.axis_index("tile")
    keeps = (p > 0, None, None, p < 7)
    even = is_even("tile")
    first, second = first_ref[...], second_ref[...]
    above = jnp.where(t > 0, jnp.where(even, second, first), 0.0)
    below = jnp.where(t < 15, jnp.where(even, first, second), 0.0)
    for plane in range(4):
        for rim, src in enumerate((above, below)):
            for col in range(4):
                i = col * 4 + plane
                v = src[i : i + 1]
                if keeps[plane] is not None:
                    v = jnp.where(keeps[plane], v, 0.0)
                i = 8 + plane * 2 + rim
                y_ref[i : i + 1, col * 128 : (col + 1) * 128] = v
    mid = y_ref[8:16, :]
    lane = lax.broadcasted_iota(jnp.int32, mid.shape, 1)
    y_ref[0:8, :] = jnp.where(lane == 0, 0.0, pltpu.roll(mid, 1, 1))
    y_ref[16:24, :] = jnp.where(lane == 511, 0.0, pltpu.roll(mid, 511, 1))
    y_ref[24:32, :] = jnp.zeros((8, 512), F32)
    slope, shift, mix = cols_ref[0:32, 0:1], cols_ref[32:40, 0:1], mix_ref[...]
    h = dot3(rim_ref[...], y_ref[...]) + part_ref[...]
    copies = []
    for z in range(2):
        for rim, row in enumerate((0, 3)):
            i = (z * 2 + rim) * 32
            out = finish(h[i : i + 32], mix, slope, shift)
            for c in range(5):
                out_ref[c, z, row : row + 1, :] += out[c : c + 1]
        copies.append(pltpu.make_async_copy(out_ref.at[:, z], out_hbm.at[:, z], sem.at[z]))
        copies[-1].start()
    for copy in copies:
        copy.wait()


def call(body, outs, in_specs, scratch=(), limit=8 << 20):
    return pl.pallas_call(
        body,
        out_shape=tuple(jax.ShapeDtypeStruct(s[0], s[1]) for s in outs),
        in_specs=in_specs,
        out_specs=tuple(VMEM for _ in outs),
        scratch_shapes=list(scratch),
        compiler_params=pltpu.CompilerParams(vmem_limit_bytes=limit),
    )


def swaps(first, second, axis):
    count = lax.axis_size(axis)
    a = lax.ppermute(first, axis, [(i, i ^ 1) for i in range(count)])
    pairs = [(i, (i - 1 if i % 2 == 0 else i + 1) % count) for i in range(count)]
    b = lax.ppermute(second, axis, pairs)
    return a, b


def per_device(
    primal, dual, measured, footprint_weights, pixel_index, bin_index, slot_count,
    dual_kernel, dual_bias, dual_slope, dual_mixing, dual_shift,
    primal_kernel, primal_bias, primal_slope, primal_mixing, primal_shift,
):
    pix = jnp.transpose(pixel_index, (2, 0, 1))
    bins = jnp.transpose(bin_index, (2, 0, 1))
    hbm = lambda x: pltpu.with_memory_space_constraint(x, pltpu.HBM)

    own = call(
        pack_kernel, [((32, 1024), F32)], [HBM] * 3,
        [
            pltpu.VMEM((5, 2, 1, 1024), F32),
            pltpu.VMEM((2, 1, 1024), F32),
            pltpu.VMEM((5, 2, 4, 512), F32),
            pltpu.SemaphoreType.DMA((3,)),
        ],
    )(hbm(dual), hbm(measured), hbm(primal))[0]
    pairs = footprint_weights.reshape(16, 6, 256, 128)

    near = swaps(own, own, "tile")

    terms, w_hi, w_lo = pl.pallas_call(
        project_kernel,
        name="project",
        out_shape=(
            jax.ShapeDtypeStruct((16, 3, 16, 128), F32),
            jax.ShapeDtypeStruct((ROOM, 256, 128), BF16),
            jax.ShapeDtypeStruct((ROOM, 256, 128), BF16),
        ),
        in_specs=[HBM] * 5 + [VMEM],
        out_specs=(VMEM, VMEM, VMEM),
        scratch_shapes=[pltpu.VMEM((16, 16, 128), F32)]
        + [pltpu.VMEM((16, 16, 128), BF16)] * 3
        + [
            pltpu.SMEM((12, 1, 16), jnp.int32),
            pltpu.SMEM((12, 1, 16), jnp.int32),
            pltpu.SMEM((1, 16), jnp.int32),
            pltpu.SMEM((128,), jnp.int32),
            pltpu.VMEM((2, 4, 512), F32),
            pltpu.VMEM((ROOM, 256, 128), F32),
            pltpu.SemaphoreType.DMA((4,)),
            pltpu.SemaphoreType.DMA((16,)),
            pltpu.SemaphoreType.DMA((ROOM - SURE,)),
        ],
        compiler_params=pltpu.CompilerParams(vmem_limit_bytes=18 << 20),
        cost_estimate=pl.CostEstimate(flops=1 << 31, bytes_accessed=25 << 20, transcendentals=0),
    )(hbm(pix), hbm(bins), hbm(slot_count), hbm(primal), hbm(pairs), own)
    terms, near = lax.optimization_barrier((terms, near))
    sp, sm, side_a, side_b = call(
        rims_kernel, [((64, 1024), F32)] * 4, [VMEM] * 4
    )(own, *near, primal)
    sides = swaps(side_a, side_b, "plane")
    got = lax.all_to_all(terms, "tile", 0, 0, tiled=True)
    total = call(total_kernel, [((48, 128), F32)], [VMEM])(got)[0]
    rows = swaps(total, total, "plane")

    known, last, cols, mix = call(
        dual_known_kernel,
        [((128, 1024), F32), ((128, 240), BF16), ((40, 128), F32), ((8, 96), BF16)],
        [VMEM] * 5 + [SMEM] * 3,
        [pltpu.VMEM((80, 96), F32), pltpu.VMEM((80, 128), F32)],
    )(
        sp, *sides, jnp.transpose(dual_kernel, (2, 3, 4, 1, 0)), dual_mixing,
        dual_bias, dual_slope, dual_shift,
    )

    new_rows, send = call(
        dual_kernel_body, [((5, 2, 1, 1024), F32), ((16, 8, 4, 128), F32)],
        [VMEM] * 10, [pltpu.VMEM((80, 1024), F32)],
    )(
        total, *rows, sp, *sides, known, last, cols, mix,
    )
    leading = lax.all_to_all(send, "tile", 0, 0, tiled=True)

    back, edge_a, edge_b, new_dual = pl.pallas_call(
        back_kernel,
        name="back",
        out_shape=(
            jax.ShapeDtypeStruct((64, 128), F32),
            jax.ShapeDtypeStruct((16, 128), F32),
            jax.ShapeDtypeStruct((16, 128), F32),
            jax.ShapeDtypeStruct((5, 2, 1, 1024), F32),
        ),
        in_specs=[HBM, HBM, HBM, VMEM, VMEM, VMEM, VMEM],
        out_specs=(VMEM, VMEM, VMEM, HBM),
        scratch_shapes=[
            pltpu.VMEM((16, 8, 8, 128), F32),
            pltpu.VMEM((17, 8, 128), F32),
            pltpu.SMEM((12, 1, 16), jnp.int32),
            pltpu.SMEM((12, 1, 16), jnp.int32),
            pltpu.SMEM((1, 16), jnp.int32),
            pltpu.SMEM((128,), jnp.int32),
            pltpu.SemaphoreType.DMA((4,)),
        ],
        compiler_params=pltpu.CompilerParams(vmem_limit_bytes=4 << 20),
    )(
        hbm(pix), hbm(bins), hbm(slot_count), leading, w_hi, w_lo, new_rows,
    )
    edges = swaps(edge_a, edge_b, "tile")

    part, rim, inner, cols, mix = pl.pallas_call(
        primal_inner_kernel,
        name="primal_inner",
        out_shape=(
            jax.ShapeDtypeStruct((128, 512), F32),
            jax.ShapeDtypeStruct((128, 96), BF16),
            jax.ShapeDtypeStruct((5, 2, 4, 512), F32),
            jax.ShapeDtypeStruct((40, 128), F32),
            jax.ShapeDtypeStruct((8, 96), BF16),
        ),
        in_specs=[VMEM] * 8 + [SMEM] * 3,
        out_specs=(VMEM,) * 5,
        scratch_shapes=[
            pltpu.VMEM((96, 384), F32),
            pltpu.VMEM((80, 256), F32),
            pltpu.VMEM((32, 128), F32),
            pltpu.VMEM((128, 512), F32),
            pltpu.VMEM((80, 512), F32),
        ],
        compiler_params=pltpu.CompilerParams(vmem_limit_bytes=8 << 20),
    )(
        sp, sm, *sides, back, primal, jnp.transpose(primal_kernel, (1, 2, 3, 4, 0)),
        primal_mixing, primal_bias, primal_slope, primal_shift,
    )

    new_primal = pl.pallas_call(
        primal_outer_kernel,
        name="primal_outer",
        out_shape=jax.ShapeDtypeStruct((5, 2, 4, 512), F32),
        in_specs=[VMEM] * 7,
        out_specs=HBM,
        scratch_shapes=[
            pltpu.VMEM((32, 512), F32),
            pltpu.VMEM((5, 2, 4, 512), F32),
            pltpu.SemaphoreType.DMA((2,)),
        ],
        compiler_params=pltpu.CompilerParams(vmem_limit_bytes=8 << 20),
    )(
        *edges, part, rim, inner, cols, mix,
    )
    return new_primal, new_dual


def solution(mesh):
    grid = P(None, "plane", "tile", None)
    in_specs = (
        grid, grid, P("plane", "tile", None), P("tile", None, None, None, None),
        P("tile", None, None), P(), P("tile", None),
    ) + (P(),) * 10
    return jax.shard_map(
        per_device, mesh=mesh, in_specs=in_specs, out_specs=(grid, grid), check_vma=False
    )
```

```python
import jax
import jax.numpy as jnp
from jax import lax
from jax.experimental import pallas as pl
from jax.experimental.pallas import tpu as pltpu
from jax.sharding import PartitionSpec as P


F32 = jnp.float32
BF16 = jnp.bfloat16
VMEM = pl.BlockSpec(memory_space=pltpu.VMEM)
HBM = pl.BlockSpec(memory_space=pltpu.HBM)


def split(x):
    hi = x.astype(BF16)
    return hi, (x - hi.astype(F32)).astype(BF16)


def is_even(axis):
    return (lax.axis_index(axis) & 1) == 0


def joined(a):
    hi, lo = split(a)
    return jnp.concatenate([hi, lo, hi], 1)


def dot3(left, b):
    hi, lo = split(b)
    return jnp.dot(left, jnp.concatenate([hi, hi, lo], 0), preferred_element_type=F32)


def tail_weights(mix_ref, bias_ref, slope_ref, shift_ref, cols_ref, mix_out_ref, vec_ref):
    vec_ref[...] = jnp.zeros((8, 128), F32)
    vec_ref[0:1, 0:32] = bias_ref[...]
    vec_ref[1:2, 0:32] = slope_ref[...]
    vec_ref[2:3, 0:5] = shift_ref[...]
    columns = vec_ref[...].T
    cols_ref[0:32, :] = jnp.broadcast_to(columns[0:32, 1:2], (32, 128))
    cols_ref[32:40, :] = jnp.broadcast_to(columns[0:8, 2:3], (8, 128))
    mix_out_ref[...] = joined(jnp.concatenate([mix_ref[...], jnp.zeros((3, 32), F32)], 0))
    return columns[0:32, 0:1]


def shifted_sum(stack):
    left, mid, right = stack
    width = mid.shape[1]
    lane = lax.broadcasted_iota(jnp.int32, mid.shape, 1)
    left = jnp.where(lane == 0, 0.0, pltpu.roll(left, 1, 1))
    right = jnp.where(lane == width - 1, 0.0, pltpu.roll(right, width - 1, 1))
    return left + mid + right


CHUNK = 8
ROOM = 96 + CHUNK
SURE = 48


def pack_kernel(dual_hbm, measured_hbm, primal_hbm, out_ref, dual_ref, measured_ref, primal_ref, sem):
    copies = [
        pltpu.make_async_copy(src, dst, sem.at[i])
        for i, (src, dst) in enumerate(
            ((dual_hbm, dual_ref), (measured_hbm, measured_ref), (primal_hbm, primal_ref))
        )
    ]
    for copy in copies:
        copy.start()
    for copy in copies:
        copy.wait()
    zero = jnp.zeros((1, 1024), F32)
    for z in range(2):
        for c in range(5):
            out_ref[z * 8 + c : z * 8 + c + 1, :] = dual_ref[c, z]
        out_ref[z * 8 + 5 : z * 8 + 6, :] = zero
        out_ref[z * 8 + 6 : z * 8 + 7, :] = measured_ref[z]
        out_ref[z * 8 + 7 : z * 8 + 8, :] = zero
    for k, row in enumerate((0, 3)):
        for c in range(5):
            for z in range(2):
                i = 16 + k * 5 + c
                out_ref[i : i + 1, z * 512 : (z + 1) * 512] = primal_ref[c, z, row : row + 1, :]
    out_ref[26:32, :] = jnp.zeros((6, 1024), F32)


def index_copies(pix_hbm, bin_hbm, cnt_hbm, pix_ref, bin_ref, cnt_ref, sem):
    t = lax.axis_index("tile")
    return [
        pltpu.make_async_copy(pix_hbm, pix_ref, sem.at[0]),
        pltpu.make_async_copy(bin_hbm.at[:, pl.ds(t, 1), :], bin_ref, sem.at[1]),
        pltpu.make_async_copy(cnt_hbm, cnt_ref, sem.at[2]),
    ]


def list_pairs(cnt_ref, list_ref):
    base = 0
    for a in range(16):
        for k in range(3):
            list_ref[base + k] = a * 8 + 3 + k
        base = base + ((cnt_ref[0, a] - 5) >> 1)
    for k in range(CHUNK):
        list_ref[base + k] = 128 + 3
    return (base + CHUNK - 1) // CHUNK


def pair_at(list_ref, cnt_ref, i):
    code = list_ref[i]
    a, k = (code >> 3) & 15, code & 7
    return a, k, jnp.where(code < 128, cnt_ref[0, a], 0)


def project_kernel(
    pix_hbm, bin_hbm, cnt_hbm, primal_hbm, w_hbm, after_ref,
    out_ref, wh_ref, wl_ref,
    acc_ref, hi_ref, lo_ref, hot_ref, pix_ref, bin_ref, cnt_ref, list_ref, primal_ref, w_ref,
    sem, sure_sem, w_sem,
):
    del after_ref
    copies = index_copies(pix_hbm, bin_hbm, cnt_hbm, pix_ref, bin_ref, cnt_ref, sem)
    copies.append(pltpu.make_async_copy(primal_hbm.at[1], primal_ref, sem.at[3]))
    for copy in copies[::-1]:
        copy.start()

    def fetch_sure(a):
        return pltpu.make_async_copy(
            w_hbm.at[a, pl.ds(0, 3)], w_ref.at[pl.ds(a * 3, 3)], sure_sem.at[a]
        )

    def fetch(i):
        a, k, _ = pair_at(list_ref, cnt_ref, i)
        return pltpu.make_async_copy(w_hbm.at[a, k], w_ref.at[SURE + i], w_sem.at[i])

    for a in range(16):
        fetch_sure(a).start()
    copies[2].wait()
    steps = list_pairs(cnt_ref, list_ref)
    for c in range(6):

        @pl.when(c < steps)
        def _():
            for j in range(CHUNK):
                fetch(c * CHUNK + j).start()

    row = lax.broadcasted_iota(jnp.int32, (16, 128), 0)
    for b in range(9):
        hot_ref[b] = jnp.where((row & 7) == b, 1.0, 0.0).astype(BF16)
    copies[3].wait()
    for q in range(16):
        r, col = q // 4, (q % 4) * 128
        v = jnp.concatenate(
            [
                jnp.broadcast_to(primal_ref[z, r : r + 1, col : col + 128], (8, 128))
                for z in range(2)
            ],
            0,
        )
        hi_ref[q], lo_ref[q] = split(v)
    copies[0].wait()
    copies[1].wait()

    def operands(i, a, k, count):
        parts = []
        for s in (k * 2, k * 2 + 1):
            q, b = pix_ref[s, 0, a], bin_ref[s, 0, a]
            hot = hot_ref[b if count is None else jnp.where(s < count, b, 8)]
            parts.append(jnp.concatenate([hi_ref[q] * hot, lo_ref[q] * hot], 0))
        w_hi, w_lo = split(w_ref[i])
        wh_ref[i], wl_ref[i] = w_hi, w_lo
        return jnp.concatenate(parts, 1), jnp.concatenate([w_hi, w_lo], 1)

    def product(left, right):
        d = jnp.dot(left, right, preferred_element_type=F32)
        return d[0:16, 0:128] + (d[0:16, 128:256] + d[16:32, 0:128])

    def sure_step(c, carry):
        for j in range(4):
            fetch_sure(c * 4 + j).wait()
        for j in range(4):
            a = c * 4 + j
            lefts, rights = zip(*(operands(a * 3 + k, a, k, None) for k in range(3)))
            acc_ref[a] = product(jnp.concatenate(lefts, 1), jnp.concatenate(rights, 0))
        return carry

    def step(c, carry):
        for j in range(CHUNK):
            fetch(c * CHUNK + j).wait()
        for j in range(CHUNK):
            i = c * CHUNK + j
            a, k, count = pair_at(list_ref, cnt_ref, i)
            acc_ref[a] += product(*operands(SURE + i, a, k, count))
        return carry

    lax.fori_loop(0, 4, sure_step, 0)
    lax.fori_loop(0, steps, step, 0)
    zero = jnp.zeros((16, 128), F32)
    for a in range(16):
        for k in range(3):
            out_ref[a, k] = acc_ref[a + k - 1] if 0 <= a + k - 1 < 16 else zero


def rims_kernel(own_ref, first_ref, second_ref, primal_ref, sp_ref, sm_ref, a_ref, b_ref):
    t = lax.axis_index("tile")
    even, even_plane = is_even("tile"), is_even("plane")

    def left(rows, lanes):
        return jnp.where(even, second_ref[rows, lanes], first_ref[rows, lanes])

    def right(rows, lanes):
        return jnp.where(even, first_ref[rows, lanes], second_ref[rows, lanes])

    every = slice(None)
    for z in range(2):
        rows = slice(z * 8, z * 8 + 8)
        blocks = (
            jnp.where(t > 0, left(rows, every), 0.0),
            own_ref[rows, :],
            jnp.where(t < 15, right(rows, every), 0.0),
        )
        for k, block in enumerate(blocks):
            base = z * 24 + k * 8
            for out in (sp_ref, sm_ref, a_ref, b_ref):
                out[base : base + 8, :] = block
    for z, out in ((0, sm_ref), (1, sp_ref)):
        half = slice(z * 512, (z + 1) * 512)
        for row in range(6):
            for c in range(5):
                if row == 0:
                    v = jnp.where(t > 0, left(slice(21 + c, 22 + c), half), 0.0)
                elif row == 5:
                    v = jnp.where(t < 15, right(slice(16 + c, 17 + c), half), 0.0)
                else:
                    v = primal_ref[c, z, row - 1 : row, :]
                i = row * 5 + c
                lane = (i // 16) * 512
                out[48 + i % 16 : 49 + i % 16, lane : lane + 512] = v
        out[62:64, 512:1024] = jnp.zeros((2, 512), F32)
    up, down = sp_ref[48:64, :], sm_ref[48:64, :]
    a_ref[48:64, :] = jnp.where(even_plane, up, down)
    b_ref[48:64, :] = jnp.where(even_plane, down, up)


def total_kernel(got_ref, out_ref):
    t = lax.axis_index("tile")
    for k, ok in enumerate((t > 0, None, t < 15)):
        total = got_ref[0, k]
        for i in range(1, 16):
            total = total + got_ref[i, k]
        if ok is not None:
            total = jnp.where(ok, total, 0.0)
        out_ref[k * 16 : k * 16 + 16, :] = total


def plane_sides(first_ref, second_ref, rows):
    p = lax.axis_index("plane")
    even = is_even("plane")
    first, second = first_ref[rows, :], second_ref[rows, :]
    before = jnp.where(p > 0, jnp.where(even, second, first), 0.0)
    return before, jnp.where(p < 7, jnp.where(even, first, second), 0.0)


def dual_inputs(own_ref, first_ref, second_ref):
    before, after = plane_sides(first_ref, second_ref, slice(0, 48))
    return jnp.concatenate(
        [
            before,
            own_ref[0:48, :],
            after,
            jnp.zeros((8, 1024), F32),
        ],
        0,
    )


def dual_known_kernel(
    own_ref, first_ref, second_ref, kern_ref, mix_ref, bias_ref, slope_ref, shift_ref,
    known_ref, last_ref, cols_ref, mix_out_ref, tt_ref, lt_ref, vec_ref,
):
    bias = tail_weights(
        mix_ref, bias_ref, slope_ref, shift_ref, cols_ref, mix_out_ref, vec_ref
    )
    tt_ref[...] = jnp.zeros((80, 96), F32)
    lt_ref[...] = jnp.zeros((80, 128), F32)
    for dz in range(3):
        for da in range(3):
            tiles = [kern_ref[dz, da, db] for db in range(3)]
            base = dz * 24 + da * 8
            tt_ref[base : base + 7, :] = jnp.concatenate(tiles, 1)
            for db in range(3):
                four = jnp.concatenate([tiles[db][5:6]] * 4, 1)
                for z in range(4):
                    i = db * 24 + (z + dz) * 3 + da
                    lt_ref[i : i + 1, z * 32 : (z + 1) * 32] = four[:, z * 32 : (z + 1) * 32]
    last_ref[...] = joined(lt_ref[...].T)
    x = dual_inputs(own_ref, first_ref, second_ref)
    tt = joined(tt_ref[...].T)
    for z in range(4):
        h = dot3(tt, x[z * 24 : z * 24 + 80])
        h = shifted_sum([h[i * 32 : (i + 1) * 32] for i in range(3)]) + bias
        known_ref[z * 32 : (z + 1) * 32, :] = h


def spread_columns(y_ref, width):
    mid = y_ref[24:48, :]
    lane = lax.broadcasted_iota(jnp.int32, mid.shape, 1)
    y_ref[0:24, :] = jnp.where(lane == 0, 0.0, pltpu.roll(mid, 1, 1))
    y_ref[48:72, :] = jnp.where(lane == width - 1, 0.0, pltpu.roll(mid, width - 1, 1))


def dual_kernel_body(
    total_ref, ta_ref, tb_ref, own_ref, first_ref, second_ref, known_ref, last_ref,
    cols_ref, mix_ref, new_ref, send_ref, y_ref,
):
    y_ref[...] = jnp.zeros((80, 1024), F32)
    before, after = plane_sides(ta_ref, tb_ref, slice(0, 48))
    for start, v in ((0, before), (2, total_ref[...]), (4, after)):
        for k in range(3):
            for z in range(2):
                row = 24 + (start + z) * 3 + k
                for b in range(8):
                    i = k * 16 + z * 8 + b
                    y_ref[row : row + 1, b * 128 : (b + 1) * 128] = v[i : i + 1]
    spread_columns(y_ref, 1024)
    slope, shift, mix = cols_ref[0:32, 0:1], cols_ref[32:40, 0:1], mix_ref[...]
    h = dot3(last_ref[...], y_ref[...]) + known_ref[...]
    dual_rows = (
        plane_sides(first_ref, second_ref, slice(32, 40))[0],
        own_ref[8:16, :],
        own_ref[32:40, :],
        plane_sides(first_ref, second_ref, slice(8, 16))[1],
    )
    for z in range(4):
        g = h[z * 32 : (z + 1) * 32]
        g = jnp.where(g > 0, g, slope * g)
        out = dot3(mix, g) + shift + dual_rows[z]
        if z in (1, 2):
            for c in range(5):
                new_ref[c, z - 1] = out[c : c + 1, :]
        for b in range(8):
            piece = jnp.broadcast_to(out[0:1, b * 128 : (b + 1) * 128], (16, 128))
            send_ref[:, b, z, :] = piece


def back_kernel(
    pix_hbm, bin_hbm, cnt_hbm, nd_ref, wh_ref, wl_ref, new_ref,
    out_ref, first_ref, second_ref, new_hbm, tab_ref, acc_ref, pix_ref, bin_ref, cnt_ref, list_ref,
    sem,
):
    even = is_even("tile")
    copies = index_copies(pix_hbm, bin_hbm, cnt_hbm, pix_ref, bin_ref, cnt_ref, sem)
    for copy in copies:
        copy.start()
    out_copy = pltpu.make_async_copy(new_ref, new_hbm, sem.at[3])
    out_copy.start()
    for a in range(16):
        for b in range(8):
            v = nd_ref[a, b]
            hi = v.astype(BF16).astype(F32)
            tab_ref[a, b, 0:4] = hi
            tab_ref[a, b, 4:8] = v - hi
    acc_ref[...] = jnp.zeros_like(acc_ref)
    zero = jnp.zeros((8, 128), F32)
    for copy in copies:
        copy.wait()

    steps = list_pairs(cnt_ref, list_ref)

    def pair(i, a, k, count):
        slots = (k * 2, k * 2 + 1)
        one, two = (tab_ref[a, bin_ref[s, 0, a]] for s in slots)
        left = jnp.concatenate(
            [jnp.concatenate([one, zero], 1), jnp.concatenate([zero, two], 1)], 0
        ).astype(BF16)
        right = jnp.concatenate(
            [jnp.concatenate([w[i, 0:128, :], w[i, 128:256, :]], 1) for w in (wh_ref, wl_ref)], 0
        )
        d = lax.dot_general(left, right, (((1,), (1,)), ((), ())), preferred_element_type=F32)
        d = d[:, 0:128] + d[:, 128:256]
        for n, s in enumerate(slots):
            q = pix_ref[s, 0, a]
            acc_ref[q if count is None else jnp.where(s < count, q, 16)] += d[n * 8 : n * 8 + 8]

    def sure_step(c, carry):
        for j in range(4):
            for k in range(3):
                a = c * 4 + j
                pair(a * 3 + k, a, k, None)
        return carry

    def step(c, carry):
        for j in range(CHUNK):
            i = c * CHUNK + j
            pair(SURE + i, *pair_at(list_ref, cnt_ref, i))
        return carry

    lax.fori_loop(0, 4, sure_step, 0)
    lax.fori_loop(0, steps, step, 0)
    for q in range(16):
        v = acc_ref[q, 0:4] + acc_ref[q, 4:8]
        out_ref[q * 4 : q * 4 + 4, :] = v
    up, down = out_ref[0:16, :], out_ref[48:64, :]
    first_ref[...] = jnp.where(even, down, up)
    second_ref[...] = jnp.where(even, up, down)
    out_copy.wait()


def finish(g, mix, slope, shift):
    g = jnp.where(g > 0, g, slope * g)
    return dot3(mix, g) + shift


def primal_inner_kernel(
    sp_ref, sm_ref, first_ref, second_ref, back_ref, primal_ref, kern_ref, mix_ref,
    bias_ref, slope_ref, shift_ref, part_ref, rim_ref, out_ref, cols_ref, mix_out_ref,
    tt_ref, lt_ref, lr_ref, x_ref, y_ref, vec_ref,
):
    p = lax.axis_index("plane")
    keeps = (p > 0, None, None, p < 7)
    before, after = plane_sides(first_ref, second_ref, slice(48, 64))
    for plane, v in enumerate((before, sm_ref[48:64, :], sp_ref[48:64, :], after)):
        for half in range(2):
            i = plane * 32 + half * 16
            x_ref[i : i + 16, :] = v[:, half * 512 : (half + 1) * 512]
    y_ref[...] = jnp.zeros((80, 512), F32)
    for plane in range(4):
        for row in range(1, 5):
            for col in range(4):
                i = (row * 4 - 4 + col) * 4 + plane
                v = back_ref[i : i + 1, :]
                if keeps[plane] is not None:
                    v = jnp.where(keeps[plane], v, 0.0)
                i = 24 + plane * 6 + row
                y_ref[i : i + 1, col * 128 : (col + 1) * 128] = v
    spread_columns(y_ref, 512)
    tt_ref[...] = jnp.zeros((96, 384), F32)
    lt_ref[...] = jnp.zeros((80, 256), F32)
    lr_ref[...] = jnp.zeros((32, 128), F32)
    for dz in range(3):
        for dr in range(3):
            block = jnp.concatenate(
                [
                    jnp.concatenate([kern_ref[c, dz, dr, db : db + 1, :] for db in range(3)], 1)
                    for c in range(5)
                ],
                0,
            )
            for r in range(4):
                i = dz * 32 + (r + dr) * 5
                tt_ref[i : i + 5, r * 96 : (r + 1) * 96] = block
            for db in range(3):
                four = jnp.concatenate([kern_ref[5, dz, dr, db : db + 1, :]] * 4, 1)
                for z in range(2):
                    for r in range(4):
                        i = db * 24 + (z + dz) * 6 + r + dr
                        lane = z * 128 + r * 32
                        lt_ref[i : i + 1, lane : lane + 32] = four[:, r * 32 : (r + 1) * 32]
                    if dr != 1:
                        i = db * 8 + (z + dz) * 2 + dr // 2
                        k = z * 2 + dr // 2
                        lr_ref[i : i + 1, k * 32 : (k + 1) * 32] = four[:, k * 32 : (k + 1) * 32]
    rim_ref[...] = joined(lr_ref[...].T)
    tt = joined(tt_ref[...].T)
    bias = tail_weights(
        mix_ref, bias_ref, slope_ref, shift_ref, cols_ref, mix_out_ref, vec_ref
    )
    slope, shift, mix = cols_ref[0:32, 0:1], cols_ref[32:40, 0:1], mix_out_ref[...]
    own = dot3(joined(lt_ref[...].T), y_ref[...])
    for z in range(2):
        h = dot3(tt, x_ref[z * 32 : z * 32 + 96])
        for r in range(4):
            g = shifted_sum([h[r * 96 + i * 32 : r * 96 + (i + 1) * 32] for i in range(3)]) + bias
            i = (z * 4 + r) * 32
            g = g + own[i : i + 32]
            if r in (0, 3):
                i = (z * 2 + r // 3) * 32
                part_ref[i : i + 32, :] = g
            else:
                out = finish(g, mix, slope, shift)
                for c in range(5):
                    out_ref[c, z, r : r + 1, :] = out[c : c + 1] + primal_ref[c, z, r : r + 1, :]
    for z in range(2):
        for c in range(5):
            for r in (0, 3):
                out_ref[c, z, r : r + 1, :] = primal_ref[c, z, r : r + 1, :]


def primal_outer_kernel(
    first_ref, second_ref, part_ref, rim_ref, inner_ref, cols_ref, mix_ref,
    out_hbm, y_ref, out_ref, sem,
):
    out_ref[...] = inner_ref[...]
    p = lax.axis_index("plane")
    t = lax.axis_index("tile")
    keeps = (p > 0, None, None, p < 7)
    even = is_even("tile")
    first, second = first_ref[...], second_ref[...]
    above = jnp.where(t > 0, jnp.where(even, second, first), 0.0)
    below = jnp.where(t < 15, jnp.where(even, first, second), 0.0)
    for plane in range(4):
        for rim, src in enumerate((above, below)):
            for col in range(4):
                i = col * 4 + plane
                v = src[i : i + 1]
                if keeps[plane] is not None:
                    v = jnp.where(keeps[plane], v, 0.0)
                i = 8 + plane * 2 + rim
                y_ref[i : i + 1, col * 128 : (col + 1) * 128] = v
    mid = y_ref[8:16, :]
    lane = lax.broadcasted_iota(jnp.int32, mid.shape, 1)
    y_ref[0:8, :] = jnp.where(lane == 0, 0.0, pltpu.roll(mid, 1, 1))
    y_ref[16:24, :] = jnp.where(lane == 511, 0.0, pltpu.roll(mid, 511, 1))
    y_ref[24:32, :] = jnp.zeros((8, 512), F32)
    slope, shift, mix = cols_ref[0:32, 0:1], cols_ref[32:40, 0:1], mix_ref[...]
    h = dot3(rim_ref[...], y_ref[...]) + part_ref[...]
    copies = []
    for z in range(2):
        for rim, row in enumerate((0, 3)):
            i = (z * 2 + rim) * 32
            out = finish(h[i : i + 32], mix, slope, shift)
            for c in range(5):
                out_ref[c, z, row : row + 1, :] += out[c : c + 1]
        copies.append(pltpu.make_async_copy(out_ref.at[:, z], out_hbm.at[:, z], sem.at[z]))
        copies[-1].start()
    for copy in copies:
        copy.wait()


def call(body, outs, in_specs, scratch=(), limit=8 << 20):
    return pl.pallas_call(
        body,
        out_shape=tuple(jax.ShapeDtypeStruct(s[0], s[1]) for s in outs),
        in_specs=in_specs,
        out_specs=tuple(VMEM for _ in outs),
        scratch_shapes=list(scratch),
        compiler_params=pltpu.CompilerParams(vmem_limit_bytes=limit),
    )


def swaps(first, second, axis):
    count = lax.axis_size(axis)
    a = lax.ppermute(first, axis, [(i, i ^ 1) for i in range(count)])
    pairs = [(i, (i - 1 if i % 2 == 0 else i + 1) % count) for i in range(count)]
    b = lax.ppermute(second, axis, pairs)
    return a, b


def per_device(
    primal, dual, measured, footprint_weights, pixel_index, bin_index, slot_count,
    dual_kernel, dual_bias, dual_slope, dual_mixing, dual_shift,
    primal_kernel, primal_bias, primal_slope, primal_mixing, primal_shift,
):
    pix = jnp.transpose(pixel_index, (2, 0, 1))
    bins = jnp.transpose(bin_index, (2, 0, 1))
    hbm = lambda x: pltpu.with_memory_space_constraint(x, pltpu.HBM)

    own = call(
        pack_kernel, [((32, 1024), F32)], [HBM] * 3,
        [
            pltpu.VMEM((5, 2, 1, 1024), F32),
            pltpu.VMEM((2, 1, 1024), F32),
            pltpu.VMEM((5, 2, 4, 512), F32),
            pltpu.SemaphoreType.DMA((3,)),
        ],
    )(hbm(dual), hbm(measured), hbm(primal))[0]
    pairs = footprint_weights.reshape(16, 6, 256, 128)

    near = swaps(own, own, "tile")

    terms, w_hi, w_lo = pl.pallas_call(
        project_kernel,
        name="project",
        out_shape=(
            jax.ShapeDtypeStruct((16, 3, 16, 128), F32),
            jax.ShapeDtypeStruct((ROOM, 256, 128), BF16),
            jax.ShapeDtypeStruct((ROOM, 256, 128), BF16),
        ),
        in_specs=[HBM] * 5 + [VMEM],
        out_specs=(VMEM, VMEM, VMEM),
        scratch_shapes=[pltpu.VMEM((16, 16, 128), F32)]
        + [pltpu.VMEM((16, 16, 128), BF16)] * 3
        + [
            pltpu.SMEM((12, 1, 16), jnp.int32),
            pltpu.SMEM((12, 1, 16), jnp.int32),
            pltpu.SMEM((1, 16), jnp.int32),
            pltpu.SMEM((128,), jnp.int32),
            pltpu.VMEM((2, 4, 512), F32),
            pltpu.VMEM((ROOM, 256, 128), F32),
            pltpu.SemaphoreType.DMA((4,)),
            pltpu.SemaphoreType.DMA((16,)),
            pltpu.SemaphoreType.DMA((ROOM - SURE,)),
        ],
        compiler_params=pltpu.CompilerParams(vmem_limit_bytes=18 << 20),
        cost_estimate=pl.CostEstimate(flops=1 << 31, bytes_accessed=25 << 20, transcendentals=0),
    )(hbm(pix), hbm(bins), hbm(slot_count), hbm(primal), hbm(pairs), own)
    terms, near = lax.optimization_barrier((terms, near))
    sp, sm, side_a, side_b = call(
        rims_kernel, [((64, 1024), F32)] * 4, [VMEM] * 4
    )(own, *near, primal)
    sides = swaps(side_a, side_b, "plane")
    got = lax.all_to_all(terms, "tile", 0, 0, tiled=True)
    total = call(total_kernel, [((48, 128), F32)], [VMEM])(got)[0]
    rows = swaps(total, total, "plane")

    known, last, cols, mix = call(
        dual_known_kernel,
        [((128, 1024), F32), ((128, 240), BF16), ((40, 128), F32), ((8, 96), BF16)],
        [VMEM] * 8,
        [
            pltpu.VMEM((80, 96), F32),
            pltpu.VMEM((80, 128), F32),
            pltpu.VMEM((8, 128), F32),
        ],
    )(
        sp, *sides, jnp.transpose(dual_kernel, (2, 3, 4, 1, 0)), dual_mixing,
        dual_bias.reshape(1, 32), dual_slope.reshape(1, 32), dual_shift.reshape(1, 5),
    )

    new_rows, send = call(
        dual_kernel_body, [((5, 2, 1, 1024), F32), ((16, 8, 4, 128), F32)],
        [VMEM] * 10, [pltpu.VMEM((80, 1024), F32)],
    )(
        total, *rows, sp, *sides, known, last, cols, mix,
    )
    leading = lax.all_to_all(send, "tile", 0, 0, tiled=True)

    back, edge_a, edge_b, new_dual = pl.pallas_call(
        back_kernel,
        name="back",
        out_shape=(
            jax.ShapeDtypeStruct((64, 128), F32),
            jax.ShapeDtypeStruct((16, 128), F32),
            jax.ShapeDtypeStruct((16, 128), F32),
            jax.ShapeDtypeStruct((5, 2, 1, 1024), F32),
        ),
        in_specs=[VMEM] * 7,
        out_specs=(VMEM, VMEM, VMEM, HBM),
        scratch_shapes=[
            pltpu.VMEM((16, 8, 8, 128), F32),
            pltpu.VMEM((17, 8, 128), F32),
            pltpu.SMEM((12, 1, 16), jnp.int32),
            pltpu.SMEM((12, 1, 16), jnp.int32),
            pltpu.SMEM((1, 16), jnp.int32),
            pltpu.SMEM((128,), jnp.int32),
            pltpu.SemaphoreType.DMA((4,)),
        ],
        compiler_params=pltpu.CompilerParams(vmem_limit_bytes=4 << 20),
    )(
        pix, bins, slot_count, leading, w_hi, w_lo, new_rows,
    )
    edges = swaps(edge_a, edge_b, "tile")

    part, rim, inner, cols, mix = pl.pallas_call(
        primal_inner_kernel,
        name="primal_inner",
        out_shape=(
            jax.ShapeDtypeStruct((128, 512), F32),
            jax.ShapeDtypeStruct((128, 96), BF16),
            jax.ShapeDtypeStruct((5, 2, 4, 512), F32),
            jax.ShapeDtypeStruct((40, 128), F32),
            jax.ShapeDtypeStruct((8, 96), BF16),
        ),
        in_specs=[VMEM] * 11,
        out_specs=(VMEM,) * 5,
        scratch_shapes=[
            pltpu.VMEM((96, 384), F32),
            pltpu.VMEM((80, 256), F32),
            pltpu.VMEM((32, 128), F32),
            pltpu.VMEM((128, 512), F32),
            pltpu.VMEM((80, 512), F32),
            pltpu.VMEM((8, 128), F32),
        ],
        compiler_params=pltpu.CompilerParams(vmem_limit_bytes=8 << 20),
    )(
        sp, sm, *sides, back, primal, jnp.transpose(primal_kernel, (1, 2, 3, 4, 0)),
        primal_mixing, primal_bias.reshape(1, 32), primal_slope.reshape(1, 32),
        primal_shift.reshape(1, 5),
    )

    new_primal = pl.pallas_call(
        primal_outer_kernel,
        name="primal_outer",
        out_shape=jax.ShapeDtypeStruct((5, 2, 4, 512), F32),
        in_specs=[VMEM] * 7,
        out_specs=HBM,
        scratch_shapes=[
            pltpu.VMEM((32, 512), F32),
            pltpu.VMEM((5, 2, 4, 512), F32),
            pltpu.SemaphoreType.DMA((2,)),
        ],
        compiler_params=pltpu.CompilerParams(vmem_limit_bytes=8 << 20),
    )(
        *edges, part, rim, inner, cols, mix,
    )
    return new_primal, new_dual


def solution(mesh):
    grid = P(None, "plane", "tile", None)
    in_specs = (
        grid, grid, P("plane", "tile", None), P("tile", None, None, None, None),
        P("tile", None, None), P(), P("tile", None),
    ) + (P(),) * 10
    return jax.shard_map(
        per_device, mesh=mesh, in_specs=in_specs, out_specs=(grid, grid), check_vma=False
    )
```
